128 devices in a mesh: board: 8 (over z, x_hi), cent: 16 (over y, x_lo, core).
Axes of the slice: x: 4 (x_hi: 2, x_lo: 2; x = x_hi * 2 + x_lo), y: 4, z: 4, core: 2. Of those that a mesh axis runs over, the one named last changes fastest.
Arguments:
- turn_hist: bfloat16 [50, 3080192], P(None, ('board', 'cent')), may hold values from 0.0009994507 to 1
- turn_assign: int32 [3080192], P(('board', 'cent')), may hold values from 0 to 199
- child_rows: int32 [47, 65536], P(None, ('board', 'cent')), may hold values from 0 to 187, as said below
- turn_centers: float32 [50, 200], replicated, may hold values from 0.001 to 1
- flop_centers: float32 [200, 2000], P(None, 'cent'), may hold values from 0.01 to 1
- flop_assign: int32 [65536], P(('board', 'cent')), may hold values from 0 to 1999
Outputs:
- nearest: float32 [65536], P(('board', 'cent'))
- turn_sums: float32 [50, 200], replicated
- flop_sums: float32 [2000, 200], P('cent')
The draws below stay inside these ranges and needn't reach their ends.
Inputs may be any that keep to these rules, and one draw needn't show every extreme that they name: `child_rows`: on each device's 512 flop hands, the entries whose n = i * 512 + g share one value of n // 188 form a permutation of 0 to 187.
All inputs are finite; a program needn't handle non-finite values.
Results may differ from the reference program's by a relative error of at most 0.0003.
Values may be sent and summed in bfloat16 or wider, within the bound.
No kernel may reach another device: no remote copies, remote signals or barrier semaphores. Data moves between devices by JAX's collectives and lax.ppermute only.
A program may use at most 128 MiB of HBM per device.

```python
import math
import jax
import jax.numpy as jnp
from jax import lax

BINS = 50
TURN_CENT = 200
FLOP_CENT = 2000
KIDS = 47
FLOP_DEV = 512
FLOP_HANDS = 65536
TURN_DEV = 24064
TURN_ROWS = 3080192
BLOCK = 188
N_BOARD = 8
N_CENT = 16


def draw_child_rows(key, part):
    devices = FLOP_HANDS // FLOP_DEV
    keys = jax.random.split(key, devices * devices)
    perms = jax.vmap(lambda single: jax.random.permutation(single, BLOCK))(keys)
    perms = perms.reshape(devices, KIDS, FLOP_DEV)
    return jnp.transpose(perms, (1, 0, 2)).reshape(KIDS, FLOP_HANDS).astype(jnp.int32)


def mixed_labels(key, total_rows, dev_rows, clusters, band):
    row = jnp.arange(total_rows, dtype=jnp.int32)
    devices = total_rows // dev_rows
    offset = row // dev_rows * clusters // devices
    key_band, key_wide, key_pick = jax.random.split(key, 3)
    spread = jax.random.randint(key_band, (total_rows,), 0, band, dtype=jnp.int32)
    banded = (offset + spread) % clusters
    anywhere = jax.random.randint(key_wide, (total_rows,), 0, clusters, dtype=jnp.int32)
    pick = jax.random.randint(key_pick, (total_rows,), 0, 2, dtype=jnp.int32)
    labels = pick * anywhere + (1 - pick) * banded
    labels = labels.at[0].set(0).at[total_rows - 1].set(clusters - 1)
    return labels.astype(jnp.int32)


def draw_turn_assign(key, part):
    return mixed_labels(key, TURN_ROWS, TURN_DEV, TURN_CENT, min(16, TURN_CENT))


def draw_flop_assign(key, part):
    return mixed_labels(key, FLOP_HANDS, FLOP_DEV, FLOP_CENT, min(128, FLOP_CENT // 2))


def level_of(stream_key, dims, cuts, smallest, high):
    factor_of, own = 1.0, jax.random.fold_in(stream_key, 6)
    for axis_at, shards_of in cuts:
        heights = jnp.exp(jax.random.uniform(jax.random.fold_in(own, axis_at), (shards_of,), jnp.float32, smallest / len(cuts), high / len(cuts)))
        factor_of = factor_of * jnp.repeat(heights, dims[axis_at] // shards_of).reshape([-1 if axis == axis_at else 1 for axis in range(len(dims))])
    return factor_of


def setup_inputs(seed: int = 0) -> dict:
    seeds = jax.random.split(jax.random.key(seed), 7)
    return {
        "turn_hist": jnp.clip(jnp.exp(math.log(1.0) - 6.9083047 * jax.random.uniform(seeds[0], (BINS, TURN_ROWS), jnp.float32) ** level_of(seeds[0], (BINS, TURN_ROWS), ((1, 128),), -0.2, 0.2)), 0.0009994507, 1.0).astype(jnp.bfloat16),
        "turn_assign": draw_turn_assign(jax.random.fold_in(seeds[6], 71), 0),
        "child_rows": draw_child_rows(jax.random.fold_in(seeds[6], 71), 0),
        "turn_centers": jnp.clip(jnp.exp(jax.random.uniform(seeds[3], (BINS, TURN_CENT), jnp.float32, math.log(0.001), math.log(1.0))), 0.001, 1.0),
        "flop_centers": jnp.clip(jnp.exp(math.log(1.0) - 4.6051702 * jax.random.uniform(seeds[4], (TURN_CENT, FLOP_CENT), jnp.float32) ** level_of(seeds[4], (TURN_CENT, FLOP_CENT), ((1, 16),), -0.2, 0.2)), 0.01, 1.0),
        "flop_assign": draw_flop_assign(jax.random.fold_in(seeds[6], 71), 0),
    }


sharpness = 4.0
highest = lax.Precision.HIGHEST


def normalize(values):
    return values / jnp.sum(values, axis=0, keepdims=True)


def cumulate(values):
    normal = normalize(values)
    padded = jnp.pad(normal, ((1, 1), (0, 0)))
    smooth = 0.25 * padded[:-2] + 0.5 * padded[1:-1] + 0.25 * padded[2:]
    return jnp.cumsum(smooth, axis=0)


def memberships(cdf, center_cdf, center_sq):
    cross = jnp.dot(center_cdf.T, cdf, precision=highest, preferred_element_type=jnp.float32)
    dist = jnp.sum(cdf * cdf, axis=0)[None, :] - 2.0 * cross + center_sq[:, None]
    kernel = 1.0 / jnp.square(1.0 + sharpness * dist)
    return kernel / jnp.sum(kernel, axis=0, keepdims=True)


def reference(turn_hist, turn_assign, child_rows, turn_centers, flop_centers, flop_assign):
    def add_block(total, start):
        values = lax.dynamic_slice_in_dim(turn_hist, start, TURN_DEV, 1).astype(jnp.float32)
        labels = lax.dynamic_slice_in_dim(turn_assign, start, TURN_DEV, 0)
        part_sum = jax.ops.segment_sum(normalize(values).T, labels, num_segments=TURN_CENT).T
        return total + part_sum, None

    starts = jnp.arange(N_BOARD * N_CENT, dtype=jnp.int32) * TURN_DEV
    total, _ = lax.scan(add_block, jnp.zeros((BINS, TURN_CENT), jnp.float32), starts)
    turn_sums = total * (BINS * TURN_CENT / TURN_ROWS)

    center_cdf = cumulate(turn_centers.astype(jnp.float32))
    center_sq = jnp.sum(center_cdf * center_cdf, axis=0)
    hand = jnp.arange(FLOP_HANDS, dtype=jnp.int32)
    owner = hand // FLOP_DEV
    local = hand % FLOP_DEV
    kid = jnp.arange(KIDS, dtype=jnp.int32)[:, None]
    flat = kid * FLOP_DEV + local[None, :]
    rows = ((flat // BLOCK) * TURN_DEV + owner[None, :] * BLOCK + child_rows).astype(jnp.int32)
    block_hands = min(FLOP_DEV, 256)

    def flop_block(start):
        index = lax.dynamic_slice_in_dim(rows, start, block_hands, 1).reshape(-1)
        cdf = cumulate(jnp.take(turn_hist, index, axis=1).astype(jnp.float32))
        weights = memberships(cdf, center_cdf, center_sq)
        return jnp.sum(weights.reshape(TURN_CENT, KIDS, block_hands), axis=1)

    blocks = lax.map(flop_block, jnp.arange(FLOP_HANDS // block_hands, dtype=jnp.int32) * block_hands)
    flop_hist = jnp.moveaxis(blocks, 0, 1).reshape(TURN_CENT, FLOP_HANDS)

    centers = flop_centers.astype(jnp.float32)
    hand_sq = jnp.sum(jnp.square(flop_hist), axis=0)
    cent_sq = jnp.sum(jnp.square(centers), axis=0)
    near_hands = 1024

    def near_block(start):
        piece = lax.dynamic_slice_in_dim(flop_hist, start, near_hands, 1)
        piece_sq = lax.dynamic_slice_in_dim(hand_sq, start, near_hands, 0)
        cross = jnp.dot(centers.T, piece, precision=highest, preferred_element_type=jnp.float32)
        dist = piece_sq[None, :] + cent_sq[:, None] - 2.0 * cross
        return jnp.min(dist, axis=0)

    nearest = lax.map(near_block, jnp.arange(FLOP_HANDS // near_hands, dtype=jnp.int32) * near_hands).reshape(FLOP_HANDS)
    flop_total = jax.ops.segment_sum(flop_hist.T, flop_assign, num_segments=FLOP_CENT)
    flop_sums = flop_total * (FLOP_CENT / FLOP_HANDS)
    return nearest, turn_sums, flop_sums
```

```python
import functools

import jax
import jax.numpy as jnp
from jax import lax
from jax.experimental import pallas as pl
from jax.experimental.pallas import tpu as pltpu
from jax.sharding import PartitionSpec as P

sharpness = 4.0
highest = lax.Precision.HIGHEST
f32, bf16, i32 = jnp.float32, jnp.bfloat16, jnp.int32
LANES = 128
BLOCK = 188
BINS = 50
KIDS = 47
TURN_CENT = 200
HANDS = 512
PANEL = 125
DEVICES = 128
SOURCES_PER_STEP = 32
PACK_ROWS = 80


def fold_table(bins):
    upper = lax.iota(i32, bins)[:, None]
    lower = lax.iota(i32, bins)[None, :]
    table = 0.5 * (lower <= upper).astype(f32)
    table = table + 0.25 * (lower <= upper - 1).astype(f32)
    table = table + 0.25 * ((lower <= upper + 1) & (lower >= 1)).astype(f32)
    return table


def pack_kernel(hist_ref, out_ref):
    lane = lax.broadcasted_iota(i32, (16, LANES), 1)
    for d in range(SOURCES_PER_STEP):
        t0, o = divmod(BLOCK * d, LANES)
        three = o + BLOCK > 2 * LANES

        def parts(lo, hi):
            tiles = [hist_ref[lo:hi, (t0 + t) * LANES:(t0 + t + 1) * LANES].astype(f32)
                     for t in range(3 if three else 2)]
            upper = lane[:hi - lo] >= o
            a = jnp.where(upper, tiles[0], tiles[1]) if o else tiles[0]
            b = jnp.where(upper, tiles[1], tiles[2]) if three else tiles[1]
            return a, b

        a0, b0 = parts(0, 16)
        a1, b1 = parts(16, 32)
        a2, b2 = parts(32, 48)
        a3, b3 = parts(48, 50)
        first = ((lane - o) & 127) < 64
        out_ref[d, 0:16, :] = a0.astype(bf16)
        out_ref[d, 16:32, :] = a1.astype(bf16)
        out_ref[d, 32:48, :] = a2.astype(bf16)
        out_ref[d, 48:64, :] = jnp.where(first, b0, pltpu.roll(b1, 64, 1)).astype(bf16)
        tail = jnp.concatenate(
            [pltpu.roll(b3, 64, 1), a3, pltpu.roll(a3, 64, 1), jnp.zeros((10, LANES), f32)], axis=0)
        out_ref[d, 64:80, :] = jnp.where(first, b2, tail).astype(bf16)


def pack(turn_hist):
    width = SOURCES_PER_STEP * BLOCK
    return pl.pallas_call(
        pack_kernel,
        grid=(DEVICES // SOURCES_PER_STEP,),
        in_specs=[pl.BlockSpec((BINS, width), lambda i: (0, i))],
        out_specs=pl.BlockSpec((SOURCES_PER_STEP, PACK_ROWS, LANES), lambda i: (i, 0, 0)),
        out_shape=jax.ShapeDtypeStruct((DEVICES, PACK_ROWS, LANES), bf16),
        name="pack",
    )(turn_hist)


def turn_kernel(hist_ref, label_ref, out_ref):
    @pl.when(pl.program_id(0) == 0)
    def _():
        out_ref[...] = jnp.zeros_like(out_ref)

    values = hist_ref[...].astype(f32)
    normal = values / jnp.sum(values, axis=0, keepdims=True)
    hi = normal.astype(bf16)
    rest = normal - hi.astype(f32)
    mid = rest.astype(bf16)
    low = (rest - mid.astype(f32)).astype(bf16)
    ids = lax.broadcasted_iota(i32, (TURN_CENT, values.shape[1]), 0)
    onehot = (label_ref[...] == ids).astype(f32).astype(bf16)
    total = out_ref[...]
    for part in (hi, mid, low):
        total = total + lax.dot_general(part, onehot, (((1,), (1,)), ((), ())), preferred_element_type=f32)
    out_ref[...] = total


def turn_partial(turn_hist, labels):
    width = SOURCES_PER_STEP * BLOCK // 2 if (SOURCES_PER_STEP * BLOCK // 2) % LANES == 0 else SOURCES_PER_STEP * BLOCK
    steps = turn_hist.shape[1] // width
    return pl.pallas_call(
        turn_kernel,
        grid=(steps,),
        in_specs=[pl.BlockSpec((BINS, width), lambda i: (0, i)), pl.BlockSpec((1, width), lambda i: (0, i))],
        out_specs=pl.BlockSpec((BINS, TURN_CENT), lambda i: (0, 0)),
        out_shape=jax.ShapeDtypeStruct((BINS, TURN_CENT), f32),
        name="turn_sums",
    )(turn_hist, labels)


TILE = 256
TILES = KIDS * HANDS // TILE


def split3(x):
    hi = x.astype(bf16)
    rest = x - hi.astype(f32)
    mid = rest.astype(bf16)
    low = (rest - mid.astype(f32)).astype(bf16)
    return hi, mid, low


def member_kernel(scalar_ref, recv_ref, place_ref, table_ref, assign_ref, hist_ref, keep_ref, send_ref, cols_ref):
    o = scalar_ref[0]
    core = scalar_ref[1]
    lane = lax.broadcasted_iota(i32, (16, LANES), 1)
    row = lax.broadcasted_iota(i32, (16, LANES), 0)
    first = ((lane - o) & 127) < 64
    from_c1 = (~first) & (row >= 2) & (row < 4)
    from_r1 = first & (row >= 4) & (row < 6)
    b3_rows = row < 2
    wide_lane = lax.broadcasted_iota(i32, (64, TILE), 1)
    one_lane = lax.broadcasted_iota(i32, (1, TILE), 1)
    sub = lax.broadcasted_iota(i32, (TILE, TILE), 0)

    def place(s, carry):
        start = s * BLOCK
        t0 = start // TILE
        a = start - t0 * TILE
        c0 = recv_ref[s, 48:64, :].astype(f32)
        c1 = recv_ref[s, 64:80, :].astype(f32)
        r0 = pltpu.roll(c0, 64, 1)
        r1 = pltpu.roll(c1, 64, 1)
        a3 = jnp.where(from_c1, c1, jnp.where(from_r1, r1, 0.0))
        b3 = jnp.where(b3_rows, r1, 0.0)
        left = jnp.concatenate([recv_ref[s, 0:48, :], a3.astype(bf16)], axis=0)
        right = jnp.concatenate(
            [recv_ref[s, 48:64, :], r0.astype(bf16), recv_ref[s, 64:80, :], b3.astype(bf16)], axis=0)
        payload = jnp.concatenate([left, right], axis=1)
        q = jnp.where(one_lane >= a, place_ref[pl.ds(t0, 1), :], place_ref[pl.ds(t0 + 1, 1), :])
        onehot = (sub == q).astype(f32).astype(bf16)
        cols = jnp.dot(payload, onehot, preferred_element_type=f32)
        cols_ref[t0] = jnp.where(wide_lane >= a, cols, cols_ref[t0])
        cols_ref[t0 + 1] = cols
        return carry

    cols_ref[0] = jnp.zeros((64, TILE), f32)
    lax.fori_loop(0, DEVICES, place, 0, unroll=2)

    hist_ref[...] = jnp.zeros_like(hist_ref)

    def kid(i, carry):
        h = jnp.concatenate([cols_ref[2 * i].astype(bf16), cols_ref[2 * i + 1].astype(bf16)], axis=1)
        z = jnp.dot(table_ref[...], jnp.concatenate([h, h, h], axis=0), preferred_element_type=f32)
        cdf = z[200:256]
        total = z[256:264]
        sq = jnp.sum(cdf * cdf, axis=0, keepdims=True)
        extra = total[0:1] + sharpness * sq / total[0:1]
        y = z[0:200] + extra
        w = 1.0 / (y * y)
        hist_ref[...] += w * (1.0 / jnp.sum(w, axis=0, keepdims=True))
        return carry

    lax.fori_loop(0, KIDS, kid, 0)

    hi, mid, low = split3(hist_ref[...])
    stack = jnp.concatenate([hi, mid, low], axis=0)
    ids = lax.broadcasted_iota(i32, (LANES, HANDS), 0)
    valid = ids < PANEL
    for i in range(8):
        halves = []
        for side in (core, 1 - core):
            base = PANEL * (2 * i + side)
            halves.append((valid & (assign_ref[...] - base == ids)).astype(f32).astype(bf16))
        onehot = jnp.concatenate(halves, axis=0)
        sums = lax.dot_general(stack, onehot, (((1,), (1,)), ((), ())), preferred_element_type=f32)
        both = sums[0:200] + sums[200:400] + sums[400:600]
        keep_ref[i] = both[:, :LANES]
        send_ref[i] = both[:, LANES:]


def member(scalars, recv, place, table, assign):
    vmem = pl.BlockSpec(memory_space=pltpu.VMEM)
    return pl.pallas_call(
        member_kernel,
        in_specs=[pl.BlockSpec(memory_space=pltpu.SMEM), vmem, vmem, vmem, vmem],
        out_specs=[vmem, vmem, vmem],
        out_shape=[
            jax.ShapeDtypeStruct((TURN_CENT, HANDS), f32),
            jax.ShapeDtypeStruct((8, TURN_CENT, LANES), f32),
            jax.ShapeDtypeStruct((8, TURN_CENT, LANES), f32),
        ],
        scratch_shapes=[pltpu.VMEM((TILES + 1, 64, TILE), f32)],
        compiler_params=pltpu.CompilerParams(vmem_limit_bytes=48 * 1024 * 1024),
        name="member",
    )(scalars, recv, place, table, assign)


def center_table(turn_centers):
    table = fold_table(BINS)
    values = turn_centers.astype(f32)
    normal = values / jnp.sum(values, axis=0, keepdims=True)
    center_cdf = jnp.dot(table, normal, precision=highest, preferred_element_type=f32)
    center_sq = jnp.sum(center_cdf * center_cdf, axis=0)
    folded = lax.dot_general(
        center_cdf, table, (((0,), (0,)), ((), ())), precision=highest, preferred_element_type=f32)
    folded = sharpness * center_sq[:, None] - 2.0 * sharpness * folded

    def spread(x):
        return jnp.concatenate(
            [x[:, :48], x[:, 48:], x[:, 48:], x[:, 48:], jnp.zeros((x.shape[0], 10), f32)], axis=1)

    hi = lax.reduce_precision(folded, 8, 7)
    mid = lax.reduce_precision(folded - hi, 8, 7)
    low = lax.reduce_precision(folded - hi - mid, 8, 7)
    top = jnp.concatenate([spread(hi), spread(mid), spread(low)], axis=1)
    rows = jnp.concatenate([table, jnp.zeros((6, BINS), f32), jnp.ones((8, BINS), f32)], axis=0)
    bottom = jnp.concatenate([spread(rows), jnp.zeros((64, 128), f32)], axis=1)
    return jnp.concatenate([top, bottom], axis=0).astype(bf16)


CHIPS = [[2 * i + c for i in range(8)] for c in range(2)]


def swap(x, axis, mask):
    size = 8 if axis == "board" else 16
    return lax.ppermute(x, axis, [(i, i ^ mask) for i in range(size)])


def add_over_board(x):
    for mask in (1, 2, 6):
        x = x + swap(x, "board", mask)
    return x


def add_over_all(x):
    for mask in (1, 2, 4, 12):
        x = x + swap(x, "cent", mask)
    return add_over_board(x)


def nearest_of(pieces, flop_hist):
    best = None
    for piece in pieces:
        cross = lax.dot_general(
            piece, flop_hist, (((1,), (0,)), ((), ())), precision=highest, preferred_element_type=f32)
        part = jnp.min(jnp.sum(jnp.square(piece), axis=1)[:, :, None] - 2.0 * cross, axis=(0, 1))
        best = part if best is None else jnp.minimum(best, part)
    return best + jnp.sum(jnp.square(flop_hist), axis=0)


def body(turn_hist, turn_assign, child_rows, turn_centers, flop_centers, flop_assign):
    sent = pack(turn_hist)
    arrived = lax.all_to_all(sent, ("board", "cent"), split_axis=0, concat_axis=0, tiled=True)

    device = lax.axis_index("board") * 16 + lax.axis_index("cent")
    offset = (device * BLOCK) % LANES
    scalars = jnp.stack([offset, lax.axis_index("cent") % 2]).astype(i32)

    turn_part = turn_partial(turn_hist, turn_assign[None, :])
    turn_sums = add_over_all(turn_part) * (BINS * TURN_CENT / (turn_hist.shape[1] * DEVICES))

    copies = jnp.broadcast_to(flop_centers[None], (8,) + flop_centers.shape)
    mine = lax.all_to_all(copies, "cent", split_axis=0, concat_axis=0, tiled=True, axis_index_groups=CHIPS)
    other = swap(mine, "cent", 1)

    place = (child_rows & 128) + ((child_rows + offset) & 127)
    place = jnp.concatenate([place.reshape(TILES, TILE), jnp.full((2, TILE), -1, i32)], axis=0)
    table = center_table(turn_centers)

    flop_hist, keep, send = member(scalars, arrived, place, table, flop_assign[None, :])

    half = keep + swap(send, "cent", 1)
    parts = lax.all_to_all(half, "cent", split_axis=0, concat_axis=0, tiled=True, axis_index_groups=CHIPS)
    flop_part = add_over_board(jnp.sum(parts, axis=0))
    flop_sums = flop_part[:, :PANEL].T * (PANEL * 16 / (HANDS * DEVICES))

    nearest = nearest_of((mine, other), flop_hist)
    return nearest, turn_sums, flop_sums


def solution(mesh):
    in_specs = (
        P(None, ("board", "cent")),
        P(("board", "cent")),
        P(None, ("board", "cent")),
        P(),
        P(None, "cent"),
        P(("board", "cent")),
    )
    out_specs = (P(("board", "cent")), P(), P("cent", None))
    return jax.shard_map(body, mesh=mesh, in_specs=in_specs, out_specs=out_specs, check_vma=False)
```

```python
import jax
import jax.numpy as jnp
from jax import lax
from jax.experimental import pallas as pl
from jax.experimental.pallas import tpu as pltpu
from jax.sharding import PartitionSpec as P


sharpness = 4.0
highest = lax.Precision.HIGHEST
f32, bf16, i32 = jnp.float32, jnp.bfloat16, jnp.int32
LANES = 128
BLOCK = 188
BINS = 50
KIDS = 47
TURN_CENT = 200
HANDS = 512
PANEL = 125
DEVICES = 128
SOURCES_PER_STEP = 32
PACK_ROWS = 80


def fold_table(bins):
    upper = lax.iota(i32, bins)[:, None]
    lower = lax.iota(i32, bins)[None, :]
    table = 0.5 * (lower <= upper).astype(f32)
    table = table + 0.25 * (lower <= upper - 1).astype(f32)
    table = table + 0.25 * ((lower <= upper + 1) & (lower >= 1)).astype(f32)
    return table


def pack_kernel(hist_ref, out_ref):
    lane = lax.broadcasted_iota(i32, (16, LANES), 1)
    for d in range(SOURCES_PER_STEP):
        t0, o = divmod(BLOCK * d, LANES)
        three = o + BLOCK > 2 * LANES

        def parts(lo, hi):
            tiles = [hist_ref[lo:hi, (t0 + t) * LANES:(t0 + t + 1) * LANES].astype(f32)
                     for t in range(3 if three else 2)]
            upper = lane[:hi - lo] >= o
            a = jnp.where(upper, tiles[0], tiles[1]) if o else tiles[0]
            b = jnp.where(upper, tiles[1], tiles[2]) if three else tiles[1]
            return a, b

        a0, b0 = parts(0, 16)
        a1, b1 = parts(16, 32)
        a2, b2 = parts(32, 48)
        a3, b3 = parts(48, 50)
        first = ((lane - o) & 127) < 64
        out_ref[d, 0:16, :] = a0.astype(bf16)
        out_ref[d, 16:32, :] = a1.astype(bf16)
        out_ref[d, 32:48, :] = a2.astype(bf16)
        out_ref[d, 48:64, :] = jnp.where(first, b0, pltpu.roll(b1, 64, 1)).astype(bf16)
        tail = jnp.concatenate(
            [pltpu.roll(b3, 64, 1), a3, pltpu.roll(a3, 64, 1), jnp.zeros((10, LANES), f32)], axis=0)
        out_ref[d, 64:80, :] = jnp.where(first, b2, tail).astype(bf16)


def pack(turn_hist):
    width = SOURCES_PER_STEP * BLOCK
    return pl.pallas_call(
        pack_kernel,
        grid=(DEVICES // SOURCES_PER_STEP,),
        in_specs=[pl.BlockSpec((BINS, width), lambda i: (0, i))],
        out_specs=pl.BlockSpec((SOURCES_PER_STEP, PACK_ROWS, LANES), lambda i: (i, 0, 0)),
        out_shape=jax.ShapeDtypeStruct((DEVICES, PACK_ROWS, LANES), bf16),
        name="pack",
    )(turn_hist)


def turn_kernel(hist_ref, label_ref, out_ref):
    @pl.when(pl.program_id(0) == 0)
    def _():
        out_ref[...] = jnp.zeros_like(out_ref)

    values = hist_ref[...].astype(f32)
    normal = values / jnp.sum(values, axis=0, keepdims=True)
    hi = normal.astype(bf16)
    rest = normal - hi.astype(f32)
    mid = rest.astype(bf16)
    low = (rest - mid.astype(f32)).astype(bf16)
    ids = lax.broadcasted_iota(i32, (TURN_CENT, values.shape[1]), 0)
    onehot = (label_ref[...] == ids).astype(f32).astype(bf16)
    total = out_ref[...]
    for part in (hi, mid, low):
        total = total + lax.dot_general(part, onehot, (((1,), (1,)), ((), ())), preferred_element_type=f32)
    out_ref[...] = total


def turn_partial(turn_hist, labels):
    width = SOURCES_PER_STEP * BLOCK // 2 if (SOURCES_PER_STEP * BLOCK // 2) % LANES == 0 else SOURCES_PER_STEP * BLOCK
    steps = turn_hist.shape[1] // width
    return pl.pallas_call(
        turn_kernel,
        grid=(steps,),
        in_specs=[pl.BlockSpec((BINS, width), lambda i: (0, i)), pl.BlockSpec((1, width), lambda i: (0, i))],
        out_specs=pl.BlockSpec((BINS, TURN_CENT), lambda i: (0, 0)),
        out_shape=jax.ShapeDtypeStruct((BINS, TURN_CENT), f32),
        name="turn_sums",
    )(turn_hist, labels)


TILE = 256
TILES = KIDS * HANDS // TILE


def split3(x):
    hi = x.astype(bf16)
    rest = x - hi.astype(f32)
    mid = rest.astype(bf16)
    low = (rest - mid.astype(f32)).astype(bf16)
    return hi, mid, low


def member_kernel(scalar_ref, recv_ref, place_ref, table_ref, assign_ref, hist_ref, keep_ref, send_ref, cols_ref):
    o = scalar_ref[0]
    core = scalar_ref[1]
    lane = lax.broadcasted_iota(i32, (16, LANES), 1)
    row = lax.broadcasted_iota(i32, (16, LANES), 0)
    first = ((lane - o) & 127) < 64
    from_c1 = (~first) & (row >= 2) & (row < 4)
    from_r1 = first & (row >= 4) & (row < 6)
    b3_rows = row < 2
    wide_lane = lax.broadcasted_iota(i32, (64, TILE), 1)
    one_lane = lax.broadcasted_iota(i32, (1, TILE), 1)
    sub = lax.broadcasted_iota(i32, (TILE, TILE), 0)

    def place(s, carry):
        start = s * BLOCK
        t0 = start // TILE
        a = start - t0 * TILE
        c0 = recv_ref[s, 48:64, :].astype(f32)
        c1 = recv_ref[s, 64:80, :].astype(f32)
        r0 = pltpu.roll(c0, 64, 1)
        r1 = pltpu.roll(c1, 64, 1)
        a3 = jnp.where(from_c1, c1, jnp.where(from_r1, r1, 0.0))
        b3 = jnp.where(b3_rows, r1, 0.0)
        left = jnp.concatenate([recv_ref[s, 0:48, :], a3.astype(bf16)], axis=0)
        right = jnp.concatenate(
            [recv_ref[s, 48:64, :], r0.astype(bf16), recv_ref[s, 64:80, :], b3.astype(bf16)], axis=0)
        payload = jnp.concatenate([left, right], axis=1)
        q = jnp.where(one_lane >= a, place_ref[pl.ds(t0, 1), :], place_ref[pl.ds(t0 + 1, 1), :])
        onehot = (sub == q).astype(f32).astype(bf16)
        cols = jnp.dot(payload, onehot, preferred_element_type=f32)
        cols_ref[t0] = jnp.where(wide_lane >= a, cols, cols_ref[t0])
        cols_ref[t0 + 1] = cols
        return carry

    cols_ref[0] = jnp.zeros((64, TILE), f32)
    lax.fori_loop(0, DEVICES, place, 0, unroll=2)

    hist_ref[...] = jnp.zeros_like(hist_ref)

    def kid(i, carry):
        h = jnp.concatenate([cols_ref[2 * i].astype(bf16), cols_ref[2 * i + 1].astype(bf16)], axis=1)
        z = jnp.dot(table_ref[...], jnp.concatenate([h, h, h], axis=0), preferred_element_type=f32)
        cdf = z[200:256]
        total = z[256:264]
        sq = jnp.sum(cdf * cdf, axis=0, keepdims=True)
        extra = total[0:1] + sharpness * sq / total[0:1]
        y = z[0:200] + extra
        w = 1.0 / (y * y)
        hist_ref[...] += w * (1.0 / jnp.sum(w, axis=0, keepdims=True))
        return carry

    lax.fori_loop(0, KIDS, kid, 0)

    hi, mid, low = split3(hist_ref[...])
    stack = jnp.concatenate([hi, mid, low], axis=0)
    ids = lax.broadcasted_iota(i32, (LANES, HANDS), 0)
    valid = ids < PANEL
    for i in range(8):
        halves = []
        for side in (core, 1 - core):
            base = PANEL * (2 * i + side)
            halves.append((valid & (assign_ref[...] - base == ids)).astype(f32).astype(bf16))
        onehot = jnp.concatenate(halves, axis=0)
        sums = lax.dot_general(stack, onehot, (((1,), (1,)), ((), ())), preferred_element_type=f32)
        both = sums[0:200] + sums[200:400] + sums[400:600]
        keep_ref[i] = both[:, :LANES]
        send_ref[i] = both[:, LANES:]


def member(scalars, recv, place, table, assign):
    vmem = pl.BlockSpec(memory_space=pltpu.VMEM)
    return pl.pallas_call(
        member_kernel,
        in_specs=[pl.BlockSpec(memory_space=pltpu.SMEM), vmem, vmem, vmem, vmem],
        out_specs=[vmem, vmem, vmem],
        out_shape=[
            jax.ShapeDtypeStruct((TURN_CENT, HANDS), f32),
            jax.ShapeDtypeStruct((8, TURN_CENT, LANES), f32),
            jax.ShapeDtypeStruct((8, TURN_CENT, LANES), f32),
        ],
        scratch_shapes=[pltpu.VMEM((TILES + 1, 64, TILE), f32)],
        compiler_params=pltpu.CompilerParams(vmem_limit_bytes=48 * 1024 * 1024),
        name="member",
    )(scalars, recv, place, table, assign)


def center_table(turn_centers):
    table = fold_table(BINS)
    values = turn_centers.astype(f32)
    normal = values / jnp.sum(values, axis=0, keepdims=True)
    center_cdf = jnp.dot(table, normal, precision=highest, preferred_element_type=f32)
    center_sq = jnp.sum(center_cdf * center_cdf, axis=0)
    folded = lax.dot_general(
        center_cdf, table, (((0,), (0,)), ((), ())), precision=highest, preferred_element_type=f32)
    folded = sharpness * center_sq[:, None] - 2.0 * sharpness * folded

    def spread(x):
        return jnp.concatenate(
            [x[:, :48], x[:, 48:], x[:, 48:], x[:, 48:], jnp.zeros((x.shape[0], 10), f32)], axis=1)

    hi = lax.reduce_precision(folded, 8, 7)
    mid = lax.reduce_precision(folded - hi, 8, 7)
    low = lax.reduce_precision(folded - hi - mid, 8, 7)
    top = jnp.concatenate([spread(hi), spread(mid), spread(low)], axis=1)
    rows = jnp.concatenate([table, jnp.zeros((6, BINS), f32), jnp.ones((8, BINS), f32)], axis=0)
    bottom = jnp.concatenate([spread(rows), jnp.zeros((64, 128), f32)], axis=1)
    return jnp.concatenate([top, bottom], axis=0).astype(bf16)


CHIPS = [[2 * i + c for i in range(8)] for c in range(2)]


def swap(x, axis, mask):
    size = 8 if axis == "board" else 16
    return lax.ppermute(x, axis, [(i, i ^ mask) for i in range(size)])


def add_over_board(x):
    for mask in (1, 2, 6):
        x = x + swap(x, "board", mask)
    return x


def add_over_all(x):
    for mask in (1, 2, 4, 12):
        x = x + swap(x, "cent", mask)
    return add_over_board(x)


def nearest_of(pieces, flop_hist):
    best = None
    for piece in pieces:
        cross = lax.dot_general(
            piece, flop_hist, (((1,), (0,)), ((), ())), precision=highest, preferred_element_type=f32)
        part = jnp.min(jnp.sum(jnp.square(piece), axis=1)[:, :, None] - 2.0 * cross, axis=(0, 1))
        best = part if best is None else jnp.minimum(best, part)
    return best + jnp.sum(jnp.square(flop_hist), axis=0)


def body(turn_hist, turn_assign, child_rows, turn_centers, flop_centers, flop_assign):
    sent = pack(turn_hist)
    device = lax.axis_index("board") * 16 + lax.axis_index("cent")
    offset = (device * BLOCK) % LANES
    scalars = jnp.stack([offset, lax.axis_index("cent") % 2]).astype(i32)

    labels, sent = lax.optimization_barrier((turn_assign[None, :], sent))
    arrived = lax.all_to_all(sent, ("board", "cent"), split_axis=0, concat_axis=0, tiled=True)
    turn_part = turn_partial(turn_hist, labels)
    flop_centers, turn_part = lax.optimization_barrier((flop_centers, turn_part))
    group = flop_centers[None]
    for mask in (2, 4, 12):
        group = jnp.concatenate([group, swap(group, "cent", mask)], axis=0)
    mine, other = group, swap(group, "cent", 1)
    turn_sums = add_over_all(turn_part) * (BINS * TURN_CENT / (turn_hist.shape[1] * DEVICES))

    place = (child_rows & 128) + ((child_rows + offset) & 127)
    place = jnp.concatenate([place.reshape(TILES, TILE), jnp.full((2, TILE), -1, i32)], axis=0)
    table = center_table(turn_centers)

    scalars, turn_sums, mine, other, place, table = lax.optimization_barrier(
        (scalars, turn_sums, mine, other, place, table))
    flop_hist, keep, send = member(scalars, arrived, place, table, flop_assign[None, :])

    half = keep + swap(send, "cent", 1)
    parts = lax.all_to_all(half, "cent", split_axis=0, concat_axis=0, tiled=True, axis_index_groups=CHIPS)
    flop_part = add_over_board(jnp.sum(parts, axis=0))
    flop_sums = flop_part[:, :PANEL].T * (PANEL * 16 / (HANDS * DEVICES))

    nearest = nearest_of((mine, other), flop_hist)
    return nearest, turn_sums, flop_sums


def solution(mesh):
    in_specs = (
        P(None, ("board", "cent")),
        P(("board", "cent")),
        P(None, ("board", "cent")),
        P(),
        P(None, "cent"),
        P(("board", "cent")),
    )
    out_specs = (P(("board", "cent")), P(), P("cent", None))
    return jax.shard_map(body, mesh=mesh, in_specs=in_specs, out_specs=out_specs, check_vma=False)
```

```python
import jax
import jax.numpy as jnp
from jax import lax
from jax.experimental import pallas as pl
from jax.experimental.pallas import tpu as pltpu
from jax.sharding import PartitionSpec as P


sharpness = 4.0
highest = lax.Precision.HIGHEST
f32, bf16, i32 = jnp.float32, jnp.bfloat16, jnp.int32
LANES = 128
BLOCK = 188
BINS = 50
KIDS = 47
TURN_CENT = 200
HANDS = 512
PANEL = 125
DEVICES = 128
SOURCES_PER_STEP = 32
PACK_ROWS = 80
TURN_SPLIT = 56
TURN_ROWS = 112


def fold_table(bins):
    upper = lax.iota(i32, bins)[:, None]
    lower = lax.iota(i32, bins)[None, :]
    table = 0.5 * (lower <= upper).astype(f32)
    table = table + 0.25 * (lower <= upper - 1).astype(f32)
    table = table + 0.25 * ((lower <= upper + 1) & (lower >= 1)).astype(f32)
    return table


def pack_kernel(hist_ref, out_ref):
    lane = lax.broadcasted_iota(i32, (16, LANES), 1)
    for d in range(SOURCES_PER_STEP):
        t0, o = divmod(BLOCK * d, LANES)
        three = o + BLOCK > 2 * LANES

        def parts(lo, hi):
            tiles = [hist_ref[lo:hi, (t0 + t) * LANES:(t0 + t + 1) * LANES].astype(f32)
                     for t in range(3 if three else 2)]
            upper = lane[:hi - lo] >= o
            a = jnp.where(upper, tiles[0], tiles[1]) if o else tiles[0]
            b = jnp.where(upper, tiles[1], tiles[2]) if three else tiles[1]
            return a, b

        a0, b0 = parts(0, 16)
        a1, b1 = parts(16, 32)
        a2, b2 = parts(32, 48)
        a3, b3 = parts(48, 50)
        first = ((lane - o) & 127) < 64
        out_ref[d, 0:16, :] = a0.astype(bf16)
        out_ref[d, 16:32, :] = a1.astype(bf16)
        out_ref[d, 32:48, :] = a2.astype(bf16)
        out_ref[d, 48:64, :] = jnp.where(first, b0, pltpu.roll(b1, 64, 1)).astype(bf16)
        tail = jnp.concatenate(
            [pltpu.roll(b3, 64, 1), a3, pltpu.roll(a3, 64, 1), jnp.zeros((10, LANES), f32)], axis=0)
        out_ref[d, 64:80, :] = jnp.where(first, b2, tail).astype(bf16)


def pack(turn_hist):
    width = SOURCES_PER_STEP * BLOCK
    return pl.pallas_call(
        pack_kernel,
        grid=(DEVICES // SOURCES_PER_STEP,),
        in_specs=[pl.BlockSpec((BINS, width), lambda i: (0, i))],
        out_specs=pl.BlockSpec((SOURCES_PER_STEP, PACK_ROWS, LANES), lambda i: (i, 0, 0)),
        out_shape=jax.ShapeDtypeStruct((DEVICES, PACK_ROWS, LANES), bf16),
        name="pack",
    )(turn_hist)


def turn_kernel(hist_ref, label_ref, out_ref):
    @pl.when(pl.program_id(0) == 0)
    def _():
        out_ref[...] = jnp.zeros_like(out_ref)

    values = hist_ref[...].astype(f32)
    normal = values / jnp.sum(values, axis=0, keepdims=True)
    hi = normal.astype(bf16)
    rest = normal - hi.astype(f32)
    mid = rest.astype(bf16)
    low = (rest - mid.astype(f32)).astype(bf16)
    ids = lax.broadcasted_iota(i32, (TURN_CENT, values.shape[1]), 0)
    onehot = (label_ref[...] == ids).astype(f32).astype(bf16)
    total = None
    for part in (hi, mid, low):
        more = lax.dot_general(part, onehot, (((1,), (1,)), ((), ())), preferred_element_type=f32)
        total = more if total is None else total + more
    out_ref[0:BINS, :] += total[:, :LANES]
    out_ref[TURN_SPLIT:TURN_SPLIT + BINS, 0:TURN_CENT - LANES] += total[:, LANES:]


def turn_partial(turn_hist, labels):
    width = SOURCES_PER_STEP * BLOCK // 2 if (SOURCES_PER_STEP * BLOCK // 2) % LANES == 0 else SOURCES_PER_STEP * BLOCK
    steps = turn_hist.shape[1] // width
    return pl.pallas_call(
        turn_kernel,
        grid=(steps,),
        in_specs=[pl.BlockSpec((BINS, width), lambda i: (0, i)), pl.BlockSpec((1, width), lambda i: (0, i))],
        out_specs=pl.BlockSpec((TURN_ROWS, LANES), lambda i: (0, 0)),
        out_shape=jax.ShapeDtypeStruct((TURN_ROWS, LANES), f32),
        name="turn_sums",
    )(turn_hist, labels)


TILE = 256
TILES = KIDS * HANDS // TILE


def split3(x):
    hi = x.astype(bf16)
    rest = x - hi.astype(f32)
    mid = rest.astype(bf16)
    low = (rest - mid.astype(f32)).astype(bf16)
    return hi, mid, low


def place_kernel(scalar_ref, recv_ref, place_ref, cols_ref):
    o = scalar_ref[0]
    lane = lax.broadcasted_iota(i32, (16, LANES), 1)
    row = lax.broadcasted_iota(i32, (16, LANES), 0)
    first = ((lane - o) & 127) < 64
    from_c1 = (~first) & (row >= 2) & (row < 4)
    from_r1 = first & (row >= 4) & (row < 6)
    b3_rows = row < 2
    wide_lane = lax.broadcasted_iota(i32, (64, TILE), 1)
    one_lane = lax.broadcasted_iota(i32, (1, TILE), 1)
    sub = lax.broadcasted_iota(i32, (TILE, TILE), 0)

    def place(s, carry):
        start = s * BLOCK
        t0 = start // TILE
        a = start - t0 * TILE
        c0 = recv_ref[s, 48:64, :].astype(f32)
        c1 = recv_ref[s, 64:80, :].astype(f32)
        r0 = pltpu.roll(c0, 64, 1)
        r1 = pltpu.roll(c1, 64, 1)
        a3 = jnp.where(from_c1, c1, jnp.where(from_r1, r1, 0.0))
        b3 = jnp.where(b3_rows, r1, 0.0)
        left = jnp.concatenate([recv_ref[s, 0:48, :], a3.astype(bf16)], axis=0)
        right = jnp.concatenate(
            [recv_ref[s, 48:64, :], r0.astype(bf16), recv_ref[s, 64:80, :], b3.astype(bf16)], axis=0)
        payload = jnp.concatenate([left, right], axis=1)
        q = jnp.where(one_lane >= a, place_ref[pl.ds(t0, 1), :], place_ref[pl.ds(t0 + 1, 1), :])
        onehot = (sub == q).astype(f32).astype(bf16)
        cols = jnp.dot(payload, onehot, preferred_element_type=f32)
        cols_ref[t0] = jnp.where(wide_lane >= a, cols, cols_ref[t0])
        cols_ref[t0 + 1] = cols
        return carry

    cols_ref[0] = jnp.zeros((64, TILE), f32)
    lax.fori_loop(0, DEVICES, place, 0, unroll=2)


def member_kernel(scalar_ref, cols_ref, table_ref, assign_ref, hist_ref, keep_ref, send_ref):
    core = scalar_ref[1]
    hist_ref[...] = jnp.zeros_like(hist_ref)

    def kid(i, carry):
        h = jnp.concatenate([cols_ref[2 * i].astype(bf16), cols_ref[2 * i + 1].astype(bf16)], axis=1)
        z = jnp.dot(table_ref[...], jnp.concatenate([h, h, h], axis=0), preferred_element_type=f32)
        cdf = z[200:256]
        total = z[256:264]
        sq = jnp.sum(cdf * cdf, axis=0, keepdims=True)
        extra = total[0:1] + sharpness * sq / total[0:1]
        y = z[0:200] + extra
        w = 1.0 / (y * y)
        hist_ref[...] += w * (1.0 / jnp.sum(w, axis=0, keepdims=True))
        return carry

    lax.fori_loop(0, KIDS, kid, 0)

    hi, mid, low = split3(hist_ref[...])
    stack = jnp.concatenate([hi, mid, low], axis=0)
    ids = lax.broadcasted_iota(i32, (LANES, HANDS), 0)
    valid = ids < PANEL
    for i in range(8):
        halves = []
        for side in (core, 1 - core):
            base = PANEL * (2 * i + side)
            halves.append((valid & (assign_ref[...] - base == ids)).astype(f32).astype(bf16))
        onehot = jnp.concatenate(halves, axis=0)
        sums = lax.dot_general(stack, onehot, (((1,), (1,)), ((), ())), preferred_element_type=f32)
        both = sums[0:200] + sums[200:400] + sums[400:600]
        keep_ref[i] = both[:, :LANES]
        send_ref[i] = both[:, LANES:]


VMEM = pl.BlockSpec(memory_space=pltpu.VMEM)
SMEM = pl.BlockSpec(memory_space=pltpu.SMEM)


def place_columns(scalars, recv, place):
    return pl.pallas_call(
        place_kernel,
        in_specs=[SMEM, VMEM, VMEM],
        out_specs=VMEM,
        out_shape=jax.ShapeDtypeStruct((TILES + 1, 64, TILE), f32),
        name="place",
    )(scalars, recv, place)


def member(scalars, cols, table, assign):
    return pl.pallas_call(
        member_kernel,
        in_specs=[SMEM, VMEM, VMEM, VMEM],
        out_specs=[VMEM, VMEM, VMEM],
        out_shape=[
            jax.ShapeDtypeStruct((TURN_CENT, HANDS), f32),
            jax.ShapeDtypeStruct((8, TURN_CENT, LANES), f32),
            jax.ShapeDtypeStruct((8, TURN_CENT, LANES), f32),
        ],
        name="member",
    )(scalars, cols, table, assign)


def center_table(turn_centers):
    table = fold_table(BINS)
    values = turn_centers.astype(f32)
    normal = values / jnp.sum(values, axis=0, keepdims=True)
    center_cdf = jnp.dot(table, normal, precision=highest, preferred_element_type=f32)
    center_sq = jnp.sum(center_cdf * center_cdf, axis=0)
    folded = lax.dot_general(
        center_cdf, table, (((0,), (0,)), ((), ())), precision=highest, preferred_element_type=f32)
    folded = sharpness * center_sq[:, None] - 2.0 * sharpness * folded

    def spread(x):
        return jnp.concatenate(
            [x[:, :48], x[:, 48:], x[:, 48:], x[:, 48:], jnp.zeros((x.shape[0], 10), f32)], axis=1)

    hi = lax.reduce_precision(folded, 8, 7)
    mid = lax.reduce_precision(folded - hi, 8, 7)
    low = lax.reduce_precision(folded - hi - mid, 8, 7)
    top = jnp.concatenate([spread(hi), spread(mid), spread(low)], axis=1)
    rows = jnp.concatenate([table, jnp.zeros((6, BINS), f32), jnp.ones((8, BINS), f32)], axis=0)
    bottom = jnp.concatenate([spread(rows), jnp.zeros((64, 128), f32)], axis=1)
    return jnp.concatenate([top, bottom], axis=0).astype(bf16)


CHIPS = [[2 * i + c for i in range(8)] for c in range(2)]


def swap(x, axis, mask):
    size = 8 if axis == "board" else 16
    return lax.ppermute(x, axis, [(i, i ^ mask) for i in range(size)])


def nearest_of(pieces, flop_hist):
    best = None
    for piece in pieces:
        cross = lax.dot_general(
            piece, flop_hist, (((1,), (0,)), ((), ())), precision=highest, preferred_element_type=f32)
        part = jnp.min(jnp.sum(jnp.square(piece), axis=1)[:, :, None] - 2.0 * cross, axis=(0, 1))
        best = part if best is None else jnp.minimum(best, part)
    return best + jnp.sum(jnp.square(flop_hist), axis=0)


def body(turn_hist, turn_assign, child_rows, turn_centers, flop_centers, flop_assign):
    sent = pack(turn_hist)
    turn_assign, sent = lax.optimization_barrier((turn_assign, sent))
    arrived = lax.all_to_all(sent, ("board", "cent"), split_axis=0, concat_axis=0, tiled=True)

    device = lax.axis_index("board") * 16 + lax.axis_index("cent")
    offset = (device * BLOCK) % LANES
    scalars = jnp.stack([offset, lax.axis_index("cent") % 2]).astype(i32)

    turn_part = turn_partial(turn_hist, turn_assign[None, :])
    own = jnp.concatenate([jnp.pad(flop_centers, ((0, 0), (0, LANES - PANEL))), turn_part], axis=0)
    pieces = [own]
    for mask in range(2, 16, 2):
        pieces.append(swap(own, "cent", mask))

    place = (child_rows & 128) + ((child_rows + offset) & 127)
    place = jnp.concatenate([place.reshape(TILES, TILE), jnp.full((2, TILE), -1, i32)], axis=0)
    table = center_table(turn_centers)
    place, table, scalars = lax.optimization_barrier((place, table, scalars))

    cols = place_columns(scalars, arrived, place)

    mine = jnp.stack([piece[:TURN_CENT] for piece in pieces])
    turn_part = sum((piece[TURN_CENT:] for piece in pieces[1:]), turn_part)
    other = swap(mine, "cent", 1)
    turn_part = turn_part + swap(turn_part, "cent", 1)

    flop_hist, keep, send = member(scalars, cols, table, flop_assign[None, :])

    half = keep + swap(send, "cent", 1)
    parts = lax.all_to_all(half, "cent", split_axis=0, concat_axis=0, tiled=True, axis_index_groups=CHIPS)
    total = jnp.concatenate([jnp.sum(parts, axis=0), turn_part], axis=0)
    for mask in (1, 2, 6):
        total = total + swap(total, "board", mask)
    flop_sums = total[:TURN_CENT, :PANEL].T * (PANEL * 16 / (HANDS * DEVICES))
    turn_low = total[TURN_CENT:TURN_CENT + BINS]
    turn_high = total[TURN_CENT + TURN_SPLIT:TURN_CENT + TURN_SPLIT + BINS, :TURN_CENT - LANES]
    turn_sums = jnp.concatenate([turn_low, turn_high], axis=1)
    turn_sums = turn_sums * (BINS * TURN_CENT / (turn_hist.shape[1] * DEVICES))

    nearest = nearest_of((mine[:, :, :PANEL], other[:, :, :PANEL]), flop_hist)
    return nearest, turn_sums, flop_sums


def solution(mesh):
    in_specs = (
        P(None, ("board", "cent")),
        P(("board", "cent")),
        P(None, ("board", "cent")),
        P(),
        P(None, "cent"),
        P(("board", "cent")),
    )
    out_specs = (P(("board", "cent")), P(), P("cent", None))
    return jax.shard_map(body, mesh=mesh, in_specs=in_specs, out_specs=out_specs, check_vma=False)
```

```python
import jax
import jax.numpy as jnp
from jax import lax
from jax.experimental import pallas as pl
from jax.experimental.pallas import tpu as pltpu
from jax.sharding import PartitionSpec as P


sharpness = 4.0
highest = lax.Precision.HIGHEST
f32, bf16, i32 = jnp.float32, jnp.bfloat16, jnp.int32
LANES = 128
BLOCK = 188
BINS = 50
KIDS = 47
TURN_CENT = 200
HANDS = 512
PANEL = 125
DEVICES = 128
SOURCES_PER_STEP = 32
PACK_ROWS = 80
TURN_SPLIT = 56
TURN_ROWS = 112


def fold_table(bins):
    upper = lax.iota(i32, bins)[:, None]
    lower = lax.iota(i32, bins)[None, :]
    table = 0.5 * (lower <= upper).astype(f32)
    table = table + 0.25 * (lower <= upper - 1).astype(f32)
    table = table + 0.25 * ((lower <= upper + 1) & (lower >= 1)).astype(f32)
    return table


def pack_kernel(hist_ref, out_ref):
    lane = lax.broadcasted_iota(i32, (16, LANES), 1)
    for d in range(SOURCES_PER_STEP):
        t0, o = divmod(BLOCK * d, LANES)
        three = o + BLOCK > 2 * LANES

        def parts(lo, hi):
            tiles = [hist_ref[lo:hi, (t0 + t) * LANES:(t0 + t + 1) * LANES].astype(f32)
                     for t in range(3 if three else 2)]
            upper = lane[:hi - lo] >= o
            a = jnp.where(upper, tiles[0], tiles[1]) if o else tiles[0]
            b = jnp.where(upper, tiles[1], tiles[2]) if three else tiles[1]
            return a, b

        a0, b0 = parts(0, 16)
        a1, b1 = parts(16, 32)
        a2, b2 = parts(32, 48)
        a3, b3 = parts(48, 50)
        first = ((lane - o) & 127) < 64
        out_ref[d, 0:16, :] = a0.astype(bf16)
        out_ref[d, 16:32, :] = a1.astype(bf16)
        out_ref[d, 32:48, :] = a2.astype(bf16)
        out_ref[d, 48:64, :] = jnp.where(first, b0, pltpu.roll(b1, 64, 1)).astype(bf16)
        tail = jnp.concatenate(
            [pltpu.roll(b3, 64, 1), a3, pltpu.roll(a3, 64, 1), jnp.zeros((10, LANES), f32)], axis=0)
        out_ref[d, 64:80, :] = jnp.where(first, b2, tail).astype(bf16)


def pack(turn_hist):
    width = SOURCES_PER_STEP * BLOCK
    return pl.pallas_call(
        pack_kernel,
        grid=(DEVICES // SOURCES_PER_STEP,),
        in_specs=[pl.BlockSpec((BINS, width), lambda i: (0, i))],
        out_specs=pl.BlockSpec((SOURCES_PER_STEP, PACK_ROWS, LANES), lambda i: (i, 0, 0)),
        out_shape=jax.ShapeDtypeStruct((DEVICES, PACK_ROWS, LANES), bf16),
        name="pack",
    )(turn_hist)


def turn_kernel(hist_ref, label_ref, out_ref):
    @pl.when(pl.program_id(0) == 0)
    def _():
        out_ref[...] = jnp.zeros_like(out_ref)

    values = hist_ref[...].astype(f32)
    normal = values / jnp.sum(values, axis=0, keepdims=True)
    hi = normal.astype(bf16)
    rest = normal - hi.astype(f32)
    mid = rest.astype(bf16)
    low = (rest - mid.astype(f32)).astype(bf16)
    ids = lax.broadcasted_iota(i32, (TURN_CENT, values.shape[1]), 0)
    onehot = (label_ref[...] == ids).astype(f32).astype(bf16)
    total = None
    for part in (hi, mid, low):
        more = lax.dot_general(part, onehot, (((1,), (1,)), ((), ())), preferred_element_type=f32)
        total = more if total is None else total + more
    out_ref[0:BINS, :] += total[:, :LANES]
    out_ref[TURN_SPLIT:TURN_SPLIT + BINS, 0:TURN_CENT - LANES] += total[:, LANES:]


def turn_partial(turn_hist, labels):
    width = SOURCES_PER_STEP * BLOCK // 2 if (SOURCES_PER_STEP * BLOCK // 2) % LANES == 0 else SOURCES_PER_STEP * BLOCK
    steps = turn_hist.shape[1] // width
    return pl.pallas_call(
        turn_kernel,
        grid=(steps,),
        in_specs=[pl.BlockSpec((BINS, width), lambda i: (0, i)), pl.BlockSpec((1, width), lambda i: (0, i))],
        out_specs=pl.BlockSpec((TURN_ROWS, LANES), lambda i: (0, 0)),
        out_shape=jax.ShapeDtypeStruct((TURN_ROWS, LANES), f32),
        name="turn_sums",
    )(turn_hist, labels)


TILE = 256
TILES = KIDS * HANDS // TILE


def place_columns(o, recv_ref, place_ref, cols_ref):
    row = lax.broadcasted_iota(i32, (8, LANES), 0)
    lane = lax.broadcasted_iota(i32, (8, LANES), 1)
    tail_hi, tail_mid, tail_low = row < 2, (row >= 2) & (row < 4), (row >= 4) & (row < 6)
    zero = jnp.zeros((8, LANES), f32)

    def gather(x, index):
        return jnp.take_along_axis(x, index, axis=1)

    def place(s, carry):
        start = s * BLOCK
        t0 = start // TILE
        a = start - t0 * TILE
        tiles = []
        for t in range(PACK_ROWS // 16):
            both = recv_ref[s, 16 * t:16 * t + 16, :].astype(f32)
            tiles += [both[0:8], both[8:16]]
        now, later = place_ref[pl.ds(t0, 1), :], place_ref[pl.ds(t0 + 1, 1), :]
        following = []
        for half in range(2):
            side = slice(half * LANES, (half + 1) * LANES)
            mask = lane + half * LANES >= a
            spill = lane + (half * LANES + TILE) < a + BLOCK
            r = jnp.where(mask, now[:, side], later[:, side])
            p = (r + o) & 127
            p2 = p ^ 64
            far = r >= LANES
            first = ((p - o) & 127) < 64
            out = []
            for g in range(6):
                source, index = tiles[(6, 7, 6, 7, 8, 9)[g]], p2 if g in (2, 3) else p
                out.append(jnp.where(far, gather(source, index), gather(tiles[g], p)))
            near, turned = gather(tiles[8], p), gather(tiles[8], p2)
            out.append(jnp.where(far & tail_hi | ~far & first & tail_low, turned,
                                 jnp.where(~far & ~first & tail_mid, near, zero)))
            merged = [jnp.where(mask, out[g], carry[7 * half + g]) for g in range(7)]
            for g in range(4):
                pair = jnp.concatenate([merged[2 * g], merged[2 * g + 1] if g < 3 else zero], axis=0)
                cols_ref[t0, 16 * g:16 * g + 16, side] = pair.astype(bf16)
            following += [jnp.where(spill, out[g], merged[g]) for g in range(7)]
        return tuple(following)

    lax.fori_loop(0, DEVICES, place, (zero,) * 14, unroll=4)


def member_kernel(scalar_ref, recv_ref, place_ref, table_ref, assign_ref,
                  hist_ref, keep_ref, send_ref, cols_ref, even_ref, odd_ref):
    core = scalar_ref[1]
    place_columns(scalar_ref[0], recv_ref, place_ref, cols_ref)

    def products(i, out_ref):
        h = jnp.concatenate([cols_ref[2 * i], cols_ref[2 * i + 1]], axis=1)
        out_ref[...] = jnp.dot(
            table_ref[...], jnp.concatenate([h, h, h], axis=0), preferred_element_type=f32)

    def add_kid(z_ref):
        for c in range(HANDS // LANES):
            at = slice(c * LANES, (c + 1) * LANES)
            cdf = z_ref[200:256, at]
            total = z_ref[256:264, at]
            sq = jnp.sum(cdf * cdf, axis=0, keepdims=True)
            extra = total + sharpness * sq / total
            y = z_ref[0:200, at].reshape(25, 8, LANES) + extra[None]
            w = 1.0 / (y * y)
            scale = 1.0 / jnp.sum(jnp.sum(w, axis=0), axis=0, keepdims=True)
            hist_ref[:, at] += (w * scale[None]).reshape(200, LANES)

    hist_ref[...] = jnp.zeros_like(hist_ref)
    products(0, even_ref)

    def two_kids(j, carry):
        products(2 * j + 1, odd_ref)
        add_kid(even_ref)
        products(2 * j + 2, even_ref)
        add_kid(odd_ref)
        return carry

    lax.fori_loop(0, KIDS // 2, two_kids, 0)
    add_kid(even_ref)

    hi = hist_ref[...].astype(bf16)
    rest = (hist_ref[...] - hi.astype(f32)).astype(bf16)
    stack = jnp.concatenate([hi, rest], axis=0)
    ids = lax.broadcasted_iota(i32, (LANES, HANDS), 0)
    valid = ids < PANEL
    for i in range(8):
        halves = []
        for side in (core, 1 - core):
            base = PANEL * (2 * i + side)
            halves.append((valid & (assign_ref[...] - base == ids)).astype(f32).astype(bf16))
        onehot = jnp.concatenate(halves, axis=0)
        sums = lax.dot_general(stack, onehot, (((1,), (1,)), ((), ())), preferred_element_type=f32)
        both = sums[0:200] + sums[200:400]
        keep_ref[i] = both[:, :LANES]
        send_ref[i] = both[:, LANES:]


VMEM = pl.BlockSpec(memory_space=pltpu.VMEM)
SMEM = pl.BlockSpec(memory_space=pltpu.SMEM)


def member(scalars, recv, place, table, assign):
    return pl.pallas_call(
        member_kernel,
        in_specs=[SMEM, VMEM, VMEM, VMEM, VMEM],
        out_specs=[VMEM, VMEM, VMEM],
        out_shape=[
            jax.ShapeDtypeStruct((TURN_CENT, HANDS), f32),
            jax.ShapeDtypeStruct((8, TURN_CENT, LANES), f32),
            jax.ShapeDtypeStruct((8, TURN_CENT, LANES), f32),
        ],
        scratch_shapes=[
            pltpu.VMEM((TILES, 64, TILE), bf16),
            pltpu.VMEM((264, HANDS), f32),
            pltpu.VMEM((264, HANDS), f32),
        ],
        name="member",
    )(scalars, recv, place, table, assign)


def nearest_kernel(mine_ref, partner_ref, *refs):
    pieces, out_ref = refs[:-1], refs[-1]
    one = jnp.where(lax.broadcasted_iota(i32, (8, 2 * HANDS), 0) == 0, 1.0, 0.0)
    hands = jnp.concatenate([jnp.concatenate([mine_ref[...], partner_ref[...]], axis=1), one], axis=0)
    lane = lax.broadcasted_iota(i32, (8, LANES), 1)
    best = None
    for ref in pieces:
        c = ref[0:TURN_CENT, :]
        sq = jnp.broadcast_to(jnp.sum(c * c, axis=0, keepdims=True), (8, LANES))
        sides = jnp.concatenate([-2.0 * c, jnp.where(lane < PANEL, sq, 1e30)], axis=0)
        dist = lax.dot_general(
            sides, hands, (((0,), (0,)), ((), ())), precision=highest, preferred_element_type=f32)
        part = jnp.min(dist, axis=0, keepdims=True)
        best = part if best is None else jnp.minimum(best, part)
    out_ref[...] = best


def nearest_of(pieces, flop_hist, partner):
    best = pl.pallas_call(
        nearest_kernel,
        in_specs=[VMEM] * (2 + len(pieces)),
        out_specs=VMEM,
        out_shape=jax.ShapeDtypeStruct((1, 2 * HANDS), f32),
        name="nearest",
    )(flop_hist, partner, *pieces)
    best = jnp.minimum(best[:, :HANDS], swap(best[:, HANDS:], "cent", 1))
    return best[0] + jnp.sum(jnp.square(flop_hist), axis=0)


def center_table(turn_centers):
    table = fold_table(BINS)
    values = turn_centers.astype(f32)
    normal = values / jnp.sum(values, axis=0, keepdims=True)
    center_cdf = jnp.dot(table, normal, precision=highest, preferred_element_type=f32)
    center_sq = jnp.sum(center_cdf * center_cdf, axis=0)
    folded = lax.dot_general(
        center_cdf, table, (((0,), (0,)), ((), ())), precision=highest, preferred_element_type=f32)
    folded = sharpness * center_sq[:, None] - 2.0 * sharpness * folded

    def spread(x):
        return jnp.concatenate(
            [x[:, :48], x[:, 48:], x[:, 48:], x[:, 48:], jnp.zeros((x.shape[0], 10), f32)], axis=1)

    hi = lax.reduce_precision(folded, 8, 7)
    mid = lax.reduce_precision(folded - hi, 8, 7)
    low = lax.reduce_precision(folded - hi - mid, 8, 7)
    top = jnp.concatenate([spread(hi), spread(mid), spread(low)], axis=1)
    rows = jnp.concatenate([table, jnp.zeros((6, BINS), f32), jnp.ones((8, BINS), f32)], axis=0)
    bottom = jnp.concatenate([spread(rows), jnp.zeros((64, 128), f32)], axis=1)
    return jnp.concatenate([top, bottom], axis=0).astype(bf16)


CHIPS = [[2 * i + c for i in range(8)] for c in range(2)]


def swap(x, axis, mask):
    size = 8 if axis == "board" else 16
    return lax.ppermute(x, axis, [(i, i ^ mask) for i in range(size)])


def body(turn_hist, turn_assign, child_rows, turn_centers, flop_centers, flop_assign):
    sent = pack(turn_hist)
    turn_assign, sent = lax.optimization_barrier((turn_assign, sent))
    arrived = lax.all_to_all(sent, ("board", "cent"), split_axis=0, concat_axis=0, tiled=True)

    device = lax.axis_index("board") * 16 + lax.axis_index("cent")
    offset = (device * BLOCK) % LANES
    scalars = jnp.stack([offset, lax.axis_index("cent") % 2]).astype(i32)

    turn_part = turn_partial(turn_hist, turn_assign[None, :])
    own = jnp.concatenate([jnp.pad(flop_centers, ((0, 0), (0, LANES - PANEL))), turn_part], axis=0)
    pieces = [own]
    for mask in range(2, 16, 2):
        pieces.append(swap(own, "cent", mask))

    place = jnp.concatenate([child_rows.reshape(TILES, TILE), jnp.zeros((2, TILE), i32)], axis=0)
    table = center_table(turn_centers)
    place, table, scalars = lax.optimization_barrier((place, table, scalars))

    flop_hist, keep, send = member(scalars, arrived, place, table, flop_assign[None, :])

    partner = swap(flop_hist, "cent", 1)
    turn_part = sum((piece[TURN_CENT:] for piece in pieces[1:]), turn_part)
    turn_part = turn_part + swap(turn_part, "cent", 1)
    half = keep + swap(send, "cent", 1)
    parts = lax.all_to_all(half, "cent", split_axis=0, concat_axis=0, tiled=True, axis_index_groups=CHIPS)
    total = jnp.concatenate([jnp.sum(parts, axis=0), turn_part], axis=0)
    for mask in (1, 2, 6):
        total = total + swap(total, "board", mask)
    flop_sums = total[:TURN_CENT, :PANEL].T * (PANEL * 16 / (HANDS * DEVICES))
    turn_low = total[TURN_CENT:TURN_CENT + BINS]
    turn_high = total[TURN_CENT + TURN_SPLIT:TURN_CENT + TURN_SPLIT + BINS, :TURN_CENT - LANES]
    turn_sums = jnp.concatenate([turn_low, turn_high], axis=1)
    turn_sums = turn_sums * (BINS * TURN_CENT / (turn_hist.shape[1] * DEVICES))

    nearest = nearest_of(pieces, flop_hist, partner)
    return nearest, turn_sums, flop_sums


def solution(mesh):
    in_specs = (
        P(None, ("board", "cent")),
        P(("board", "cent")),
        P(None, ("board", "cent")),
        P(),
        P(None, "cent"),
        P(("board", "cent")),
    )
    out_specs = (P(("board", "cent")), P(), P("cent", None))
    return jax.shard_map(body, mesh=mesh, in_specs=in_specs, out_specs=out_specs, check_vma=False)
```

```python
import jax
import jax.numpy as jnp
from jax import lax
from jax.experimental import pallas as pl
from jax.experimental.pallas import tpu as pltpu
from jax.sharding import PartitionSpec as P


sharpness = 4.0
highest = lax.Precision.HIGHEST
f32, bf16, i32 = jnp.float32, jnp.bfloat16, jnp.int32
LANES = 128
BLOCK = 188
BINS = 50
KIDS = 47
TURN_CENT = 200
HANDS = 512
PANEL = 125
DEVICES = 128
SOURCES_PER_STEP = 32
PACK_ROWS = 80
TURN_SPLIT = 56
TURN_ROWS = 112


def fold_table(bins):
    upper = lax.iota(i32, bins)[:, None]
    lower = lax.iota(i32, bins)[None, :]
    table = 0.5 * (lower <= upper).astype(f32)
    table = table + 0.25 * (lower <= upper - 1).astype(f32)
    table = table + 0.25 * ((lower <= upper + 1) & (lower >= 1)).astype(f32)
    return table


def pack_kernel(hist_ref, out_ref):
    lane = lax.broadcasted_iota(i32, (16, LANES), 1)
    for d in range(SOURCES_PER_STEP):
        t0, o = divmod(BLOCK * d, LANES)
        three = o + BLOCK > 2 * LANES

        def parts(lo, hi):
            tiles = [hist_ref[lo:hi, (t0 + t) * LANES:(t0 + t + 1) * LANES].astype(f32)
                     for t in range(3 if three else 2)]
            upper = lane[:hi - lo] >= o
            a = jnp.where(upper, tiles[0], tiles[1]) if o else tiles[0]
            b = jnp.where(upper, tiles[1], tiles[2]) if three else tiles[1]
            return a, b

        a0, b0 = parts(0, 16)
        a1, b1 = parts(16, 32)
        a2, b2 = parts(32, 48)
        a3, b3 = parts(48, 50)
        first = ((lane - o) & 127) < 64
        out_ref[d, 0:16, :] = a0.astype(bf16)
        out_ref[d, 16:32, :] = a1.astype(bf16)
        out_ref[d, 32:48, :] = a2.astype(bf16)
        out_ref[d, 48:64, :] = jnp.where(first, b0, pltpu.roll(b1, 64, 1)).astype(bf16)
        tail = jnp.concatenate(
            [pltpu.roll(b3, 64, 1), a3, pltpu.roll(a3, 64, 1), jnp.zeros((10, LANES), f32)], axis=0)
        out_ref[d, 64:80, :] = jnp.where(first, b2, tail).astype(bf16)


def pack(turn_hist):
    width = SOURCES_PER_STEP * BLOCK
    return pl.pallas_call(
        pack_kernel,
        grid=(DEVICES // SOURCES_PER_STEP,),
        in_specs=[pl.BlockSpec((BINS, width), lambda i: (0, i))],
        out_specs=pl.BlockSpec((SOURCES_PER_STEP, PACK_ROWS, LANES), lambda i: (i, 0, 0)),
        out_shape=jax.ShapeDtypeStruct((DEVICES, PACK_ROWS, LANES), bf16),
        name="pack",
    )(turn_hist)


def turn_kernel(hist_ref, label_ref, out_ref):
    @pl.when(pl.program_id(0) == 0)
    def _():
        out_ref[...] = jnp.zeros_like(out_ref)

    values = hist_ref[...].astype(f32)
    normal = values / jnp.sum(values, axis=0, keepdims=True)
    hi = normal.astype(bf16)
    rest = normal - hi.astype(f32)
    mid = rest.astype(bf16)
    low = (rest - mid.astype(f32)).astype(bf16)
    ids = lax.broadcasted_iota(i32, (TURN_CENT, values.shape[1]), 0)
    onehot = (label_ref[...] == ids).astype(f32).astype(bf16)
    total = None
    for part in (hi, mid, low):
        more = lax.dot_general(part, onehot, (((1,), (1,)), ((), ())), preferred_element_type=f32)
        total = more if total is None else total + more
    out_ref[0:BINS, :] += total[:, :LANES]
    out_ref[TURN_SPLIT:TURN_SPLIT + BINS, 0:TURN_CENT - LANES] += total[:, LANES:]


def turn_partial(turn_hist, labels):
    width = SOURCES_PER_STEP * BLOCK // 2 if (SOURCES_PER_STEP * BLOCK // 2) % LANES == 0 else SOURCES_PER_STEP * BLOCK
    steps = turn_hist.shape[1] // width
    return pl.pallas_call(
        turn_kernel,
        grid=(steps,),
        in_specs=[pl.BlockSpec((BINS, width), lambda i: (0, i)), pl.BlockSpec((1, width), lambda i: (0, i))],
        out_specs=pl.BlockSpec((TURN_ROWS, LANES), lambda i: (0, 0)),
        out_shape=jax.ShapeDtypeStruct((TURN_ROWS, LANES), f32),
        name="turn_sums",
    )(turn_hist, labels)


TILE = 256
TILES = KIDS * HANDS // TILE
EARLY = 16
AHEAD = 6


def place_columns(o, recv_ref, place_ref, cols_ref):
    row = lax.broadcasted_iota(i32, (8, LANES), 0)
    lane = lax.broadcasted_iota(i32, (8, LANES), 1)
    tail_hi, tail_mid, tail_low = row < 2, (row >= 2) & (row < 4), (row >= 4) & (row < 6)
    zero = jnp.zeros((8, LANES), f32)

    def gather(x, index):
        return jnp.take_along_axis(x, index, axis=1)

    def place(s, carry):
        start = s * BLOCK
        t0 = start // TILE
        a = start - t0 * TILE
        tiles = []
        for t in range(PACK_ROWS // 16):
            both = recv_ref[s, 16 * t:16 * t + 16, :].astype(f32)
            tiles += [both[0:8], both[8:16]]
        now, later = place_ref[pl.ds(t0, 1), :], place_ref[pl.ds(t0 + 1, 1), :]
        following = []
        for half in range(2):
            side = slice(half * LANES, (half + 1) * LANES)
            mask = lane + half * LANES >= a
            spill = lane + (half * LANES + TILE) < a + BLOCK
            r = jnp.where(mask, now[:, side], later[:, side])
            p = (r + o) & 127
            p2 = p ^ 64
            far = r >= LANES
            first = ((p - o) & 127) < 64
            out = []
            for g in range(6):
                source, index = tiles[(6, 7, 6, 7, 8, 9)[g]], p2 if g in (2, 3) else p
                out.append(jnp.where(far, gather(source, index), gather(tiles[g], p)))
            near, turned = gather(tiles[8], p), gather(tiles[8], p2)
            out.append(jnp.where(far & tail_hi | ~far & first & tail_low, turned,
                                 jnp.where(~far & ~first & tail_mid, near, zero)))
            merged = [jnp.where(mask, out[g], carry[7 * half + g]) for g in range(7)]
            for g in range(4):
                pair = jnp.concatenate([merged[2 * g], merged[2 * g + 1] if g < 3 else zero], axis=0)
                cols_ref[t0, 16 * g:16 * g + 16, side] = pair.astype(bf16)
            following += [jnp.where(spill, out[g], merged[g]) for g in range(7)]
        return tuple(following)

    return place, (zero,) * 14


def member_kernel(scalar_ref, arrived_ref, place_ref, table_ref, assign_ref,
                  hist_ref, keep_ref, send_ref, cols_ref, even_ref, odd_ref, recv_ref, sems):
    core = scalar_ref[1]

    def load(at):
        span = (pl.ds(0, EARLY), pl.ds(EARLY, DEVICES - EARLY))[at]
        return pltpu.make_async_copy(arrived_ref.at[span], recv_ref.at[span], sems.at[at])

    load(0).start()
    load(1).start()
    place, carry = place_columns(scalar_ref[0], recv_ref, place_ref, cols_ref)

    def products(i, out_ref):
        h = jnp.concatenate([cols_ref[2 * i], cols_ref[2 * i + 1]], axis=1)
        out_ref[...] = jnp.dot(
            table_ref[...], jnp.concatenate([h, h, h], axis=0), preferred_element_type=f32)

    def add_kid(z_ref):
        for c in range(HANDS // LANES):
            at = slice(c * LANES, (c + 1) * LANES)
            cdf = z_ref[200:256, at]
            total = z_ref[256:264, at]
            sq = jnp.sum(cdf * cdf, axis=0, keepdims=True)
            extra = total + sharpness * sq / total
            y = z_ref[0:200, at].reshape(25, 8, LANES) + extra[None]
            w = 1.0 / (y * y)
            scale = 1.0 / jnp.sum(jnp.sum(w, axis=0), axis=0, keepdims=True)
            hist_ref[:, at] += (w * scale[None]).reshape(200, LANES)

    hist_ref[...] = jnp.zeros_like(hist_ref)
    load(0).wait()
    carry = lax.fori_loop(0, AHEAD, place, carry, unroll=3)
    products(0, even_ref)

    def two_kids(j, carry):
        def some(at, carry):
            for k in range(AHEAD // 2):
                carry = place(jnp.minimum(AHEAD * (j + 1) + at + k, DEVICES - 1), carry)
            return carry

        @pl.when(j == 1)
        def _():
            load(1).wait()

        products(2 * j + 1, odd_ref)
        carry = some(0, carry)
        add_kid(even_ref)
        products(2 * j + 2, even_ref)
        carry = some(AHEAD // 2, carry)
        add_kid(odd_ref)
        return carry

    lax.fori_loop(0, KIDS // 2, two_kids, carry)
    add_kid(even_ref)

    hi = hist_ref[...].astype(bf16)
    rest = (hist_ref[...] - hi.astype(f32)).astype(bf16)
    stack = jnp.concatenate([hi, rest], axis=0)
    ids = lax.broadcasted_iota(i32, (LANES, HANDS), 0)
    valid = ids < PANEL
    for i in range(8):
        halves = []
        for side in (core, 1 - core):
            base = PANEL * (2 * i + side)
            halves.append((valid & (assign_ref[...] - base == ids)).astype(f32).astype(bf16))
        onehot = jnp.concatenate(halves, axis=0)
        sums = lax.dot_general(stack, onehot, (((1,), (1,)), ((), ())), preferred_element_type=f32)
        both = sums[0:200] + sums[200:400]
        keep_ref[i] = both[:, :LANES]
        send_ref[i] = both[:, LANES:]


VMEM = pl.BlockSpec(memory_space=pltpu.VMEM)
SMEM = pl.BlockSpec(memory_space=pltpu.SMEM)


def member(scalars, recv, place, table, assign):
    return pl.pallas_call(
        member_kernel,
        in_specs=[SMEM, pl.BlockSpec(memory_space=pl.ANY), VMEM, VMEM, VMEM],
        out_specs=[VMEM, VMEM, VMEM],
        out_shape=[
            jax.ShapeDtypeStruct((TURN_CENT, HANDS), f32),
            jax.ShapeDtypeStruct((8, TURN_CENT, LANES), f32),
            jax.ShapeDtypeStruct((8, TURN_CENT, LANES), f32),
        ],
        scratch_shapes=[
            pltpu.VMEM((TILES, 64, TILE), bf16),
            pltpu.VMEM((264, HANDS), f32),
            pltpu.VMEM((264, HANDS), f32),
            pltpu.VMEM((DEVICES, PACK_ROWS, LANES), bf16),
            pltpu.SemaphoreType.DMA((2,)),
        ],
        name="member",
    )(scalars, recv, place, table, assign)


def nearest_kernel(mine_ref, partner_ref, *refs):
    pieces, out_ref = refs[:-1], refs[-1]
    one = jnp.where(lax.broadcasted_iota(i32, (8, 2 * HANDS), 0) == 0, 1.0, 0.0)
    hands = jnp.concatenate([jnp.concatenate([mine_ref[...], partner_ref[...]], axis=1), one], axis=0)
    lane = lax.broadcasted_iota(i32, (8, LANES), 1)
    best = None
    for ref in pieces:
        c = ref[0:TURN_CENT, :]
        sq = jnp.broadcast_to(jnp.sum(c * c, axis=0, keepdims=True), (8, LANES))
        sides = jnp.concatenate([-2.0 * c, jnp.where(lane < PANEL, sq, 1e30)], axis=0)
        dist = lax.dot_general(
            sides, hands, (((0,), (0,)), ((), ())), precision=highest, preferred_element_type=f32)
        part = jnp.min(dist, axis=0, keepdims=True)
        best = part if best is None else jnp.minimum(best, part)
    out_ref[...] = best


def nearest_of(pieces, flop_hist, partner):
    best = pl.pallas_call(
        nearest_kernel,
        in_specs=[VMEM] * (2 + len(pieces)),
        out_specs=VMEM,
        out_shape=jax.ShapeDtypeStruct((1, 2 * HANDS), f32),
        name="nearest",
    )(flop_hist, partner, *pieces)
    best = jnp.minimum(best[:, :HANDS], swap(best[:, HANDS:], "cent", 1))
    return best[0] + jnp.sum(jnp.square(flop_hist), axis=0)


def center_table(turn_centers):
    table = fold_table(BINS)
    values = turn_centers.astype(f32)
    normal = values / jnp.sum(values, axis=0, keepdims=True)
    center_cdf = jnp.dot(table, normal, precision=highest, preferred_element_type=f32)
    center_sq = jnp.sum(center_cdf * center_cdf, axis=0)
    folded = lax.dot_general(
        center_cdf, table, (((0,), (0,)), ((), ())), precision=highest, preferred_element_type=f32)
    folded = sharpness * center_sq[:, None] - 2.0 * sharpness * folded

    def spread(x):
        return jnp.concatenate(
            [x[:, :48], x[:, 48:], x[:, 48:], x[:, 48:], jnp.zeros((x.shape[0], 10), f32)], axis=1)

    hi = lax.reduce_precision(folded, 8, 7)
    mid = lax.reduce_precision(folded - hi, 8, 7)
    low = lax.reduce_precision(folded - hi - mid, 8, 7)
    top = jnp.concatenate([spread(hi), spread(mid), spread(low)], axis=1)
    rows = jnp.concatenate([table, jnp.zeros((6, BINS), f32), jnp.ones((8, BINS), f32)], axis=0)
    bottom = jnp.concatenate([spread(rows), jnp.zeros((64, 128), f32)], axis=1)
    return jnp.concatenate([top, bottom], axis=0).astype(bf16)


CHIPS = [[2 * i + c for i in range(8)] for c in range(2)]


def swap(x, axis, mask):
    size = 8 if axis == "board" else 16
    return lax.ppermute(x, axis, [(i, i ^ mask) for i in range(size)])


def body(turn_hist, turn_assign, child_rows, turn_centers, flop_centers, flop_assign):
    sent = pack(turn_hist)
    turn_assign, sent = lax.optimization_barrier((turn_assign, sent))
    arrived = lax.all_to_all(sent, ("board", "cent"), split_axis=0, concat_axis=0, tiled=True)

    device = lax.axis_index("board") * 16 + lax.axis_index("cent")
    offset = (device * BLOCK) % LANES
    scalars = jnp.stack([offset, lax.axis_index("cent") % 2]).astype(i32)

    turn_part = turn_partial(turn_hist, turn_assign[None, :])
    own = jnp.concatenate([jnp.pad(flop_centers, ((0, 0), (0, LANES - PANEL))), turn_part], axis=0)
    pieces = [own]
    for mask in range(2, 16, 2):
        pieces.append(swap(own, "cent", mask))

    place = jnp.concatenate([child_rows.reshape(TILES, TILE), jnp.zeros((2, TILE), i32)], axis=0)
    table = center_table(turn_centers)
    place, table, scalars = lax.optimization_barrier((place, table, scalars))

    flop_hist, keep, send = member(scalars, arrived, place, table, flop_assign[None, :])

    turn_part = sum((piece[TURN_CENT:] for piece in pieces[1:]), turn_part)
    turn_part = turn_part + swap(turn_part, "cent", 1)
    received, partner = lax.optimization_barrier((swap(send, "cent", 1), swap(flop_hist, "cent", 1)))
    half = keep + received
    parts = lax.all_to_all(half, "cent", split_axis=0, concat_axis=0, tiled=True, axis_index_groups=CHIPS)
    total = jnp.concatenate([jnp.sum(parts, axis=0), turn_part], axis=0)
    for mask in (1, 2, 6):
        total = total + swap(total, "board", mask)
    flop_sums = total[:TURN_CENT, :PANEL].T * (PANEL * 16 / (HANDS * DEVICES))
    turn_low = total[TURN_CENT:TURN_CENT + BINS]
    turn_high = total[TURN_CENT + TURN_SPLIT:TURN_CENT + TURN_SPLIT + BINS, :TURN_CENT - LANES]
    turn_sums = jnp.concatenate([turn_low, turn_high], axis=1)
    turn_sums = turn_sums * (BINS * TURN_CENT / (turn_hist.shape[1] * DEVICES))

    nearest = nearest_of(pieces, flop_hist, partner)
    return nearest, turn_sums, flop_sums


def solution(mesh):
    in_specs = (
        P(None, ("board", "cent")),
        P(("board", "cent")),
        P(None, ("board", "cent")),
        P(),
        P(None, "cent"),
        P(("board", "cent")),
    )
    out_specs = (P(("board", "cent")), P(), P("cent", None))
    return jax.shard_map(body, mesh=mesh, in_specs=in_specs, out_specs=out_specs, check_vma=False)
```

```python
import jax
import jax.numpy as jnp
from jax import lax
from jax.experimental import pallas as pl
from jax.experimental.pallas import tpu as pltpu
from jax.sharding import PartitionSpec as P


sharpness = 4.0
highest = lax.Precision.HIGHEST
f32, bf16, i32 = jnp.float32, jnp.bfloat16, jnp.int32
LANES = 128
BLOCK = 188
BINS = 50
KIDS = 47
TURN_CENT = 200
HANDS = 512
PANEL = 125
DEVICES = 128
SOURCES_PER_STEP = 32
PACK_ROWS = 80
TURN_SPLIT = 56
TURN_ROWS = 112


def fold_table(bins):
    upper = lax.iota(i32, bins)[:, None]
    lower = lax.iota(i32, bins)[None, :]
    table = 0.5 * (lower <= upper).astype(f32)
    table = table + 0.25 * (lower <= upper - 1).astype(f32)
    table = table + 0.25 * ((lower <= upper + 1) & (lower >= 1)).astype(f32)
    return table


def pack_kernel(hist_ref, out_ref):
    lane = lax.broadcasted_iota(i32, (16, LANES), 1)
    for d in range(SOURCES_PER_STEP):
        t0, o = divmod(BLOCK * d, LANES)
        three = o + BLOCK > 2 * LANES

        def parts(lo, hi):
            tiles = [hist_ref[lo:hi, (t0 + t) * LANES:(t0 + t + 1) * LANES].astype(f32)
                     for t in range(3 if three else 2)]
            upper = lane[:hi - lo] >= o
            a = jnp.where(upper, tiles[0], tiles[1]) if o else tiles[0]
            b = jnp.where(upper, tiles[1], tiles[2]) if three else tiles[1]
            return a, b

        a0, b0 = parts(0, 16)
        a1, b1 = parts(16, 32)
        a2, b2 = parts(32, 48)
        a3, b3 = parts(48, 50)
        first = ((lane - o) & 127) < 64
        out_ref[d, 0:16, :] = a0.astype(bf16)
        out_ref[d, 16:32, :] = a1.astype(bf16)
        out_ref[d, 32:48, :] = a2.astype(bf16)
        out_ref[d, 48:64, :] = jnp.where(first, b0, pltpu.roll(b1, 64, 1)).astype(bf16)
        tail = jnp.concatenate(
            [pltpu.roll(b3, 64, 1), a3, pltpu.roll(a3, 64, 1), jnp.zeros((10, LANES), f32)], axis=0)
        out_ref[d, 64:80, :] = jnp.where(first, b2, tail).astype(bf16)


def pack(turn_hist):
    width = SOURCES_PER_STEP * BLOCK
    return pl.pallas_call(
        pack_kernel,
        grid=(DEVICES // SOURCES_PER_STEP,),
        in_specs=[pl.BlockSpec((BINS, width), lambda i: (0, i))],
        out_specs=pl.BlockSpec((SOURCES_PER_STEP, PACK_ROWS, LANES), lambda i: (i, 0, 0)),
        out_shape=jax.ShapeDtypeStruct((DEVICES, PACK_ROWS, LANES), bf16),
        name="pack",
    )(turn_hist)


def turn_kernel(hist_ref, label_ref, out_ref):
    @pl.when(pl.program_id(0) == 0)
    def _():
        out_ref[...] = jnp.zeros_like(out_ref)

    values = hist_ref[...].astype(f32)
    normal = values / jnp.sum(values, axis=0, keepdims=True)
    hi = normal.astype(bf16)
    rest = normal - hi.astype(f32)
    mid = rest.astype(bf16)
    low = (rest - mid.astype(f32)).astype(bf16)
    ids = lax.broadcasted_iota(i32, (TURN_CENT, values.shape[1]), 0)
    onehot = (label_ref[...] == ids).astype(f32).astype(bf16)
    total = None
    for part in (hi, mid, low):
        more = lax.dot_general(part, onehot, (((1,), (1,)), ((), ())), preferred_element_type=f32)
        total = more if total is None else total + more
    out_ref[0:BINS, :] += total[:, :LANES]
    out_ref[TURN_SPLIT:TURN_SPLIT + BINS, 0:TURN_CENT - LANES] += total[:, LANES:]


def turn_partial(turn_hist, labels):
    width = SOURCES_PER_STEP * BLOCK // 2 if (SOURCES_PER_STEP * BLOCK // 2) % LANES == 0 else SOURCES_PER_STEP * BLOCK
    steps = turn_hist.shape[1] // width
    return pl.pallas_call(
        turn_kernel,
        grid=(steps,),
        in_specs=[pl.BlockSpec((BINS, width), lambda i: (0, i)), pl.BlockSpec((1, width), lambda i: (0, i))],
        out_specs=pl.BlockSpec((TURN_ROWS, LANES), lambda i: (0, 0)),
        out_shape=jax.ShapeDtypeStruct((TURN_ROWS, LANES), f32),
        name="turn_sums",
    )(turn_hist, labels)


TILE = 256
TILES = KIDS * HANDS // TILE
AHEAD = 6


def place_columns(o, recv_ref, place_ref, cols_ref):
    row = lax.broadcasted_iota(i32, (8, LANES), 0)
    lane = lax.broadcasted_iota(i32, (8, LANES), 1)
    tail_hi, tail_mid, tail_low = row < 2, (row >= 2) & (row < 4), (row >= 4) & (row < 6)
    zero = jnp.zeros((8, LANES), f32)

    def gather(x, index):
        return jnp.take_along_axis(x, index, axis=1)

    def place(s, carry):
        start = s * BLOCK
        t0 = start // TILE
        a = start - t0 * TILE
        tiles = []
        for t in range(PACK_ROWS // 16):
            both = recv_ref[s, 16 * t:16 * t + 16, :].astype(f32)
            tiles += [both[0:8], both[8:16]]
        now, later = place_ref[pl.ds(t0, 1), :], place_ref[pl.ds(t0 + 1, 1), :]
        following = []
        for half in range(2):
            side = slice(half * LANES, (half + 1) * LANES)
            mask = lane + half * LANES >= a
            spill = lane + (half * LANES + TILE) < a + BLOCK
            r = jnp.where(mask, now[:, side], later[:, side])
            p = (r + o) & 127
            p2 = p ^ 64
            far = r >= LANES
            first = ((p - o) & 127) < 64
            out = []
            for g in range(6):
                source, index = tiles[(6, 7, 6, 7, 8, 9)[g]], p2 if g in (2, 3) else p
                out.append(jnp.where(far, gather(source, index), gather(tiles[g], p)))
            near, turned = gather(tiles[8], p), gather(tiles[8], p2)
            out.append(jnp.where(far & tail_hi | ~far & first & tail_low, turned,
                                 jnp.where(~far & ~first & tail_mid, near, zero)))
            merged = [jnp.where(mask, out[g], carry[7 * half + g]) for g in range(7)]
            for g in range(4):
                pair = jnp.concatenate([merged[2 * g], merged[2 * g + 1] if g < 3 else zero], axis=0)
                cols_ref[t0, 16 * g:16 * g + 16, side] = pair.astype(bf16)
            following += [jnp.where(spill, out[g], merged[g]) for g in range(7)]
        return tuple(following)

    return place, (zero,) * 14


def member_kernel(scalar_ref, recv_ref, place_ref, table_ref, assign_ref,
                  hist_ref, keep_ref, send_ref, cols_ref, even_ref, odd_ref):
    core = scalar_ref[1]
    place, carry = place_columns(scalar_ref[0], recv_ref, place_ref, cols_ref)

    def products(i, out_ref):
        h = jnp.concatenate([cols_ref[2 * i], cols_ref[2 * i + 1]], axis=1)
        out_ref[...] = jnp.dot(
            table_ref[...], jnp.concatenate([h, h, h], axis=0), preferred_element_type=f32)

    def add_kid(z_ref):
        for c in range(HANDS // LANES):
            at = slice(c * LANES, (c + 1) * LANES)
            cdf = z_ref[200:256, at]
            total = z_ref[256:264, at]
            sq = jnp.sum(cdf * cdf, axis=0, keepdims=True)
            extra = total + sharpness * sq / total
            y = z_ref[0:200, at].reshape(25, 8, LANES) + extra[None]
            w = 1.0 / (y * y)
            scale = 1.0 / jnp.sum(jnp.sum(w, axis=0), axis=0, keepdims=True)
            hist_ref[:, at] += (w * scale[None]).reshape(200, LANES)

    hist_ref[...] = jnp.zeros_like(hist_ref)
    carry = lax.fori_loop(0, AHEAD, place, carry, unroll=3)
    products(0, even_ref)

    def two_kids(j, carry):
        def some(at, carry):
            for k in range(AHEAD // 2):
                carry = place(jnp.minimum(AHEAD * (j + 1) + at + k, DEVICES - 1), carry)
            return carry

        products(2 * j + 1, odd_ref)
        carry = some(0, carry)
        add_kid(even_ref)
        products(2 * j + 2, even_ref)
        carry = some(AHEAD // 2, carry)
        add_kid(odd_ref)
        return carry

    lax.fori_loop(0, KIDS // 2, two_kids, carry)
    add_kid(even_ref)

    hi = hist_ref[...].astype(bf16)
    rest = (hist_ref[...] - hi.astype(f32)).astype(bf16)
    stack = jnp.concatenate([hi, rest], axis=0)
    ids = lax.broadcasted_iota(i32, (LANES, HANDS), 0)
    valid = ids < PANEL
    for i in range(8):
        halves = []
        for side in (core, 1 - core):
            base = PANEL * (2 * i + side)
            halves.append((valid & (assign_ref[...] - base == ids)).astype(f32).astype(bf16))
        onehot = jnp.concatenate(halves, axis=0)
        sums = lax.dot_general(stack, onehot, (((1,), (1,)), ((), ())), preferred_element_type=f32)
        both = sums[0:200] + sums[200:400]
        keep_ref[i] = both[:, :LANES]
        send_ref[i] = both[:, LANES:]


VMEM = pl.BlockSpec(memory_space=pltpu.VMEM)
SMEM = pl.BlockSpec(memory_space=pltpu.SMEM)


def member(scalars, recv, place, table, assign):
    return pl.pallas_call(
        member_kernel,
        in_specs=[SMEM, VMEM, VMEM, VMEM, VMEM],
        out_specs=[VMEM, VMEM, VMEM],
        out_shape=[
            jax.ShapeDtypeStruct((TURN_CENT, HANDS), f32),
            jax.ShapeDtypeStruct((8, TURN_CENT, LANES), f32),
            jax.ShapeDtypeStruct((8, TURN_CENT, LANES), f32),
        ],
        scratch_shapes=[
            pltpu.VMEM((TILES, 64, TILE), bf16),
            pltpu.VMEM((264, HANDS), f32),
            pltpu.VMEM((264, HANDS), f32),
        ],
        compiler_params=pltpu.CompilerParams(vmem_limit_bytes=24 * 1024 * 1024),
        name="member",
    )(scalars, recv, place, table, assign)


def nearest_kernel(mine_ref, partner_ref, *refs):
    pieces, out_ref = refs[:-1], refs[-1]
    one = jnp.where(lax.broadcasted_iota(i32, (8, 2 * HANDS), 0) == 0, 1.0, 0.0)
    hands = jnp.concatenate([jnp.concatenate([mine_ref[...], partner_ref[...]], axis=1), one], axis=0)
    lane = lax.broadcasted_iota(i32, (8, LANES), 1)
    best = None
    for ref in pieces:
        c = ref[0:TURN_CENT, :]
        sq = jnp.broadcast_to(jnp.sum(c * c, axis=0, keepdims=True), (8, LANES))
        sides = jnp.concatenate([-2.0 * c, jnp.where(lane < PANEL, sq, 1e30)], axis=0)
        dist = lax.dot_general(
            sides, hands, (((0,), (0,)), ((), ())), precision=highest, preferred_element_type=f32)
        part = jnp.min(dist, axis=0, keepdims=True)
        best = part if best is None else jnp.minimum(best, part)
    out_ref[...] = best


def nearest_of(pieces, flop_hist, partner):
    best = pl.pallas_call(
        nearest_kernel,
        in_specs=[VMEM] * (2 + len(pieces)),
        out_specs=VMEM,
        out_shape=jax.ShapeDtypeStruct((1, 2 * HANDS), f32),
    compiler_params=pltpu.CompilerParams(vmem_limit_bytes=24 * 1024 * 1024),
        name="nearest",
    )(flop_hist, partner, *pieces)
    best = jnp.minimum(best[:, :HANDS], swap(best[:, HANDS:], "cent", 1))
    return best[0] + jnp.sum(jnp.square(flop_hist), axis=0)


def center_table(turn_centers):
    table = fold_table(BINS)
    values = turn_centers.astype(f32)
    normal = values / jnp.sum(values, axis=0, keepdims=True)
    center_cdf = jnp.dot(table, normal, precision=highest, preferred_element_type=f32)
    center_sq = jnp.sum(center_cdf * center_cdf, axis=0)
    folded = lax.dot_general(
        center_cdf, table, (((0,), (0,)), ((), ())), precision=highest, preferred_element_type=f32)
    folded = sharpness * center_sq[:, None] - 2.0 * sharpness * folded

    def spread(x):
        return jnp.concatenate(
            [x[:, :48], x[:, 48:], x[:, 48:], x[:, 48:], jnp.zeros((x.shape[0], 10), f32)], axis=1)

    hi = lax.reduce_precision(folded, 8, 7)
    mid = lax.reduce_precision(folded - hi, 8, 7)
    low = lax.reduce_precision(folded - hi - mid, 8, 7)
    top = jnp.concatenate([spread(hi), spread(mid), spread(low)], axis=1)
    rows = jnp.concatenate([table, jnp.zeros((6, BINS), f32), jnp.ones((8, BINS), f32)], axis=0)
    bottom = jnp.concatenate([spread(rows), jnp.zeros((64, 128), f32)], axis=1)
    return jnp.concatenate([top, bottom], axis=0).astype(bf16)


CHIPS = [[2 * i + c for i in range(8)] for c in range(2)]


def swap(x, axis, mask):
    size = 8 if axis == "board" else 16
    return lax.ppermute(x, axis, [(i, i ^ mask) for i in range(size)])


def body(turn_hist, turn_assign, child_rows, turn_centers, flop_centers, flop_assign):
    sent = pack(turn_hist)
    turn_assign, sent = lax.optimization_barrier((turn_assign, sent))
    arrived = lax.all_to_all(sent, ("board", "cent"), split_axis=0, concat_axis=0, tiled=True)

    device = lax.axis_index("board") * 16 + lax.axis_index("cent")
    offset = (device * BLOCK) % LANES
    scalars = jnp.stack([offset, lax.axis_index("cent") % 2]).astype(i32)

    turn_part = turn_partial(turn_hist, turn_assign[None, :])
    own = jnp.concatenate([jnp.pad(flop_centers, ((0, 0), (0, LANES - PANEL))), turn_part], axis=0)
    pieces = [own]
    for mask in range(2, 16, 2):
        pieces.append(swap(own, "cent", mask))

    place = jnp.concatenate([child_rows.reshape(TILES, TILE), jnp.zeros((2, TILE), i32)], axis=0)
    table = center_table(turn_centers)
    place, table, scalars = lax.optimization_barrier((place, table, scalars))

    flop_hist, keep, send = member(scalars, arrived, place, table, flop_assign[None, :])

    turn_part = sum((piece[TURN_CENT:] for piece in pieces[1:]), turn_part)
    turn_part = turn_part + swap(turn_part, "cent", 1)
    turn_part = turn_part + swap(turn_part, "board", 1)
    received, partner = lax.optimization_barrier((swap(send, "cent", 1), swap(flop_hist, "cent", 1)))
    half = keep + received
    parts = lax.all_to_all(half, "cent", split_axis=0, concat_axis=0, tiled=True, axis_index_groups=CHIPS)
    flop_part = jnp.sum(parts, axis=0)
    flop_part = flop_part + swap(flop_part, "board", 1)
    total = jnp.concatenate([flop_part, turn_part], axis=0)
    total = (total + swap(total, "board", 2)) + (swap(total, "board", 4) + swap(total, "board", 6))
    flop_sums = total[:TURN_CENT, :PANEL].T * (PANEL * 16 / (HANDS * DEVICES))
    turn_low = total[TURN_CENT:TURN_CENT + BINS]
    turn_high = total[TURN_CENT + TURN_SPLIT:TURN_CENT + TURN_SPLIT + BINS, :TURN_CENT - LANES]
    turn_sums = jnp.concatenate([turn_low, turn_high], axis=1)
    turn_sums = turn_sums * (BINS * TURN_CENT / (turn_hist.shape[1] * DEVICES))

    nearest = nearest_of(pieces, flop_hist, partner)
    return nearest, turn_sums, flop_sums


def solution(mesh):
    in_specs = (
        P(None, ("board", "cent")),
        P(("board", "cent")),
        P(None, ("board", "cent")),
        P(),
        P(None, "cent"),
        P(("board", "cent")),
    )
    out_specs = (P(("board", "cent")), P(), P("cent", None))
    return jax.shard_map(body, mesh=mesh, in_specs=in_specs, out_specs=out_specs, check_vma=False)
```

```python
import jax
import jax.numpy as jnp
from jax import lax
from jax.experimental import pallas as pl
from jax.experimental.pallas import tpu as pltpu
from jax.sharding import PartitionSpec as P


sharpness = 4.0
highest = lax.Precision.HIGHEST
f32, bf16, i32 = jnp.float32, jnp.bfloat16, jnp.int32
LANES = 128
BLOCK = 188
BINS = 50
KIDS = 47
TURN_CENT = 200
HANDS = 512
PANEL = 125
DEVICES = 128
SOURCES_PER_STEP = 32
PACK_ROWS = 80
TURN_SPLIT = 56
TURN_ROWS = 112


def fold_table(bins):
    upper = lax.iota(i32, bins)[:, None]
    lower = lax.iota(i32, bins)[None, :]
    table = 0.5 * (lower <= upper).astype(f32)
    table = table + 0.25 * (lower <= upper - 1).astype(f32)
    table = table + 0.25 * ((lower <= upper + 1) & (lower >= 1)).astype(f32)
    return table


def pack_kernel(hist_ref, out_ref):
    lane = lax.broadcasted_iota(i32, (16, LANES), 1)
    for d in range(SOURCES_PER_STEP):
        t0, o = divmod(BLOCK * d, LANES)
        three = o + BLOCK > 2 * LANES

        def parts(lo, hi):
            tiles = [hist_ref[lo:hi, (t0 + t) * LANES:(t0 + t + 1) * LANES].astype(f32)
                     for t in range(3 if three else 2)]
            upper = lane[:hi - lo] >= o
            a = jnp.where(upper, tiles[0], tiles[1]) if o else tiles[0]
            b = jnp.where(upper, tiles[1], tiles[2]) if three else tiles[1]
            return a, b

        a0, b0 = parts(0, 16)
        a1, b1 = parts(16, 32)
        a2, b2 = parts(32, 48)
        a3, b3 = parts(48, 50)
        first = ((lane - o) & 127) < 64
        out_ref[d, 0:16, :] = a0.astype(bf16)
        out_ref[d, 16:32, :] = a1.astype(bf16)
        out_ref[d, 32:48, :] = a2.astype(bf16)
        out_ref[d, 48:64, :] = jnp.where(first, b0, pltpu.roll(b1, 64, 1)).astype(bf16)
        tail = jnp.concatenate(
            [pltpu.roll(b3, 64, 1), a3, pltpu.roll(a3, 64, 1), jnp.zeros((10, LANES), f32)], axis=0)
        out_ref[d, 64:80, :] = jnp.where(first, b2, tail).astype(bf16)


def pack(turn_hist):
    width = SOURCES_PER_STEP * BLOCK
    return pl.pallas_call(
        pack_kernel,
        grid=(DEVICES // SOURCES_PER_STEP,),
        in_specs=[pl.BlockSpec((BINS, width), lambda i: (0, i))],
        out_specs=pl.BlockSpec((SOURCES_PER_STEP, PACK_ROWS, LANES), lambda i: (i, 0, 0)),
        out_shape=jax.ShapeDtypeStruct((DEVICES, PACK_ROWS, LANES), bf16),
        name="pack",
    )(turn_hist)


def turn_kernel(hist_ref, label_ref, out_ref):
    @pl.when(pl.program_id(0) == 0)
    def _():
        out_ref[...] = jnp.zeros_like(out_ref)

    values = hist_ref[...].astype(f32)
    normal = values / jnp.sum(values, axis=0, keepdims=True)
    hi = normal.astype(bf16)
    rest = normal - hi.astype(f32)
    mid = rest.astype(bf16)
    low = (rest - mid.astype(f32)).astype(bf16)
    ids = lax.broadcasted_iota(i32, (TURN_CENT, values.shape[1]), 0)
    onehot = (label_ref[...] == ids).astype(f32).astype(bf16)
    total = None
    for part in (hi, mid, low):
        more = lax.dot_general(part, onehot, (((1,), (1,)), ((), ())), preferred_element_type=f32)
        total = more if total is None else total + more
    out_ref[0:BINS, :] += total[:, :LANES]
    out_ref[TURN_SPLIT:TURN_SPLIT + BINS, 0:TURN_CENT - LANES] += total[:, LANES:]


def turn_partial(turn_hist, labels):
    width = SOURCES_PER_STEP * BLOCK // 2 if (SOURCES_PER_STEP * BLOCK // 2) % LANES == 0 else SOURCES_PER_STEP * BLOCK
    steps = turn_hist.shape[1] // width
    return pl.pallas_call(
        turn_kernel,
        grid=(steps,),
        in_specs=[pl.BlockSpec((BINS, width), lambda i: (0, i)), pl.BlockSpec((1, width), lambda i: (0, i))],
        out_specs=pl.BlockSpec((TURN_ROWS, LANES), lambda i: (0, 0)),
        out_shape=jax.ShapeDtypeStruct((TURN_ROWS, LANES), f32),
        name="turn_sums",
    )(turn_hist, labels)


TILE = 256
TILES = KIDS * HANDS // TILE
AHEAD = 6


def place_columns(o, recv_ref, place_ref, cols_ref):
    row = lax.broadcasted_iota(i32, (8, LANES), 0)
    lane = lax.broadcasted_iota(i32, (8, LANES), 1)
    tail_hi, tail_mid, tail_low = row < 2, (row >= 2) & (row < 4), (row >= 4) & (row < 6)
    zero = jnp.zeros((8, LANES), f32)

    def gather(x, index):
        return jnp.take_along_axis(x, index, axis=1)

    def place(s, carry):
        start = s * BLOCK
        t0 = start // TILE
        a = start - t0 * TILE
        tiles = []
        for t in range(PACK_ROWS // 16):
            both = recv_ref[s, 16 * t:16 * t + 16, :].astype(f32)
            tiles += [both[0:8], both[8:16]]
        now, later = place_ref[pl.ds(t0, 1), :], place_ref[pl.ds(t0 + 1, 1), :]
        following = []
        for half in range(2):
            side = slice(half * LANES, (half + 1) * LANES)
            mask = lane + half * LANES >= a
            spill = lane + (half * LANES + TILE) < a + BLOCK
            r = jnp.where(mask, now[:, side], later[:, side])
            p = (r + o) & 127
            p2 = p ^ 64
            far = r >= LANES
            first = ((p - o) & 127) < 64
            out = []
            for g in range(6):
                source, index = tiles[(6, 7, 6, 7, 8, 9)[g]], p2 if g in (2, 3) else p
                out.append(jnp.where(far, gather(source, index), gather(tiles[g], p)))
            near, turned = gather(tiles[8], p), gather(tiles[8], p2)
            out.append(jnp.where(far & tail_hi | ~far & first & tail_low, turned,
                                 jnp.where(~far & ~first & tail_mid, near, zero)))
            merged = [jnp.where(mask, out[g], carry[7 * half + g]) for g in range(7)]
            for g in range(4):
                pair = jnp.concatenate([merged[2 * g], merged[2 * g + 1] if g < 3 else zero], axis=0)
                cols_ref[t0, 16 * g:16 * g + 16, side] = pair.astype(bf16)
            following += [jnp.where(spill, out[g], merged[g]) for g in range(7)]
        return tuple(following)

    return place, (zero,) * 14


def member_kernel(scalar_ref, recv_ref, place_ref, table_ref, assign_ref,
                  hist_ref, keep_ref, send_ref, cols_ref, even_ref, odd_ref):
    core = scalar_ref[1]
    place, carry = place_columns(scalar_ref[0], recv_ref, place_ref, cols_ref)

    def products(i, out_ref):
        h = jnp.concatenate([cols_ref[2 * i], cols_ref[2 * i + 1]], axis=1)
        out_ref[...] = jnp.dot(
            table_ref[...], jnp.concatenate([h, h, h], axis=0), preferred_element_type=f32)

    def add_kid(z_ref):
        for c in range(HANDS // LANES):
            at = slice(c * LANES, (c + 1) * LANES)
            cdf = z_ref[200:256, at]
            total = z_ref[256:264, at]
            sq = jnp.sum(cdf * cdf, axis=0, keepdims=True)
            extra = total + sharpness * sq / total
            y = z_ref[0:200, at].reshape(25, 8, LANES) + extra[None]
            w = 1.0 / (y * y)
            scale = 1.0 / jnp.sum(jnp.sum(w, axis=0), axis=0, keepdims=True)
            hist_ref[:, at] += (w * scale[None]).reshape(200, LANES)

    hist_ref[...] = jnp.zeros_like(hist_ref)
    carry = lax.fori_loop(0, AHEAD, place, carry, unroll=3)
    products(0, even_ref)

    def two_kids(j, carry):
        def some(at, carry):
            for k in range(AHEAD // 2):
                carry = place(jnp.minimum(AHEAD * (j + 1) + at + k, DEVICES - 1), carry)
            return carry

        products(2 * j + 1, odd_ref)
        carry = some(0, carry)
        add_kid(even_ref)
        products(2 * j + 2, even_ref)
        carry = some(AHEAD // 2, carry)
        add_kid(odd_ref)
        return carry

    lax.fori_loop(0, KIDS // 2, two_kids, carry)
    add_kid(even_ref)

    hi = hist_ref[...].astype(bf16)
    rest = (hist_ref[...] - hi.astype(f32)).astype(bf16)
    stack = jnp.concatenate([hi, rest], axis=0)
    ids = lax.broadcasted_iota(i32, (LANES, HANDS), 0)
    valid = ids < PANEL
    for i in range(8):
        halves = []
        for side in (core, 1 - core):
            base = PANEL * (2 * i + side)
            halves.append((valid & (assign_ref[...] - base == ids)).astype(f32).astype(bf16))
        onehot = jnp.concatenate(halves, axis=0)
        sums = lax.dot_general(stack, onehot, (((1,), (1,)), ((), ())), preferred_element_type=f32)
        both = sums[0:200] + sums[200:400]
        keep_ref[i] = both[:, :LANES]
        send_ref[i] = both[:, LANES:]


VMEM = pl.BlockSpec(memory_space=pltpu.VMEM)
SMEM = pl.BlockSpec(memory_space=pltpu.SMEM)


def member(scalars, recv, place, table, assign):
    return pl.pallas_call(
        member_kernel,
        in_specs=[SMEM, VMEM, VMEM, VMEM, VMEM],
        out_specs=[VMEM, VMEM, VMEM],
        out_shape=[
            jax.ShapeDtypeStruct((TURN_CENT, HANDS), f32),
            jax.ShapeDtypeStruct((8, TURN_CENT, LANES), f32),
            jax.ShapeDtypeStruct((8, TURN_CENT, LANES), f32),
        ],
        scratch_shapes=[
            pltpu.VMEM((TILES, 64, TILE), bf16),
            pltpu.VMEM((264, HANDS), f32),
            pltpu.VMEM((264, HANDS), f32),
        ],
        compiler_params=pltpu.CompilerParams(vmem_limit_bytes=24 * 1024 * 1024),
        name="member",
    )(scalars, recv, place, table, assign)


def nearest_kernel(mine_ref, partner_ref, *refs):
    pieces, out_ref = refs[:-1], refs[-1]
    one = jnp.where(lax.broadcasted_iota(i32, (8, 2 * HANDS), 0) == 0, 1.0, 0.0)
    hands = jnp.concatenate([jnp.concatenate([mine_ref[...], partner_ref[...]], axis=1), one], axis=0)
    lane = lax.broadcasted_iota(i32, (8, LANES), 1)
    best = None
    for ref in pieces:
        c = ref[0:TURN_CENT, :]
        sq = jnp.broadcast_to(jnp.sum(c * c, axis=0, keepdims=True), (8, LANES))
        sides = jnp.concatenate([-2.0 * c, jnp.where(lane < PANEL, sq, 1e30)], axis=0)
        dist = lax.dot_general(
            sides, hands, (((0,), (0,)), ((), ())), precision=highest, preferred_element_type=f32)
        part = jnp.min(dist, axis=0, keepdims=True)
        best = part if best is None else jnp.minimum(best, part)
    out_ref[...] = best


def nearest_of(pieces, flop_hist, partner):
    best = pl.pallas_call(
        nearest_kernel,
        in_specs=[VMEM] * (2 + len(pieces)),
        out_specs=VMEM,
        out_shape=jax.ShapeDtypeStruct((1, 2 * HANDS), f32),
    compiler_params=pltpu.CompilerParams(vmem_limit_bytes=24 * 1024 * 1024),
        name="nearest",
    )(flop_hist, partner, *pieces)
    best = jnp.minimum(best[:, :HANDS], swap(best[:, HANDS:], "cent", 1))
    return best[0] + jnp.sum(jnp.square(flop_hist), axis=0)


def center_table(turn_centers):
    table = fold_table(BINS)
    values = turn_centers.astype(f32)
    normal = values / jnp.sum(values, axis=0, keepdims=True)
    center_cdf = jnp.dot(table, normal, precision=highest, preferred_element_type=f32)
    center_sq = jnp.sum(center_cdf * center_cdf, axis=0)
    folded = lax.dot_general(
        center_cdf, table, (((0,), (0,)), ((), ())), precision=highest, preferred_element_type=f32)
    folded = sharpness * center_sq[:, None] - 2.0 * sharpness * folded

    def spread(x):
        return jnp.concatenate(
            [x[:, :48], x[:, 48:], x[:, 48:], x[:, 48:], jnp.zeros((x.shape[0], 10), f32)], axis=1)

    hi = lax.reduce_precision(folded, 8, 7)
    mid = lax.reduce_precision(folded - hi, 8, 7)
    low = lax.reduce_precision(folded - hi - mid, 8, 7)
    top = jnp.concatenate([spread(hi), spread(mid), spread(low)], axis=1)
    rows = jnp.concatenate([table, jnp.zeros((6, BINS), f32), jnp.ones((8, BINS), f32)], axis=0)
    bottom = jnp.concatenate([spread(rows), jnp.zeros((64, 128), f32)], axis=1)
    return jnp.concatenate([top, bottom], axis=0).astype(bf16)


CHIPS = [[2 * i + c for i in range(8)] for c in range(2)]


def swap(x, axis, mask):
    size = 8 if axis == "board" else 16
    return lax.ppermute(x, axis, [(i, i ^ mask) for i in range(size)])


def add_over_z(x):
    return (x + swap(x, "board", 2)) + (swap(x, "board", 4) + swap(x, "board", 6))


def body(turn_hist, turn_assign, child_rows, turn_centers, flop_centers, flop_assign):
    sent = pack(turn_hist)
    turn_assign, sent = lax.optimization_barrier((turn_assign, sent))
    arrived = lax.all_to_all(sent, ("board", "cent"), split_axis=0, concat_axis=0, tiled=True)

    device = lax.axis_index("board") * 16 + lax.axis_index("cent")
    offset = (device * BLOCK) % LANES
    scalars = jnp.stack([offset, lax.axis_index("cent") % 2]).astype(i32)

    turn_part = turn_partial(turn_hist, turn_assign[None, :])
    own = jnp.concatenate([jnp.pad(flop_centers, ((0, 0), (0, LANES - PANEL))), turn_part], axis=0)
    pieces = [own]
    for mask in range(2, 16, 2):
        pieces.append(swap(own, "cent", mask))

    place = jnp.concatenate([child_rows.reshape(TILES, TILE), jnp.zeros((2, TILE), i32)], axis=0)
    table = center_table(turn_centers)
    place, table, scalars = lax.optimization_barrier((place, table, scalars))

    flop_hist, keep, send = member(scalars, arrived, place, table, flop_assign[None, :])

    turn_part = sum((piece[TURN_CENT:] for piece in pieces[1:]), turn_part)
    turn_part = turn_part + swap(turn_part, "cent", 1)
    turn_part = turn_part + swap(turn_part, "board", 1)
    received, partner = lax.optimization_barrier((swap(send, "cent", 1), swap(flop_hist, "cent", 1)))
    half = keep + received
    parts = lax.all_to_all(half, "cent", split_axis=0, concat_axis=0, tiled=True, axis_index_groups=CHIPS)
    flop_part, turn_part = lax.optimization_barrier((jnp.sum(parts, axis=0), turn_part))
    flop_part = flop_part + swap(flop_part, "board", 1)
    flop_part = add_over_z(flop_part)
    turn_part = add_over_z(turn_part)
    flop_sums = flop_part[:, :PANEL].T * (PANEL * 16 / (HANDS * DEVICES))
    turn_low = turn_part[:BINS]
    turn_high = turn_part[TURN_SPLIT:TURN_SPLIT + BINS, :TURN_CENT - LANES]
    turn_sums = jnp.concatenate([turn_low, turn_high], axis=1)
    turn_sums = turn_sums * (BINS * TURN_CENT / (turn_hist.shape[1] * DEVICES))

    nearest = nearest_of(pieces, flop_hist, partner)
    return nearest, turn_sums, flop_sums


def solution(mesh):
    in_specs = (
        P(None, ("board", "cent")),
        P(("board", "cent")),
        P(None, ("board", "cent")),
        P(),
        P(None, "cent"),
        P(("board", "cent")),
    )
    out_specs = (P(("board", "cent")), P(), P("cent", None))
    return jax.shard_map(body, mesh=mesh, in_specs=in_specs, out_specs=out_specs, check_vma=False)
```

```python
import jax
import jax.numpy as jnp
from jax import lax
from jax.experimental import pallas as pl
from jax.experimental.pallas import tpu as pltpu
from jax.sharding import PartitionSpec as P


sharpness = 4.0
highest = lax.Precision.HIGHEST
f32, bf16, i32 = jnp.float32, jnp.bfloat16, jnp.int32
LANES = 128
BLOCK = 188
BINS = 50
KIDS = 47
TURN_CENT = 200
HANDS = 512
PANEL = 125
DEVICES = 128
SOURCES_PER_STEP = 32
PACK_ROWS = 80
TURN_SPLIT = 56
TURN_ROWS = 112


def fold_table(bins):
    upper = lax.iota(i32, bins)[:, None]
    lower = lax.iota(i32, bins)[None, :]
    table = 0.5 * (lower <= upper).astype(f32)
    table = table + 0.25 * (lower <= upper - 1).astype(f32)
    table = table + 0.25 * ((lower <= upper + 1) & (lower >= 1)).astype(f32)
    return table


def pack_kernel(hist_ref, out_ref):
    lane = lax.broadcasted_iota(i32, (16, LANES), 1)
    for d in range(SOURCES_PER_STEP):
        t0, o = divmod(BLOCK * d, LANES)
        three = o + BLOCK > 2 * LANES

        def parts(lo, hi):
            tiles = [hist_ref[lo:hi, (t0 + t) * LANES:(t0 + t + 1) * LANES].astype(f32)
                     for t in range(3 if three else 2)]
            upper = lane[:hi - lo] >= o
            a = jnp.where(upper, tiles[0], tiles[1]) if o else tiles[0]
            b = jnp.where(upper, tiles[1], tiles[2]) if three else tiles[1]
            return a, b

        a0, b0 = parts(0, 16)
        a1, b1 = parts(16, 32)
        a2, b2 = parts(32, 48)
        a3, b3 = parts(48, 50)
        first = ((lane - o) & 127) < 64
        out_ref[d, 0:16, :] = a0.astype(bf16)
        out_ref[d, 16:32, :] = a1.astype(bf16)
        out_ref[d, 32:48, :] = a2.astype(bf16)
        out_ref[d, 48:64, :] = jnp.where(first, b0, pltpu.roll(b1, 64, 1)).astype(bf16)
        tail = jnp.concatenate(
            [pltpu.roll(b3, 64, 1), a3, pltpu.roll(a3, 64, 1), jnp.zeros((10, LANES), f32)], axis=0)
        out_ref[d, 64:80, :] = jnp.where(first, b2, tail).astype(bf16)


def pack(turn_hist):
    width = SOURCES_PER_STEP * BLOCK
    return pl.pallas_call(
        pack_kernel,
        grid=(DEVICES // SOURCES_PER_STEP,),
        in_specs=[pl.BlockSpec((BINS, width), lambda i: (0, i))],
        out_specs=pl.BlockSpec((SOURCES_PER_STEP, PACK_ROWS, LANES), lambda i: (i, 0, 0)),
        out_shape=jax.ShapeDtypeStruct((DEVICES, PACK_ROWS, LANES), bf16),
        name="pack",
    )(turn_hist)


def turn_kernel(hist_ref, label_ref, out_ref):
    @pl.when(pl.program_id(0) == 0)
    def _():
        out_ref[...] = jnp.zeros_like(out_ref)

    values = hist_ref[...].astype(f32)
    normal = values / jnp.sum(values, axis=0, keepdims=True)
    hi = normal.astype(bf16)
    rest = normal - hi.astype(f32)
    mid = rest.astype(bf16)
    low = (rest - mid.astype(f32)).astype(bf16)
    ids = lax.broadcasted_iota(i32, (TURN_CENT, values.shape[1]), 0)
    onehot = (label_ref[...] == ids).astype(f32).astype(bf16)
    total = None
    for part in (hi, mid, low):
        more = lax.dot_general(part, onehot, (((1,), (1,)), ((), ())), preferred_element_type=f32)
        total = more if total is None else total + more
    out_ref[0:BINS, :] += total[:, :LANES]
    out_ref[TURN_SPLIT:TURN_SPLIT + BINS, 0:TURN_CENT - LANES] += total[:, LANES:]


def turn_partial(turn_hist, labels):
    width = SOURCES_PER_STEP * BLOCK // 2 if (SOURCES_PER_STEP * BLOCK // 2) % LANES == 0 else SOURCES_PER_STEP * BLOCK
    steps = turn_hist.shape[1] // width
    return pl.pallas_call(
        turn_kernel,
        grid=(steps,),
        in_specs=[pl.BlockSpec((BINS, width), lambda i: (0, i)), pl.BlockSpec((1, width), lambda i: (0, i))],
        out_specs=pl.BlockSpec((TURN_ROWS, LANES), lambda i: (0, 0)),
        out_shape=jax.ShapeDtypeStruct((TURN_ROWS, LANES), f32),
        name="turn_sums",
    )(turn_hist, labels)


TILE = 256
TILES = KIDS * HANDS // TILE
AHEAD = 6


def place_columns(o, recv_ref, place_ref, cols_ref):
    row = lax.broadcasted_iota(i32, (8, LANES), 0)
    lane = lax.broadcasted_iota(i32, (8, LANES), 1)
    tail_hi, tail_mid, tail_low = row < 2, (row >= 2) & (row < 4), (row >= 4) & (row < 6)
    zero = jnp.zeros((8, LANES), f32)

    def gather(x, index):
        return jnp.take_along_axis(x, index, axis=1)

    def place(s, carry):
        start = s * BLOCK
        t0 = start // TILE
        a = start - t0 * TILE
        tiles = []
        for t in range(PACK_ROWS // 16):
            both = recv_ref[s, 16 * t:16 * t + 16, :].astype(f32)
            tiles += [both[0:8], both[8:16]]
        now, later = place_ref[pl.ds(t0, 1), :], place_ref[pl.ds(t0 + 1, 1), :]
        following = []
        for half in range(2):
            side = slice(half * LANES, (half + 1) * LANES)
            mask = lane + half * LANES >= a
            spill = lane + (half * LANES + TILE) < a + BLOCK
            r = jnp.where(mask, now[:, side], later[:, side])
            p = (r + o) & 127
            p2 = p ^ 64
            far = r >= LANES
            first = ((p - o) & 127) < 64
            out = []
            for g in range(6):
                source, index = tiles[(6, 7, 6, 7, 8, 9)[g]], p2 if g in (2, 3) else p
                out.append(jnp.where(far, gather(source, index), gather(tiles[g], p)))
            near, turned = gather(tiles[8], p), gather(tiles[8], p2)
            out.append(jnp.where(far & tail_hi | ~far & first & tail_low, turned,
                                 jnp.where(~far & ~first & tail_mid, near, zero)))
            merged = [jnp.where(mask, out[g], carry[7 * half + g]) for g in range(7)]
            for g in range(4):
                pair = jnp.concatenate([merged[2 * g], merged[2 * g + 1] if g < 3 else zero], axis=0)
                cols_ref[t0, 16 * g:16 * g + 16, side] = pair.astype(bf16)
            following += [jnp.where(spill, out[g], merged[g]) for g in range(7)]
        return tuple(following)

    return place, (zero,) * 14


def member_kernel(scalar_ref, recv_ref, place_ref, table_ref, assign_ref,
                  hist_ref, keep_ref, send_ref, cols_ref, even_ref, odd_ref):
    core = scalar_ref[1]
    place, carry = place_columns(scalar_ref[0], recv_ref, place_ref, cols_ref)

    def products(i, out_ref):
        h = jnp.concatenate([cols_ref[2 * i], cols_ref[2 * i + 1]], axis=1)
        out_ref[...] = jnp.dot(
            table_ref[...], jnp.concatenate([h, h, h], axis=0), preferred_element_type=f32)

    def add_kid(z_ref):
        for c in range(HANDS // LANES):
            at = slice(c * LANES, (c + 1) * LANES)
            cdf = z_ref[200:256, at]
            total = z_ref[256:264, at]
            sq = jnp.sum(cdf * cdf, axis=0, keepdims=True)
            extra = total + sharpness * sq / total
            y = z_ref[0:200, at].reshape(25, 8, LANES) + extra[None]
            w = 1.0 / (y * y)
            scale = 1.0 / jnp.sum(jnp.sum(w, axis=0), axis=0, keepdims=True)
            hist_ref[:, at] += (w * scale[None]).reshape(200, LANES)

    hist_ref[...] = jnp.zeros_like(hist_ref)
    carry = lax.fori_loop(0, AHEAD, place, carry, unroll=3)
    products(0, even_ref)

    def two_kids(j, carry):
        def some(at, carry):
            for k in range(AHEAD // 2):
                carry = place(jnp.minimum(AHEAD * (j + 1) + at + k, DEVICES - 1), carry)
            return carry

        products(2 * j + 1, odd_ref)
        carry = some(0, carry)
        add_kid(even_ref)
        products(2 * j + 2, even_ref)
        carry = some(AHEAD // 2, carry)
        add_kid(odd_ref)
        return carry

    lax.fori_loop(0, KIDS // 2, two_kids, carry)
    add_kid(even_ref)

    hi = hist_ref[...].astype(bf16)
    rest = (hist_ref[...] - hi.astype(f32)).astype(bf16)
    stack = jnp.concatenate([hi, rest], axis=0)
    ids = lax.broadcasted_iota(i32, (LANES, HANDS), 0)
    valid = ids < PANEL
    for i in range(8):
        halves = []
        for side in (core, 1 - core):
            base = PANEL * (2 * i + side)
            halves.append((valid & (assign_ref[...] - base == ids)).astype(f32).astype(bf16))
        onehot = jnp.concatenate(halves, axis=0)
        sums = lax.dot_general(stack, onehot, (((1,), (1,)), ((), ())), preferred_element_type=f32)
        both = sums[0:200] + sums[200:400]
        keep_ref[i] = both[:, :LANES]
        send_ref[i] = both[:, LANES:]


VMEM = pl.BlockSpec(memory_space=pltpu.VMEM)
SMEM = pl.BlockSpec(memory_space=pltpu.SMEM)


def member(scalars, recv, place, table, assign):
    return pl.pallas_call(
        member_kernel,
        in_specs=[SMEM, VMEM, VMEM, VMEM, VMEM],
        out_specs=[VMEM, VMEM, VMEM],
        out_shape=[
            jax.ShapeDtypeStruct((TURN_CENT, HANDS), f32),
            jax.ShapeDtypeStruct((8, TURN_CENT, LANES), f32),
            jax.ShapeDtypeStruct((8, TURN_CENT, LANES), f32),
        ],
        scratch_shapes=[
            pltpu.VMEM((TILES, 64, TILE), bf16),
            pltpu.VMEM((264, HANDS), f32),
            pltpu.VMEM((264, HANDS), f32),
        ],
        compiler_params=pltpu.CompilerParams(vmem_limit_bytes=24 * 1024 * 1024),
        name="member",
    )(scalars, recv, place, table, assign)


def nearest_kernel(mine_ref, partner_ref, pieces_ref, out_ref):
    one = jnp.where(lax.broadcasted_iota(i32, (8, 2 * HANDS), 0) == 0, 1.0, 0.0)
    hands = jnp.concatenate([jnp.concatenate([mine_ref[...], partner_ref[...]], axis=1), one], axis=0)
    lane = lax.broadcasted_iota(i32, (8, LANES), 1)
    best = None
    for i in range(pieces_ref.shape[0]):
        c = pieces_ref[i, 0:TURN_CENT, :]
        sq = jnp.broadcast_to(jnp.sum(c * c, axis=0, keepdims=True), (8, LANES))
        sides = jnp.concatenate([-2.0 * c, jnp.where(lane < PANEL, sq, 1e30)], axis=0)
        dist = lax.dot_general(
            sides, hands, (((0,), (0,)), ((), ())), precision=highest, preferred_element_type=f32)
        part = jnp.min(dist, axis=0, keepdims=True)
        best = part if best is None else jnp.minimum(best, part)
    out_ref[...] = best


def nearest_of(pieces, flop_hist, partner):
    best = pl.pallas_call(
        nearest_kernel,
        in_specs=[VMEM, VMEM, VMEM],
        out_specs=VMEM,
        out_shape=jax.ShapeDtypeStruct((1, 2 * HANDS), f32),
    compiler_params=pltpu.CompilerParams(vmem_limit_bytes=24 * 1024 * 1024),
        name="nearest",
    )(flop_hist, partner, pieces)
    best = jnp.minimum(best[:, :HANDS], swap(best[:, HANDS:], "cent", 1))
    return best[0] + jnp.sum(jnp.square(flop_hist), axis=0)


def center_table(turn_centers):
    table = fold_table(BINS)
    values = turn_centers.astype(f32)
    normal = values / jnp.sum(values, axis=0, keepdims=True)
    center_cdf = jnp.dot(table, normal, precision=highest, preferred_element_type=f32)
    center_sq = jnp.sum(center_cdf * center_cdf, axis=0)
    folded = lax.dot_general(
        center_cdf, table, (((0,), (0,)), ((), ())), precision=highest, preferred_element_type=f32)
    folded = sharpness * center_sq[:, None] - 2.0 * sharpness * folded

    def spread(x):
        return jnp.concatenate(
            [x[:, :48], x[:, 48:], x[:, 48:], x[:, 48:], jnp.zeros((x.shape[0], 10), f32)], axis=1)

    hi = lax.reduce_precision(folded, 8, 7)
    mid = lax.reduce_precision(folded - hi, 8, 7)
    low = lax.reduce_precision(folded - hi - mid, 8, 7)
    top = jnp.concatenate([spread(hi), spread(mid), spread(low)], axis=1)
    rows = jnp.concatenate([table, jnp.zeros((6, BINS), f32), jnp.ones((8, BINS), f32)], axis=0)
    bottom = jnp.concatenate([spread(rows), jnp.zeros((64, 128), f32)], axis=1)
    return jnp.concatenate([top, bottom], axis=0).astype(bf16)


CHIPS = [[2 * i + c for i in range(8)] for c in range(2)]


def swap(x, axis, mask):
    size = 8 if axis == "board" else 16
    return lax.ppermute(x, axis, [(i, i ^ mask) for i in range(size)])


def body(turn_hist, turn_assign, child_rows, turn_centers, flop_centers, flop_assign):
    sent = pack(turn_hist)
    turn_assign, sent = lax.optimization_barrier((turn_assign, sent))
    arrived = lax.all_to_all(sent, ("board", "cent"), split_axis=0, concat_axis=0, tiled=True)

    device = lax.axis_index("board") * 16 + lax.axis_index("cent")
    offset = (device * BLOCK) % LANES
    scalars = jnp.stack([offset, lax.axis_index("cent") % 2]).astype(i32)

    turn_part = turn_partial(turn_hist, turn_assign[None, :])
    own = jnp.concatenate([jnp.pad(flop_centers, ((0, 0), (0, LANES - PANEL))), turn_part], axis=0)
    place = jnp.concatenate([child_rows.reshape(TILES, TILE), jnp.zeros((2, TILE), i32)], axis=0)
    table = center_table(turn_centers)

    own, place, table, scalars = lax.optimization_barrier((own, place, table, scalars))
    copies = jnp.broadcast_to(own[None], (8,) + own.shape)
    pieces = lax.all_to_all(copies, "cent", split_axis=0, concat_axis=0, tiled=True, axis_index_groups=CHIPS)

    flop_hist, keep, send = member(scalars, arrived, place, table, flop_assign[None, :])

    turn_part = jnp.sum(pieces[:, TURN_CENT:], axis=0)
    turn_part = turn_part + swap(turn_part, "cent", 1)
    turn_part = turn_part + swap(turn_part, "board", 1)
    received, partner = lax.optimization_barrier((swap(send, "cent", 1), swap(flop_hist, "cent", 1)))
    half = keep + received
    parts = lax.all_to_all(half, "cent", split_axis=0, concat_axis=0, tiled=True, axis_index_groups=CHIPS)
    flop_part = jnp.sum(parts, axis=0)
    flop_part = flop_part + swap(flop_part, "board", 1)
    total = jnp.concatenate([flop_part, turn_part], axis=0)
    total = (total + swap(total, "board", 2)) + (swap(total, "board", 4) + swap(total, "board", 6))
    flop_sums = total[:TURN_CENT, :PANEL].T * (PANEL * 16 / (HANDS * DEVICES))
    turn_low = total[TURN_CENT:TURN_CENT + BINS]
    turn_high = total[TURN_CENT + TURN_SPLIT:TURN_CENT + TURN_SPLIT + BINS, :TURN_CENT - LANES]
    turn_sums = jnp.concatenate([turn_low, turn_high], axis=1)
    turn_sums = turn_sums * (BINS * TURN_CENT / (turn_hist.shape[1] * DEVICES))

    nearest = nearest_of(pieces, flop_hist, partner)
    return nearest, turn_sums, flop_sums


def solution(mesh):
    in_specs = (
        P(None, ("board", "cent")),
        P(("board", "cent")),
        P(None, ("board", "cent")),
        P(),
        P(None, "cent"),
        P(("board", "cent")),
    )
    out_specs = (P(("board", "cent")), P(), P("cent", None))
    return jax.shard_map(body, mesh=mesh, in_specs=in_specs, out_specs=out_specs, check_vma=False)
```

```python
import jax
import jax.numpy as jnp
from jax import lax
from jax.experimental import pallas as pl
from jax.experimental.pallas import tpu as pltpu
from jax.sharding import PartitionSpec as P


sharpness = 4.0
highest = lax.Precision.HIGHEST
f32, bf16, i32 = jnp.float32, jnp.bfloat16, jnp.int32
LANES = 128
BLOCK = 188
BINS = 50
KIDS = 47
TURN_CENT = 200
HANDS = 512
PANEL = 125
DEVICES = 128
SOURCES_PER_STEP = 32
PACK_ROWS = 80
TURN_SPLIT = 56
TURN_ROWS = 112


def fold_table(bins):
    upper = lax.iota(i32, bins)[:, None]
    lower = lax.iota(i32, bins)[None, :]
    table = 0.5 * (lower <= upper).astype(f32)
    table = table + 0.25 * (lower <= upper - 1).astype(f32)
    table = table + 0.25 * ((lower <= upper + 1) & (lower >= 1)).astype(f32)
    return table


def pack_kernel(hist_ref, out_ref):
    lane = lax.broadcasted_iota(i32, (16, LANES), 1)
    for d in range(SOURCES_PER_STEP):
        t0, o = divmod(BLOCK * d, LANES)
        three = o + BLOCK > 2 * LANES

        def parts(lo, hi):
            tiles = [hist_ref[lo:hi, (t0 + t) * LANES:(t0 + t + 1) * LANES].astype(f32)
                     for t in range(3 if three else 2)]
            upper = lane[:hi - lo] >= o
            a = jnp.where(upper, tiles[0], tiles[1]) if o else tiles[0]
            b = jnp.where(upper, tiles[1], tiles[2]) if three else tiles[1]
            return a, b

        a0, b0 = parts(0, 16)
        a1, b1 = parts(16, 32)
        a2, b2 = parts(32, 48)
        a3, b3 = parts(48, 50)
        first = ((lane - o) & 127) < 64
        out_ref[d, 0:16, :] = a0.astype(bf16)
        out_ref[d, 16:32, :] = a1.astype(bf16)
        out_ref[d, 32:48, :] = a2.astype(bf16)
        out_ref[d, 48:64, :] = jnp.where(first, b0, pltpu.roll(b1, 64, 1)).astype(bf16)
        tail = jnp.concatenate(
            [pltpu.roll(b3, 64, 1), a3, pltpu.roll(a3, 64, 1), jnp.zeros((10, LANES), f32)], axis=0)
        out_ref[d, 64:80, :] = jnp.where(first, b2, tail).astype(bf16)


def pack(turn_hist):
    width = SOURCES_PER_STEP * BLOCK
    return pl.pallas_call(
        pack_kernel,
        grid=(DEVICES // SOURCES_PER_STEP,),
        in_specs=[pl.BlockSpec((BINS, width), lambda i: (0, i))],
        out_specs=pl.BlockSpec((SOURCES_PER_STEP, PACK_ROWS, LANES), lambda i: (i, 0, 0)),
        out_shape=jax.ShapeDtypeStruct((DEVICES, PACK_ROWS, LANES), bf16),
        name="pack",
    )(turn_hist)


def turn_kernel(hist_ref, label_ref, out_ref):
    @pl.when(pl.program_id(0) == 0)
    def _():
        out_ref[...] = jnp.zeros_like(out_ref)

    values = hist_ref[...].astype(f32)
    normal = values / jnp.sum(values, axis=0, keepdims=True)
    hi = normal.astype(bf16)
    rest = normal - hi.astype(f32)
    mid = rest.astype(bf16)
    low = (rest - mid.astype(f32)).astype(bf16)
    ids = lax.broadcasted_iota(i32, (TURN_CENT, values.shape[1]), 0)
    onehot = (label_ref[...] == ids).astype(f32).astype(bf16)
    total = None
    for part in (hi, mid, low):
        more = lax.dot_general(part, onehot, (((1,), (1,)), ((), ())), preferred_element_type=f32)
        total = more if total is None else total + more
    out_ref[0:BINS, :] += total[:, :LANES]
    out_ref[TURN_SPLIT:TURN_SPLIT + BINS, 0:TURN_CENT - LANES] += total[:, LANES:]


def turn_partial(turn_hist, labels):
    width = SOURCES_PER_STEP * BLOCK // 2 if (SOURCES_PER_STEP * BLOCK // 2) % LANES == 0 else SOURCES_PER_STEP * BLOCK
    steps = turn_hist.shape[1] // width
    return pl.pallas_call(
        turn_kernel,
        grid=(steps,),
        in_specs=[pl.BlockSpec((BINS, width), lambda i: (0, i)), pl.BlockSpec((1, width), lambda i: (0, i))],
        out_specs=pl.BlockSpec((TURN_ROWS, LANES), lambda i: (0, 0)),
        out_shape=jax.ShapeDtypeStruct((TURN_ROWS, LANES), f32),
        name="turn_sums",
    )(turn_hist, labels)


TILE = 256
TILES = KIDS * HANDS // TILE
AHEAD = 6


def place_columns(o, recv_ref, place_ref, cols_ref):
    row = lax.broadcasted_iota(i32, (8, LANES), 0)
    lane = lax.broadcasted_iota(i32, (8, LANES), 1)
    tail_hi, tail_mid, tail_low = row < 2, (row >= 2) & (row < 4), (row >= 4) & (row < 6)
    zero = jnp.zeros((8, LANES), f32)

    def gather(x, index):
        return jnp.take_along_axis(x, index, axis=1)

    def place(s, carry):
        start = s * BLOCK
        t0 = start // TILE
        a = start - t0 * TILE
        tiles = []
        for t in range(PACK_ROWS // 16):
            both = recv_ref[s, 16 * t:16 * t + 16, :].astype(f32)
            tiles += [both[0:8], both[8:16]]
        now, later = place_ref[pl.ds(t0, 1), :], place_ref[pl.ds(t0 + 1, 1), :]
        following = []
        for half in range(2):
            side = slice(half * LANES, (half + 1) * LANES)
            mask = lane + half * LANES >= a
            spill = lane + (half * LANES + TILE) < a + BLOCK
            r = jnp.where(mask, now[:, side], later[:, side])
            p = (r + o) & 127
            p2 = p ^ 64
            far = r >= LANES
            first = ((p - o) & 127) < 64
            out = []
            for g in range(6):
                source, index = tiles[(6, 7, 6, 7, 8, 9)[g]], p2 if g in (2, 3) else p
                out.append(jnp.where(far, gather(source, index), gather(tiles[g], p)))
            near, turned = gather(tiles[8], p), gather(tiles[8], p2)
            out.append(jnp.where(far & tail_hi | ~far & first & tail_low, turned,
                                 jnp.where(~far & ~first & tail_mid, near, zero)))
            merged = [jnp.where(mask, out[g], carry[7 * half + g]) for g in range(7)]
            for g in range(4):
                pair = jnp.concatenate([merged[2 * g], merged[2 * g + 1] if g < 3 else zero], axis=0)
                cols_ref[t0, 16 * g:16 * g + 16, side] = pair.astype(bf16)
            following += [jnp.where(spill, out[g], merged[g]) for g in range(7)]
        return tuple(following)

    return place, (zero,) * 14


def member_kernel(scalar_ref, recv_ref, place_ref, table_ref, assign_ref,
                  hist_ref, keep_ref, send_ref, cols_ref, even_ref, odd_ref):
    core = scalar_ref[1]
    place, carry = place_columns(scalar_ref[0], recv_ref, place_ref, cols_ref)

    def products(i, out_ref):
        h = jnp.concatenate([cols_ref[2 * i], cols_ref[2 * i + 1]], axis=1)
        out_ref[...] = jnp.dot(
            table_ref[...], jnp.concatenate([h, h, h], axis=0), preferred_element_type=f32)

    def add_kid(z_ref):
        for c in range(HANDS // LANES):
            at = slice(c * LANES, (c + 1) * LANES)
            cdf = z_ref[200:256, at]
            total = z_ref[256:264, at]
            sq = jnp.sum(cdf * cdf, axis=0, keepdims=True)
            extra = total + sharpness * sq / total
            y = z_ref[0:200, at].reshape(25, 8, LANES) + extra[None]
            w = 1.0 / (y * y)
            scale = 1.0 / jnp.sum(jnp.sum(w, axis=0), axis=0, keepdims=True)
            hist_ref[:, at] += (w * scale[None]).reshape(200, LANES)

    hist_ref[...] = jnp.zeros_like(hist_ref)
    carry = lax.fori_loop(0, AHEAD, place, carry, unroll=3)
    products(0, even_ref)

    def two_kids(j, carry):
        def some(at, carry):
            for k in range(AHEAD // 2):
                carry = place(jnp.minimum(AHEAD * (j + 1) + at + k, DEVICES - 1), carry)
            return carry

        products(2 * j + 1, odd_ref)
        carry = some(0, carry)
        add_kid(even_ref)
        products(2 * j + 2, even_ref)
        carry = some(AHEAD // 2, carry)
        add_kid(odd_ref)
        return carry

    lax.fori_loop(0, KIDS // 2, two_kids, carry)
    add_kid(even_ref)

    hi = hist_ref[...].astype(bf16)
    rest = (hist_ref[...] - hi.astype(f32)).astype(bf16)
    stack = jnp.concatenate([hi, rest], axis=0)
    ids = lax.broadcasted_iota(i32, (LANES, HANDS), 0)
    valid = ids < PANEL
    for i in range(8):
        halves = []
        for side in (core, 1 - core):
            base = PANEL * (2 * i + side)
            halves.append((valid & (assign_ref[...] - base == ids)).astype(f32).astype(bf16))
        onehot = jnp.concatenate(halves, axis=0)
        sums = lax.dot_general(stack, onehot, (((1,), (1,)), ((), ())), preferred_element_type=f32)
        both = sums[0:200] + sums[200:400]
        keep_ref[i] = both[:, :LANES]
        send_ref[i] = both[:, LANES:]


VMEM = pl.BlockSpec(memory_space=pltpu.VMEM)
SMEM = pl.BlockSpec(memory_space=pltpu.SMEM)


def member(scalars, recv, place, table, assign):
    return pl.pallas_call(
        member_kernel,
        in_specs=[SMEM, VMEM, VMEM, VMEM, VMEM],
        out_specs=[VMEM, VMEM, VMEM],
        out_shape=[
            jax.ShapeDtypeStruct((TURN_CENT, HANDS), f32),
            jax.ShapeDtypeStruct((8, TURN_CENT, LANES), f32),
            jax.ShapeDtypeStruct((8, TURN_CENT, LANES), f32),
        ],
        scratch_shapes=[
            pltpu.VMEM((TILES, 64, TILE), bf16),
            pltpu.VMEM((264, HANDS), f32),
            pltpu.VMEM((264, HANDS), f32),
        ],
        compiler_params=pltpu.CompilerParams(vmem_limit_bytes=24 * 1024 * 1024),
        name="member",
    )(scalars, recv, place, table, assign)


def nearest_kernel(mine_ref, partner_ref, pieces_ref, out_ref):
    one = jnp.where(lax.broadcasted_iota(i32, (8, 2 * HANDS), 0) == 0, 1.0, 0.0)
    hands = jnp.concatenate([jnp.concatenate([mine_ref[...], partner_ref[...]], axis=1), one], axis=0)
    lane = lax.broadcasted_iota(i32, (8, LANES), 1)
    best = None
    for i in range(pieces_ref.shape[0]):
        c = pieces_ref[i, 0:TURN_CENT, :]
        sq = jnp.broadcast_to(jnp.sum(c * c, axis=0, keepdims=True), (8, LANES))
        sides = jnp.concatenate([-2.0 * c, jnp.where(lane < PANEL, sq, 1e30)], axis=0)
        dist = lax.dot_general(
            sides, hands, (((0,), (0,)), ((), ())), precision=highest, preferred_element_type=f32)
        part = jnp.min(dist, axis=0, keepdims=True)
        best = part if best is None else jnp.minimum(best, part)
    out_ref[...] = best


def nearest_of(pieces, flop_hist, partner):
    best = pl.pallas_call(
        nearest_kernel,
        in_specs=[VMEM, VMEM, VMEM],
        out_specs=VMEM,
        out_shape=jax.ShapeDtypeStruct((1, 2 * HANDS), f32),
    compiler_params=pltpu.CompilerParams(vmem_limit_bytes=24 * 1024 * 1024),
        name="nearest",
    )(flop_hist, partner, pieces)
    best = jnp.minimum(best[:, :HANDS], swap(best[:, HANDS:], "cent", 1))
    return best[0] + jnp.sum(jnp.square(flop_hist), axis=0)


def center_table(turn_centers):
    table = fold_table(BINS)
    values = turn_centers.astype(f32)
    normal = values / jnp.sum(values, axis=0, keepdims=True)
    center_cdf = jnp.dot(table, normal, precision=highest, preferred_element_type=f32)
    center_sq = jnp.sum(center_cdf * center_cdf, axis=0)
    folded = lax.dot_general(
        center_cdf, table, (((0,), (0,)), ((), ())), precision=highest, preferred_element_type=f32)
    folded = sharpness * center_sq[:, None] - 2.0 * sharpness * folded

    def spread(x):
        return jnp.concatenate(
            [x[:, :48], x[:, 48:], x[:, 48:], x[:, 48:], jnp.zeros((x.shape[0], 10), f32)], axis=1)

    hi = lax.reduce_precision(folded, 8, 7)
    mid = lax.reduce_precision(folded - hi, 8, 7)
    low = lax.reduce_precision(folded - hi - mid, 8, 7)
    top = jnp.concatenate([spread(hi), spread(mid), spread(low)], axis=1)
    rows = jnp.concatenate([table, jnp.zeros((6, BINS), f32), jnp.ones((8, BINS), f32)], axis=0)
    bottom = jnp.concatenate([spread(rows), jnp.zeros((64, 128), f32)], axis=1)
    return jnp.concatenate([top, bottom], axis=0).astype(bf16)


CHIPS = [[2 * i + c for i in range(8)] for c in range(2)]


def swap(x, axis, mask):
    size = 8 if axis == "board" else 16
    return lax.ppermute(x, axis, [(i, i ^ mask) for i in range(size)])


def body(turn_hist, turn_assign, child_rows, turn_centers, flop_centers, flop_assign):
    sent = pack(turn_hist)
    turn_assign, sent = lax.optimization_barrier((turn_assign, sent))
    arrived = lax.all_to_all(sent, ("board", "cent"), split_axis=0, concat_axis=0, tiled=True)

    device = lax.axis_index("board") * 16 + lax.axis_index("cent")
    offset = (device * BLOCK) % LANES
    scalars = jnp.stack([offset, lax.axis_index("cent") % 2]).astype(i32)

    turn_part = turn_partial(turn_hist, turn_assign[None, :])
    own = jnp.concatenate([jnp.pad(flop_centers, ((0, 0), (0, LANES - PANEL))), turn_part], axis=0)
    place = jnp.concatenate([child_rows.reshape(TILES, TILE), jnp.zeros((2, TILE), i32)], axis=0)
    table = center_table(turn_centers)

    own, place, table, scalars = lax.optimization_barrier((own, place, table, scalars))
    copies = jnp.broadcast_to(own[None], (8,) + own.shape)
    pieces = lax.all_to_all(copies, "cent", split_axis=0, concat_axis=0, tiled=True, axis_index_groups=CHIPS)

    flop_hist, keep, send = member(scalars, arrived, place, table, flop_assign[None, :])

    turn_part = jnp.sum(pieces[:, TURN_CENT:], axis=0)
    turn_part = turn_part + swap(turn_part, "cent", 1)
    turn_part = turn_part + swap(turn_part, "board", 1)
    half = keep + swap(send, "cent", 1)
    flop_hist, half = lax.optimization_barrier((flop_hist, half))
    partner = swap(flop_hist, "cent", 1)
    parts = lax.all_to_all(half, "cent", split_axis=0, concat_axis=0, tiled=True, axis_index_groups=CHIPS)
    flop_part = jnp.sum(parts, axis=0)
    flop_part = flop_part + swap(flop_part, "board", 1)
    total = jnp.concatenate([flop_part, turn_part], axis=0)
    total = (total + swap(total, "board", 2)) + (swap(total, "board", 4) + swap(total, "board", 6))
    flop_sums = total[:TURN_CENT, :PANEL].T * (PANEL * 16 / (HANDS * DEVICES))
    turn_low = total[TURN_CENT:TURN_CENT + BINS]
    turn_high = total[TURN_CENT + TURN_SPLIT:TURN_CENT + TURN_SPLIT + BINS, :TURN_CENT - LANES]
    turn_sums = jnp.concatenate([turn_low, turn_high], axis=1)
    turn_sums = turn_sums * (BINS * TURN_CENT / (turn_hist.shape[1] * DEVICES))

    nearest = nearest_of(pieces, flop_hist, partner)
    return nearest, turn_sums, flop_sums


def solution(mesh):
    in_specs = (
        P(None, ("board", "cent")),
        P(("board", "cent")),
        P(None, ("board", "cent")),
        P(),
        P(None, "cent"),
        P(("board", "cent")),
    )
    out_specs = (P(("board", "cent")), P(), P("cent", None))
    return jax.shard_map(body, mesh=mesh, in_specs=in_specs, out_specs=out_specs, check_vma=False)
```

```python
import jax
import jax.numpy as jnp
from jax import lax
from jax.experimental import pallas as pl
from jax.experimental.pallas import tpu as pltpu
from jax.sharding import PartitionSpec as P


sharpness = 4.0
highest = lax.Precision.HIGHEST
f32, bf16, i32 = jnp.float32, jnp.bfloat16, jnp.int32
LANES = 128
BLOCK = 188
BINS = 50
KIDS = 47
TURN_CENT = 200
HANDS = 512
PANEL = 125
DEVICES = 128
SOURCES_PER_STEP = 32
PACK_ROWS = 80
TURN_SPLIT = 56
TURN_ROWS = 112


def fold_table(bins):
    upper = lax.iota(i32, bins)[:, None]
    lower = lax.iota(i32, bins)[None, :]
    table = 0.5 * (lower <= upper).astype(f32)
    table = table + 0.25 * (lower <= upper - 1).astype(f32)
    table = table + 0.25 * ((lower <= upper + 1) & (lower >= 1)).astype(f32)
    return table


def pack_kernel(ref0, ref1, ref2, ref3, out_ref):
    groups = (ref0, ref1, ref2, ref3)
    lane = lax.broadcasted_iota(i32, (16, LANES), 1)
    for d in range(SOURCES_PER_STEP):
        t0, o = divmod(BLOCK * d, LANES)
        three = o + BLOCK > 2 * LANES

        def parts(lo, hi):
            tiles = [groups[lo // 16][0:hi - lo, (t0 + t) * LANES:(t0 + t + 1) * LANES].astype(f32)
                     for t in range(3 if three else 2)]
            upper = lane[:hi - lo] >= o
            a = jnp.where(upper, tiles[0], tiles[1]) if o else tiles[0]
            b = jnp.where(upper, tiles[1], tiles[2]) if three else tiles[1]
            return a, b

        a0, b0 = parts(0, 16)
        a1, b1 = parts(16, 32)
        a2, b2 = parts(32, 48)
        a3, b3 = parts(48, 50)
        first = ((lane - o) & 127) < 64
        out_ref[d, 0:16, :] = a0.astype(bf16)
        out_ref[d, 16:32, :] = a1.astype(bf16)
        out_ref[d, 32:48, :] = a2.astype(bf16)
        out_ref[d, 48:64, :] = jnp.where(first, b0, pltpu.roll(b1, 64, 1)).astype(bf16)
        tail = jnp.concatenate(
            [pltpu.roll(b3, 64, 1), a3, pltpu.roll(a3, 64, 1), jnp.zeros((10, LANES), f32)], axis=0)
        out_ref[d, 64:80, :] = jnp.where(first, b2, tail).astype(bf16)


def pack(turn_hist):
    width = SOURCES_PER_STEP * BLOCK
    return pl.pallas_call(
        pack_kernel,
        grid=(DEVICES // SOURCES_PER_STEP,),
        in_specs=[pl.BlockSpec((16, width), lambda i, g=g: (g, i)) for g in range(4)],
        out_specs=pl.BlockSpec((SOURCES_PER_STEP, PACK_ROWS, LANES), lambda i: (i, 0, 0)),
        out_shape=jax.ShapeDtypeStruct((DEVICES, PACK_ROWS, LANES), bf16),
        name="pack",
    )(turn_hist, turn_hist, turn_hist, turn_hist)


def turn_kernel(hist_ref, label_ref, out_ref):
    @pl.when(pl.program_id(0) == 0)
    def _():
        out_ref[...] = jnp.zeros_like(out_ref)

    values = hist_ref[...].astype(f32)
    normal = values / jnp.sum(values, axis=0, keepdims=True)
    hi = normal.astype(bf16)
    rest = normal - hi.astype(f32)
    mid = rest.astype(bf16)
    low = (rest - mid.astype(f32)).astype(bf16)
    ids = lax.broadcasted_iota(i32, (TURN_CENT, values.shape[1]), 0)
    onehot = (label_ref[...] == ids).astype(f32).astype(bf16)
    total = None
    for part in (hi, mid, low):
        more = lax.dot_general(part, onehot, (((1,), (1,)), ((), ())), preferred_element_type=f32)
        total = more if total is None else total + more
    out_ref[0:BINS, :] += total[:, :LANES]
    out_ref[TURN_SPLIT:TURN_SPLIT + BINS, 0:TURN_CENT - LANES] += total[:, LANES:]


def turn_partial(turn_hist, labels):
    width = SOURCES_PER_STEP * BLOCK // 2 if (SOURCES_PER_STEP * BLOCK // 2) % LANES == 0 else SOURCES_PER_STEP * BLOCK
    steps = turn_hist.shape[1] // width
    return pl.pallas_call(
        turn_kernel,
        grid=(steps,),
        in_specs=[pl.BlockSpec((BINS, width), lambda i: (0, i)), pl.BlockSpec((1, width), lambda i: (0, i))],
        out_specs=pl.BlockSpec((TURN_ROWS, LANES), lambda i: (0, 0)),
        out_shape=jax.ShapeDtypeStruct((TURN_ROWS, LANES), f32),
        name="turn_sums",
    )(turn_hist, labels)


TILE = 256
TILES = KIDS * HANDS // TILE
AHEAD = 6


def place_columns(o, recv_ref, place_ref, cols_ref):
    row = lax.broadcasted_iota(i32, (8, LANES), 0)
    lane = lax.broadcasted_iota(i32, (8, LANES), 1)
    tail_hi, tail_mid, tail_low = row < 2, (row >= 2) & (row < 4), (row >= 4) & (row < 6)
    zero = jnp.zeros((8, LANES), f32)

    def gather(x, index):
        return jnp.take_along_axis(x, index, axis=1)

    def place(s, carry):
        start = s * BLOCK
        t0 = start // TILE
        a = start - t0 * TILE
        tiles = []
        for t in range(PACK_ROWS // 16):
            both = recv_ref[s, 16 * t:16 * t + 16, :].astype(f32)
            tiles += [both[0:8], both[8:16]]
        now, later = place_ref[pl.ds(t0, 1), :], place_ref[pl.ds(t0 + 1, 1), :]
        following = []
        for half in range(2):
            side = slice(half * LANES, (half + 1) * LANES)
            mask = lane + half * LANES >= a
            spill = lane + (half * LANES + TILE) < a + BLOCK
            r = jnp.where(mask, now[:, side], later[:, side])
            p = (r + o) & 127
            p2 = p ^ 64
            far = r >= LANES
            first = ((p - o) & 127) < 64
            out = []
            for g in range(6):
                source, index = tiles[(6, 7, 6, 7, 8, 9)[g]], p2 if g in (2, 3) else p
                out.append(jnp.where(far, gather(source, index), gather(tiles[g], p)))
            near, turned = gather(tiles[8], p), gather(tiles[8], p2)
            out.append(jnp.where(far & tail_hi | ~far & first & tail_low, turned,
                                 jnp.where(~far & ~first & tail_mid, near, zero)))
            merged = [jnp.where(mask, out[g], carry[7 * half + g]) for g in range(7)]
            for g in range(4):
                pair = jnp.concatenate([merged[2 * g], merged[2 * g + 1] if g < 3 else zero], axis=0)
                cols_ref[t0, 16 * g:16 * g + 16, side] = pair.astype(bf16)
            following += [jnp.where(spill, out[g], merged[g]) for g in range(7)]
        return tuple(following)

    return place, (zero,) * 14


def member_kernel(scalar_ref, recv_ref, place_ref, table_ref, assign_ref,
                  hist_ref, keep_ref, send_ref, cols_ref, even_ref, odd_ref):
    core = scalar_ref[1]
    place, carry = place_columns(scalar_ref[0], recv_ref, place_ref, cols_ref)

    def products(i, out_ref):
        h = jnp.concatenate([cols_ref[2 * i], cols_ref[2 * i + 1]], axis=1)
        out_ref[...] = jnp.dot(
            table_ref[...], jnp.concatenate([h, h, h], axis=0), preferred_element_type=f32)

    def add_kid(z_ref):
        for c in range(HANDS // LANES):
            at = slice(c * LANES, (c + 1) * LANES)
            cdf = z_ref[200:256, at]
            total = z_ref[256:264, at]
            sq = jnp.sum(cdf * cdf, axis=0, keepdims=True)
            extra = total + sharpness * sq / total
            y = z_ref[0:200, at].reshape(25, 8, LANES) + extra[None]
            w = 1.0 / (y * y)
            scale = 1.0 / jnp.sum(jnp.sum(w, axis=0), axis=0, keepdims=True)
            hist_ref[:, at] += (w * scale[None]).reshape(200, LANES)

    hist_ref[...] = jnp.zeros_like(hist_ref)
    carry = lax.fori_loop(0, AHEAD, place, carry, unroll=3)
    products(0, even_ref)

    def two_kids(j, carry):
        def some(at, carry):
            for k in range(AHEAD // 2):
                carry = place(jnp.minimum(AHEAD * (j + 1) + at + k, DEVICES - 1), carry)
            return carry

        products(2 * j + 1, odd_ref)
        carry = some(0, carry)
        add_kid(even_ref)
        products(2 * j + 2, even_ref)
        carry = some(AHEAD // 2, carry)
        add_kid(odd_ref)
        return carry

    lax.fori_loop(0, KIDS // 2, two_kids, carry)
    add_kid(even_ref)

    hi = hist_ref[...].astype(bf16)
    rest = (hist_ref[...] - hi.astype(f32)).astype(bf16)
    stack = jnp.concatenate([hi, rest], axis=0)
    ids = lax.broadcasted_iota(i32, (LANES, HANDS), 0)
    valid = ids < PANEL
    for i in range(8):
        halves = []
        for side in (core, 1 - core):
            base = PANEL * (2 * i + side)
            halves.append((valid & (assign_ref[...] - base == ids)).astype(f32).astype(bf16))
        onehot = jnp.concatenate(halves, axis=0)
        sums = lax.dot_general(stack, onehot, (((1,), (1,)), ((), ())), preferred_element_type=f32)
        both = sums[0:200] + sums[200:400]
        keep_ref[i] = both[:, :LANES]
        send_ref[i] = both[:, LANES:]


VMEM = pl.BlockSpec(memory_space=pltpu.VMEM)
SMEM = pl.BlockSpec(memory_space=pltpu.SMEM)


def member(scalars, recv, place, table, assign):
    return pl.pallas_call(
        member_kernel,
        in_specs=[SMEM, VMEM, VMEM, VMEM, VMEM],
        out_specs=[VMEM, VMEM, VMEM],
        out_shape=[
            jax.ShapeDtypeStruct((TURN_CENT, HANDS), f32),
            jax.ShapeDtypeStruct((8, TURN_CENT, LANES), f32),
            jax.ShapeDtypeStruct((8, TURN_CENT, LANES), f32),
        ],
        scratch_shapes=[
            pltpu.VMEM((TILES, 64, TILE), bf16),
            pltpu.VMEM((264, HANDS), f32),
            pltpu.VMEM((264, HANDS), f32),
        ],
        compiler_params=pltpu.CompilerParams(vmem_limit_bytes=24 * 1024 * 1024),
        name="member",
    )(scalars, recv, place, table, assign)


def nearest_kernel(mine_ref, partner_ref, pieces_ref, out_ref):
    one = jnp.where(lax.broadcasted_iota(i32, (8, 2 * HANDS), 0) == 0, 1.0, 0.0)
    hands = jnp.concatenate([jnp.concatenate([mine_ref[...], partner_ref[...]], axis=1), one], axis=0)
    lane = lax.broadcasted_iota(i32, (8, LANES), 1)
    best = None
    for i in range(pieces_ref.shape[0]):
        c = pieces_ref[i, 0:TURN_CENT, :]
        sq = jnp.broadcast_to(jnp.sum(c * c, axis=0, keepdims=True), (8, LANES))
        sides = jnp.concatenate([-2.0 * c, jnp.where(lane < PANEL, sq, 1e30)], axis=0)
        dist = lax.dot_general(
            sides, hands, (((0,), (0,)), ((), ())), precision=highest, preferred_element_type=f32)
        part = jnp.min(dist, axis=0, keepdims=True)
        best = part if best is None else jnp.minimum(best, part)
    out_ref[...] = best


def nearest_of(pieces, flop_hist, partner):
    best = pl.pallas_call(
        nearest_kernel,
        in_specs=[VMEM, VMEM, VMEM],
        out_specs=VMEM,
        out_shape=jax.ShapeDtypeStruct((1, 2 * HANDS), f32),
    compiler_params=pltpu.CompilerParams(vmem_limit_bytes=24 * 1024 * 1024),
        name="nearest",
    )(flop_hist, partner, pieces)
    best = jnp.minimum(best[:, :HANDS], swap(best[:, HANDS:], "cent", 1))
    return best[0] + jnp.sum(jnp.square(flop_hist), axis=0)


def center_table(turn_centers):
    table = fold_table(BINS)
    values = turn_centers.astype(f32)
    normal = values / jnp.sum(values, axis=0, keepdims=True)
    center_cdf = jnp.dot(table, normal, precision=highest, preferred_element_type=f32)
    center_sq = jnp.sum(center_cdf * center_cdf, axis=0)
    folded = lax.dot_general(
        center_cdf, table, (((0,), (0,)), ((), ())), precision=highest, preferred_element_type=f32)
    folded = sharpness * center_sq[:, None] - 2.0 * sharpness * folded

    def spread(x):
        return jnp.concatenate(
            [x[:, :48], x[:, 48:], x[:, 48:], x[:, 48:], jnp.zeros((x.shape[0], 10), f32)], axis=1)

    hi = lax.reduce_precision(folded, 8, 7)
    mid = lax.reduce_precision(folded - hi, 8, 7)
    low = lax.reduce_precision(folded - hi - mid, 8, 7)
    top = jnp.concatenate([spread(hi), spread(mid), spread(low)], axis=1)
    rows = jnp.concatenate([table, jnp.zeros((6, BINS), f32), jnp.ones((8, BINS), f32)], axis=0)
    bottom = jnp.concatenate([spread(rows), jnp.zeros((64, 128), f32)], axis=1)
    return jnp.concatenate([top, bottom], axis=0).astype(bf16)


CHIPS = [[2 * i + c for i in range(8)] for c in range(2)]


def swap(x, axis, mask):
    size = 8 if axis == "board" else 16
    return lax.ppermute(x, axis, [(i, i ^ mask) for i in range(size)])


def finish(first, second, third, fourth, flop_scale, turn_scale):
    def kernel(a_ref, b_ref, c_ref, d_ref, flop_ref, turn_ref):
        total = (a_ref[...] + b_ref[...]) + (c_ref[...] + d_ref[...])
        flop_ref[...] = total[:TURN_CENT, :PANEL] * flop_scale
        turn = total[TURN_CENT:] * turn_scale
        turn_ref[:, :LANES] = turn[:BINS]
        turn_ref[:, LANES:] = turn[TURN_SPLIT:TURN_SPLIT + BINS, :TURN_CENT - LANES]

    return pl.pallas_call(
        kernel,
        in_specs=[VMEM] * 4,
        out_specs=[VMEM] * 2,
        out_shape=[
            jax.ShapeDtypeStruct((TURN_CENT, PANEL), f32),
            jax.ShapeDtypeStruct((BINS, TURN_CENT), f32),
        ],
        compiler_params=pltpu.CompilerParams(vmem_limit_bytes=8 * 1024 * 1024),
        name="finish",
    )(first, second, third, fourth)


def body(turn_hist, turn_assign, child_rows, turn_centers, flop_centers, flop_assign):
    sent = pack(turn_hist)
    turn_assign, sent = lax.optimization_barrier((turn_assign, sent))
    arrived = lax.all_to_all(sent, ("board", "cent"), split_axis=0, concat_axis=0, tiled=True)

    device = lax.axis_index("board") * 16 + lax.axis_index("cent")
    offset = (device * BLOCK) % LANES
    scalars = jnp.stack([offset, lax.axis_index("cent") % 2]).astype(i32)

    turn_part = turn_partial(turn_hist, turn_assign[None, :])
    own = jnp.concatenate([jnp.pad(flop_centers, ((0, 0), (0, LANES - PANEL))), turn_part], axis=0)
    place = jnp.concatenate([child_rows.reshape(TILES, TILE), jnp.zeros((2, TILE), i32)], axis=0)
    table = center_table(turn_centers)

    own, place, table, scalars = lax.optimization_barrier((own, place, table, scalars))
    copies = jnp.broadcast_to(own[None], (8,) + own.shape)
    pieces = lax.all_to_all(copies, "cent", split_axis=0, concat_axis=0, tiled=True, axis_index_groups=CHIPS)

    flop_hist, keep, send = member(scalars, arrived, place, table, flop_assign[None, :])

    turn_part = jnp.sum(pieces[:, TURN_CENT:], axis=0)
    turn_part = turn_part + swap(turn_part, "cent", 1)
    turn_part = turn_part + swap(turn_part, "board", 1)
    half = keep + swap(send, "cent", 1)
    flop_hist, half = lax.optimization_barrier((flop_hist, half))
    partner = swap(flop_hist, "cent", 1)
    parts = lax.all_to_all(half, "cent", split_axis=0, concat_axis=0, tiled=True, axis_index_groups=CHIPS)
    flop_part = jnp.sum(parts, axis=0)
    flop_part = flop_part + swap(flop_part, "board", 1)
    total = jnp.concatenate([flop_part, turn_part], axis=0)
    flop_sums, turn_sums = finish(
        total, swap(total, "board", 2), swap(total, "board", 4), swap(total, "board", 6),
        PANEL * 16 / (HANDS * DEVICES), BINS * TURN_CENT / (turn_hist.shape[1] * DEVICES))
    flop_sums = flop_sums.T

    nearest = nearest_of(pieces, flop_hist, partner)
    return nearest, turn_sums, flop_sums


def solution(mesh):
    in_specs = (
        P(None, ("board", "cent")),
        P(("board", "cent")),
        P(None, ("board", "cent")),
        P(),
        P(None, "cent"),
        P(("board", "cent")),
    )
    out_specs = (P(("board", "cent")), P(), P("cent", None))
    return jax.shard_map(body, mesh=mesh, in_specs=in_specs, out_specs=out_specs, check_vma=False)
```

```python
import jax
import jax.numpy as jnp
from jax import lax
from jax.experimental import pallas as pl
from jax.experimental.pallas import tpu as pltpu
from jax.sharding import PartitionSpec as P


sharpness = 4.0
highest = lax.Precision.HIGHEST
f32, bf16, i32 = jnp.float32, jnp.bfloat16, jnp.int32
LANES = 128
BLOCK = 188
BINS = 50
KIDS = 47
TURN_CENT = 200
HANDS = 512
PANEL = 125
DEVICES = 128
SOURCES_PER_STEP = 32
PACK_ROWS = 80
TURN_SPLIT = 50
TURN_ROWS = 104


def fold_table(bins):
    upper = lax.iota(i32, bins)[:, None]
    lower = lax.iota(i32, bins)[None, :]
    table = 0.5 * (lower <= upper).astype(f32)
    table = table + 0.25 * (lower <= upper - 1).astype(f32)
    table = table + 0.25 * ((lower <= upper + 1) & (lower >= 1)).astype(f32)
    return table


def pack_kernel(hist_ref, out_ref):
    lane = lax.broadcasted_iota(i32, (16, LANES), 1)
    for d in range(SOURCES_PER_STEP):
        t0, o = divmod(BLOCK * d, LANES)
        three = o + BLOCK > 2 * LANES

        def parts(lo, hi):
            tiles = [hist_ref[lo:hi, (t0 + t) * LANES:(t0 + t + 1) * LANES].astype(f32)
                     for t in range(3 if three else 2)]
            upper = lane[:hi - lo] >= o
            a = jnp.where(upper, tiles[0], tiles[1]) if o else tiles[0]
            b = jnp.where(upper, tiles[1], tiles[2]) if three else tiles[1]
            return a, b

        a0, b0 = parts(0, 16)
        a1, b1 = parts(16, 32)
        a2, b2 = parts(32, 48)
        a3, b3 = parts(48, 50)
        first = ((lane - o) & 127) < 64
        out_ref[d, 0:16, :] = a0.astype(bf16)
        out_ref[d, 16:32, :] = a1.astype(bf16)
        out_ref[d, 32:48, :] = a2.astype(bf16)
        out_ref[d, 48:64, :] = jnp.where(first, b0, pltpu.roll(b1, 64, 1)).astype(bf16)
        tail = jnp.concatenate(
            [pltpu.roll(b3, 64, 1), a3, pltpu.roll(a3, 64, 1), jnp.zeros((10, LANES), f32)], axis=0)
        out_ref[d, 64:80, :] = jnp.where(first, b2, tail).astype(bf16)


def pack(turn_hist):
    width = SOURCES_PER_STEP * BLOCK
    return pl.pallas_call(
        pack_kernel,
        grid=(DEVICES // SOURCES_PER_STEP,),
        in_specs=[pl.BlockSpec((BINS, width), lambda i: (0, i))],
        out_specs=pl.BlockSpec((SOURCES_PER_STEP, PACK_ROWS, LANES), lambda i: (i, 0, 0)),
        out_shape=jax.ShapeDtypeStruct((DEVICES, PACK_ROWS, LANES), bf16),
        name="pack",
    )(turn_hist)


def turn_kernel(hist_ref, label_ref, out_ref):
    @pl.when(pl.program_id(0) == 0)
    def _():
        out_ref[...] = jnp.zeros_like(out_ref)

    values = hist_ref[...].astype(f32)
    normal = values / jnp.sum(values, axis=0, keepdims=True)
    hi = normal.astype(bf16)
    rest = normal - hi.astype(f32)
    mid = rest.astype(bf16)
    low = (rest - mid.astype(f32)).astype(bf16)
    ids = lax.broadcasted_iota(i32, (TURN_CENT, values.shape[1]), 0)
    onehot = (label_ref[...] == ids).astype(f32).astype(bf16)
    total = None
    for part in (hi, mid, low):
        more = lax.dot_general(part, onehot, (((1,), (1,)), ((), ())), preferred_element_type=f32)
        total = more if total is None else total + more
    out_ref[0:BINS, :] += total[:, :LANES]
    out_ref[TURN_SPLIT:TURN_SPLIT + BINS, 0:TURN_CENT - LANES] += total[:, LANES:]


def turn_partial(turn_hist, labels):
    width = SOURCES_PER_STEP * BLOCK // 2 if (SOURCES_PER_STEP * BLOCK // 2) % LANES == 0 else SOURCES_PER_STEP * BLOCK
    steps = turn_hist.shape[1] // width
    return pl.pallas_call(
        turn_kernel,
        grid=(steps,),
        in_specs=[pl.BlockSpec((BINS, width), lambda i: (0, i)), pl.BlockSpec((1, width), lambda i: (0, i))],
        out_specs=pl.BlockSpec((TURN_ROWS, LANES), lambda i: (0, 0)),
        out_shape=jax.ShapeDtypeStruct((TURN_ROWS, LANES), f32),
        name="turn_sums",
    )(turn_hist, labels)


TILE = 256
TILES = KIDS * HANDS // TILE
AHEAD = 6


def place_columns(o, recv_ref, place_ref, cols_ref):
    row = lax.broadcasted_iota(i32, (8, LANES), 0)
    lane = lax.broadcasted_iota(i32, (8, LANES), 1)
    tail_hi, tail_mid, tail_low = row < 2, (row >= 2) & (row < 4), (row >= 4) & (row < 6)
    zero = jnp.zeros((8, LANES), f32)

    def gather(x, index):
        return jnp.take_along_axis(x, index, axis=1)

    def place(s, carry):
        start = s * BLOCK
        t0 = start // TILE
        a = start - t0 * TILE
        tiles = []
        for t in range(PACK_ROWS // 16):
            both = recv_ref[s, 16 * t:16 * t + 16, :].astype(f32)
            tiles += [both[0:8], both[8:16]]
        now, later = place_ref[pl.ds(t0, 1), :], place_ref[pl.ds(t0 + 1, 1), :]
        following = []
        for half in range(2):
            side = slice(half * LANES, (half + 1) * LANES)
            mask = lane + half * LANES >= a
            spill = lane + (half * LANES + TILE) < a + BLOCK
            r = jnp.where(mask, now[:, side], later[:, side])
            p = (r + o) & 127
            p2 = p ^ 64
            far = r >= LANES
            first = ((p - o) & 127) < 64
            out = []
            for g in range(6):
                source, index = tiles[(6, 7, 6, 7, 8, 9)[g]], p2 if g in (2, 3) else p
                out.append(jnp.where(far, gather(source, index), gather(tiles[g], p)))
            near, turned = gather(tiles[8], p), gather(tiles[8], p2)
            out.append(jnp.where(far & tail_hi | ~far & first & tail_low, turned,
                                 jnp.where(~far & ~first & tail_mid, near, zero)))
            merged = [jnp.where(mask, out[g], carry[7 * half + g]) for g in range(7)]
            for g in range(4):
                pair = jnp.concatenate([merged[2 * g], merged[2 * g + 1] if g < 3 else zero], axis=0)
                cols_ref[t0, 16 * g:16 * g + 16, side] = pair.astype(bf16)
            following += [jnp.where(spill, out[g], merged[g]) for g in range(7)]
        return tuple(following)

    return place, (zero,) * 14


def member_kernel(scalar_ref, recv_ref, place_ref, table_ref, assign_ref,
                  hist_ref, keep_ref, send_ref, cols_ref, even_ref, odd_ref):
    core = scalar_ref[1]
    place, carry = place_columns(scalar_ref[0], recv_ref, place_ref, cols_ref)

    def products(i, out_ref):
        h = jnp.concatenate([cols_ref[2 * i], cols_ref[2 * i + 1]], axis=1)
        out_ref[...] = jnp.dot(
            table_ref[...], jnp.concatenate([h, h, h], axis=0), preferred_element_type=f32)

    def add_kid(z_ref):
        for c in range(HANDS // LANES):
            at = slice(c * LANES, (c + 1) * LANES)
            cdf = z_ref[200:256, at]
            total = z_ref[256:264, at]
            sq = jnp.sum(cdf * cdf, axis=0, keepdims=True)
            extra = total + sharpness * sq / total
            y = z_ref[0:200, at].reshape(25, 8, LANES) + extra[None]
            w = 1.0 / (y * y)
            scale = 1.0 / jnp.sum(jnp.sum(w, axis=0), axis=0, keepdims=True)
            hist_ref[:, at] += (w * scale[None]).reshape(200, LANES)

    hist_ref[...] = jnp.zeros_like(hist_ref)
    carry = lax.fori_loop(0, AHEAD, place, carry, unroll=3)
    products(0, even_ref)

    def two_kids(j, carry):
        def some(at, carry):
            for k in range(AHEAD // 2):
                carry = place(jnp.minimum(AHEAD * (j + 1) + at + k, DEVICES - 1), carry)
            return carry

        products(2 * j + 1, odd_ref)
        carry = some(0, carry)
        add_kid(even_ref)
        products(2 * j + 2, even_ref)
        carry = some(AHEAD // 2, carry)
        add_kid(odd_ref)
        return carry

    lax.fori_loop(0, KIDS // 2, two_kids, carry)
    add_kid(even_ref)

    hi = hist_ref[...].astype(bf16)
    rest = (hist_ref[...] - hi.astype(f32)).astype(bf16)
    stack = jnp.concatenate([hi, rest], axis=0)
    ids = lax.broadcasted_iota(i32, (LANES, HANDS), 0)
    valid = ids < PANEL
    for i in range(8):
        halves = []
        for side in (core, 1 - core):
            base = PANEL * (2 * i + side)
            halves.append((valid & (assign_ref[...] - base == ids)).astype(f32).astype(bf16))
        onehot = jnp.concatenate(halves, axis=0)
        sums = lax.dot_general(stack, onehot, (((1,), (1,)), ((), ())), preferred_element_type=f32)
        both = sums[0:200] + sums[200:400]
        keep_ref[i] = both[:, :LANES]
        send_ref[i] = both[:, LANES:]


VMEM = pl.BlockSpec(memory_space=pltpu.VMEM)
SMEM = pl.BlockSpec(memory_space=pltpu.SMEM)


def member(scalars, recv, place, table, assign):
    return pl.pallas_call(
        member_kernel,
        in_specs=[SMEM, VMEM, VMEM, VMEM, VMEM],
        out_specs=[VMEM, VMEM, VMEM],
        out_shape=[
            jax.ShapeDtypeStruct((TURN_CENT, HANDS), f32),
            jax.ShapeDtypeStruct((8, TURN_CENT, LANES), f32),
            jax.ShapeDtypeStruct((8, TURN_CENT, LANES), f32),
        ],
        scratch_shapes=[
            pltpu.VMEM((TILES, 64, TILE), bf16),
            pltpu.VMEM((264, HANDS), f32),
            pltpu.VMEM((264, HANDS), f32),
        ],
        compiler_params=pltpu.CompilerParams(vmem_limit_bytes=24 * 1024 * 1024),
        name="member",
    )(scalars, recv, place, table, assign)


def nearest_kernel(mine_ref, partner_ref, pieces_ref, out_ref):
    one = jnp.where(lax.broadcasted_iota(i32, (8, 2 * HANDS), 0) == 0, 1.0, 0.0)
    hands = jnp.concatenate([jnp.concatenate([mine_ref[...], partner_ref[...]], axis=1), one], axis=0)
    lane = lax.broadcasted_iota(i32, (8, LANES), 1)
    best = None
    for i in range(pieces_ref.shape[0]):
        c = pieces_ref[i, 0:TURN_CENT, :]
        sq = jnp.broadcast_to(jnp.sum(c * c, axis=0, keepdims=True), (8, LANES))
        sides = jnp.concatenate([-2.0 * c, jnp.where(lane < PANEL, sq, 1e30)], axis=0)
        dist = lax.dot_general(
            sides, hands, (((0,), (0,)), ((), ())), precision=highest, preferred_element_type=f32)
        part = jnp.min(dist, axis=0, keepdims=True)
        best = part if best is None else jnp.minimum(best, part)
    out_ref[...] = best


def nearest_of(pieces, flop_hist, partner):
    best = pl.pallas_call(
        nearest_kernel,
        in_specs=[VMEM, VMEM, VMEM],
        out_specs=VMEM,
        out_shape=jax.ShapeDtypeStruct((1, 2 * HANDS), f32),
    compiler_params=pltpu.CompilerParams(vmem_limit_bytes=24 * 1024 * 1024),
        name="nearest",
    )(flop_hist, partner, pieces)
    best = jnp.minimum(best[:, :HANDS], swap(best[:, HANDS:], "cent", 1))
    return best[0] + jnp.sum(jnp.square(flop_hist), axis=0)


def center_table(turn_centers):
    table = fold_table(BINS)
    values = turn_centers.astype(f32)
    normal = values / jnp.sum(values, axis=0, keepdims=True)
    center_cdf = jnp.dot(table, normal, precision=highest, preferred_element_type=f32)
    center_sq = jnp.sum(center_cdf * center_cdf, axis=0)
    folded = lax.dot_general(
        center_cdf, table, (((0,), (0,)), ((), ())), precision=highest, preferred_element_type=f32)
    folded = sharpness * center_sq[:, None] - 2.0 * sharpness * folded

    def spread(x):
        return jnp.concatenate(
            [x[:, :48], x[:, 48:], x[:, 48:], x[:, 48:], jnp.zeros((x.shape[0], 10), f32)], axis=1)

    hi = lax.reduce_precision(folded, 8, 7)
    mid = lax.reduce_precision(folded - hi, 8, 7)
    low = lax.reduce_precision(folded - hi - mid, 8, 7)
    top = jnp.concatenate([spread(hi), spread(mid), spread(low)], axis=1)
    rows = jnp.concatenate([table, jnp.zeros((6, BINS), f32), jnp.ones((8, BINS), f32)], axis=0)
    bottom = jnp.concatenate([spread(rows), jnp.zeros((64, 128), f32)], axis=1)
    return jnp.concatenate([top, bottom], axis=0).astype(bf16)


CHIPS = [[2 * i + c for i in range(8)] for c in range(2)]


def swap(x, axis, mask):
    size = 8 if axis == "board" else 16
    return lax.ppermute(x, axis, [(i, i ^ mask) for i in range(size)])


def finish(first, second, third, fourth, flop_scale, turn_scale):
    def kernel(a_ref, b_ref, c_ref, d_ref, flop_ref, turn_ref):
        total = (a_ref[...] + b_ref[...]) + (c_ref[...] + d_ref[...])
        flop_ref[...] = total[:TURN_CENT, :PANEL] * flop_scale
        turn = total[TURN_CENT:] * turn_scale
        turn_ref[:, :LANES] = turn[:BINS]
        turn_ref[:, LANES:] = turn[TURN_SPLIT:TURN_SPLIT + BINS, :TURN_CENT - LANES]

    return pl.pallas_call(
        kernel,
        in_specs=[VMEM] * 4,
        out_specs=[VMEM] * 2,
        out_shape=[
            jax.ShapeDtypeStruct((TURN_CENT, PANEL), f32),
            jax.ShapeDtypeStruct((BINS, TURN_CENT), f32),
        ],
        compiler_params=pltpu.CompilerParams(vmem_limit_bytes=8 * 1024 * 1024),
        name="finish",
    )(first, second, third, fourth)


def body(turn_hist, turn_assign, child_rows, turn_centers, flop_centers, flop_assign):
    sent = pack(turn_hist)
    turn_assign, sent = lax.optimization_barrier((turn_assign, sent))
    arrived = lax.all_to_all(sent, ("board", "cent"), split_axis=0, concat_axis=0, tiled=True)

    device = lax.axis_index("board") * 16 + lax.axis_index("cent")
    offset = (device * BLOCK) % LANES
    scalars = jnp.stack([offset, lax.axis_index("cent") % 2]).astype(i32)

    turn_part = turn_partial(turn_hist, turn_assign[None, :])
    own = jnp.concatenate([jnp.pad(flop_centers, ((0, 0), (0, LANES - PANEL))), turn_part], axis=0)
    place = jnp.concatenate([child_rows.reshape(TILES, TILE), jnp.zeros((2, TILE), i32)], axis=0)
    table = center_table(turn_centers)

    own, place, table, scalars = lax.optimization_barrier((own, place, table, scalars))
    copies = jnp.broadcast_to(own[None], (8,) + own.shape)
    pieces = lax.all_to_all(copies, "cent", split_axis=0, concat_axis=0, tiled=True, axis_index_groups=CHIPS)

    flop_hist, keep, send = member(scalars, arrived, place, table, flop_assign[None, :])

    turn_part = jnp.sum(pieces[:, TURN_CENT:], axis=0)
    turn_part = turn_part + swap(turn_part, "cent", 1)
    turn_part = turn_part + swap(turn_part, "board", 1)
    half = keep + swap(send, "cent", 1)
    flop_hist, half = lax.optimization_barrier((flop_hist, half))
    partner = swap(flop_hist, "cent", 1)
    parts = lax.all_to_all(half, "cent", split_axis=0, concat_axis=0, tiled=True, axis_index_groups=CHIPS)
    flop_part = jnp.sum(parts, axis=0)
    flop_part = flop_part + swap(flop_part, "board", 1)
    total = jnp.concatenate([flop_part, turn_part], axis=0)
    flop_sums, turn_sums = finish(
        total, swap(total, "board", 2), swap(total, "board", 4), swap(total, "board", 6),
        PANEL * 16 / (HANDS * DEVICES), BINS * TURN_CENT / (turn_hist.shape[1] * DEVICES))
    flop_sums = flop_sums.T

    nearest = nearest_of(pieces, flop_hist, partner)
    return nearest, turn_sums, flop_sums


def solution(mesh):
    in_specs = (
        P(None, ("board", "cent")),
        P(("board", "cent")),
        P(None, ("board", "cent")),
        P(),
        P(None, "cent"),
        P(("board", "cent")),
    )
    out_specs = (P(("board", "cent")), P(), P("cent", None))
    return jax.shard_map(body, mesh=mesh, in_specs=in_specs, out_specs=out_specs, check_vma=False)
```

```python
import jax
import jax.numpy as jnp
from jax import lax
from jax.experimental import pallas as pl
from jax.experimental.pallas import tpu as pltpu
from jax.sharding import PartitionSpec as P


sharpness = 4.0
highest = lax.Precision.HIGHEST
f32, bf16, i32 = jnp.float32, jnp.bfloat16, jnp.int32
LANES = 128
BLOCK = 188
BINS = 50
KIDS = 47
TURN_CENT = 200
HANDS = 512
PANEL = 125
DEVICES = 128
SOURCES_PER_STEP = 32
PACK_ROWS = 80
TURN_SPLIT = 50
TURN_ROWS = 104


def fold_table(bins):
    upper = lax.iota(i32, bins)[:, None]
    lower = lax.iota(i32, bins)[None, :]
    table = 0.5 * (lower <= upper).astype(f32)
    table = table + 0.25 * (lower <= upper - 1).astype(f32)
    table = table + 0.25 * ((lower <= upper + 1) & (lower >= 1)).astype(f32)
    return table


def pack_kernel(hist_ref, out_ref):
    lane = lax.broadcasted_iota(i32, (16, LANES), 1)
    for d in range(SOURCES_PER_STEP):
        t0, o = divmod(BLOCK * d, LANES)
        three = o + BLOCK > 2 * LANES

        def parts(lo, hi):
            tiles = [hist_ref[lo:hi, (t0 + t) * LANES:(t0 + t + 1) * LANES].astype(f32)
                     for t in range(3 if three else 2)]
            upper = lane[:hi - lo] >= o
            a = jnp.where(upper, tiles[0], tiles[1]) if o else tiles[0]
            b = jnp.where(upper, tiles[1], tiles[2]) if three else tiles[1]
            return a, b

        a0, b0 = parts(0, 16)
        a1, b1 = parts(16, 32)
        a2, b2 = parts(32, 48)
        a3, b3 = parts(48, 50)
        first = ((lane - o) & 127) < 64
        out_ref[d, 0:16, :] = a0.astype(bf16)
        out_ref[d, 16:32, :] = a1.astype(bf16)
        out_ref[d, 32:48, :] = a2.astype(bf16)
        out_ref[d, 48:64, :] = jnp.where(first, b0, pltpu.roll(b1, 64, 1)).astype(bf16)
        tail = jnp.concatenate(
            [pltpu.roll(b3, 64, 1), a3, pltpu.roll(a3, 64, 1), jnp.zeros((10, LANES), f32)], axis=0)
        out_ref[d, 64:80, :] = jnp.where(first, b2, tail).astype(bf16)


def pack(turn_hist):
    width = SOURCES_PER_STEP * BLOCK
    return pl.pallas_call(
        pack_kernel,
        grid=(DEVICES // SOURCES_PER_STEP,),
        in_specs=[pl.BlockSpec((BINS, width), lambda i: (0, i))],
        out_specs=pl.BlockSpec((SOURCES_PER_STEP, PACK_ROWS, LANES), lambda i: (i, 0, 0)),
        out_shape=jax.ShapeDtypeStruct((DEVICES, PACK_ROWS, LANES), bf16),
        name="pack",
    )(turn_hist)


def turn_kernel(hist_ref, label_ref, out_ref):
    @pl.when(pl.program_id(0) == 0)
    def _():
        out_ref[...] = jnp.zeros_like(out_ref)

    values = hist_ref[...].astype(f32)
    normal = values / jnp.sum(values, axis=0, keepdims=True)
    hi = normal.astype(bf16)
    rest = normal - hi.astype(f32)
    mid = rest.astype(bf16)
    low = (rest - mid.astype(f32)).astype(bf16)
    ids = lax.broadcasted_iota(i32, (TURN_CENT, values.shape[1]), 0)
    onehot = (label_ref[...] == ids).astype(f32).astype(bf16)
    total = None
    for part in (hi, mid, low):
        more = lax.dot_general(part, onehot, (((1,), (1,)), ((), ())), preferred_element_type=f32)
        total = more if total is None else total + more
    out_ref[0:BINS, :] += total[:, :LANES]
    out_ref[TURN_SPLIT:TURN_SPLIT + BINS, 0:TURN_CENT - LANES] += total[:, LANES:]


def turn_partial(turn_hist, labels):
    width = SOURCES_PER_STEP * BLOCK // 2 if (SOURCES_PER_STEP * BLOCK // 2) % LANES == 0 else SOURCES_PER_STEP * BLOCK
    steps = turn_hist.shape[1] // width
    return pl.pallas_call(
        turn_kernel,
        grid=(steps,),
        in_specs=[pl.BlockSpec((BINS, width), lambda i: (0, i)), pl.BlockSpec((1, width), lambda i: (0, i))],
        out_specs=pl.BlockSpec((TURN_ROWS, LANES), lambda i: (0, 0)),
        out_shape=jax.ShapeDtypeStruct((TURN_ROWS, LANES), f32),
        name="turn_sums",
    )(turn_hist, labels)


TILE = 256
TILES = KIDS * HANDS // TILE
AHEAD = 6


def place_columns(o, recv_ref, place_ref, cols_ref):
    row = lax.broadcasted_iota(i32, (8, LANES), 0)
    lane = lax.broadcasted_iota(i32, (8, LANES), 1)
    tail_hi, tail_mid, tail_low = row < 2, (row >= 2) & (row < 4), (row >= 4) & (row < 6)
    zero = jnp.zeros((8, LANES), f32)

    def gather(x, index):
        return jnp.take_along_axis(x, index, axis=1)

    def place(s, carry):
        start = s * BLOCK
        t0 = start // TILE
        a = start - t0 * TILE
        tiles = []
        for t in range(PACK_ROWS // 16):
            both = recv_ref[s, 16 * t:16 * t + 16, :].astype(f32)
            tiles += [both[0:8], both[8:16]]
        now, later = place_ref[pl.ds(t0, 1), :], place_ref[pl.ds(t0 + 1, 1), :]
        following = []
        for half in range(2):
            side = slice(half * LANES, (half + 1) * LANES)
            mask = lane + half * LANES >= a
            spill = lane + (half * LANES + TILE) < a + BLOCK
            r = jnp.where(mask, now[:, side], later[:, side])
            p = (r + o) & 127
            p2 = p ^ 64
            far = r >= LANES
            first = ((p - o) & 127) < 64
            out = []
            for g in range(6):
                source, index = tiles[(6, 7, 6, 7, 8, 9)[g]], p2 if g in (2, 3) else p
                out.append(jnp.where(far, gather(source, index), gather(tiles[g], p)))
            near, turned = gather(tiles[8], p), gather(tiles[8], p2)
            out.append(jnp.where(far & tail_hi | ~far & first & tail_low, turned,
                                 jnp.where(~far & ~first & tail_mid, near, zero)))
            merged = [jnp.where(mask, out[g], carry[7 * half + g]) for g in range(7)]
            for g in range(4):
                pair = jnp.concatenate([merged[2 * g], merged[2 * g + 1] if g < 3 else zero], axis=0)
                cols_ref[t0, 16 * g:16 * g + 16, side] = pair.astype(bf16)
            following += [jnp.where(spill, out[g], merged[g]) for g in range(7)]
        return tuple(following)

    return place, (zero,) * 14


def member_kernel(scalar_ref, recv_ref, place_ref, table_ref, assign_ref,
                  hist_ref, keep_ref, send_ref, cols_ref, even_ref, odd_ref):
    core = scalar_ref[1]
    place, carry = place_columns(scalar_ref[0], recv_ref, place_ref, cols_ref)

    def products(i, out_ref):
        h = jnp.concatenate([cols_ref[2 * i], cols_ref[2 * i + 1]], axis=1)
        out_ref[...] = jnp.dot(
            table_ref[...], jnp.concatenate([h, h, h], axis=0), preferred_element_type=f32)

    def add_kid(z_ref):
        for c in range(HANDS // LANES):
            at = slice(c * LANES, (c + 1) * LANES)
            cdf = z_ref[200:256, at]
            total = z_ref[256:264, at]
            sq = jnp.sum(cdf * cdf, axis=0, keepdims=True)
            extra = total + sharpness * sq / total
            y = z_ref[0:200, at].reshape(25, 8, LANES) + extra[None]
            w = 1.0 / (y * y)
            scale = 1.0 / jnp.sum(jnp.sum(w, axis=0), axis=0, keepdims=True)
            hist_ref[:, at] += (w * scale[None]).reshape(200, LANES)

    hist_ref[...] = jnp.zeros_like(hist_ref)
    carry = lax.fori_loop(0, AHEAD, place, carry, unroll=3)
    products(0, even_ref)

    def two_kids(j, carry):
        def some(at, carry):
            for k in range(AHEAD // 2):
                carry = place(jnp.minimum(AHEAD * (j + 1) + at + k, DEVICES - 1), carry)
            return carry

        products(2 * j + 1, odd_ref)
        carry = some(0, carry)
        add_kid(even_ref)
        products(2 * j + 2, even_ref)
        carry = some(AHEAD // 2, carry)
        add_kid(odd_ref)
        return carry

    lax.fori_loop(0, KIDS // 2, two_kids, carry)
    add_kid(even_ref)

    hi = hist_ref[...].astype(bf16)
    rest = (hist_ref[...] - hi.astype(f32)).astype(bf16)
    stack = jnp.concatenate([hi, rest], axis=0)
    ids = lax.broadcasted_iota(i32, (LANES, HANDS), 0)
    valid = ids < PANEL
    for i in range(8):
        halves = []
        for side in (core, 1 - core):
            base = PANEL * (2 * i + side)
            halves.append((valid & (assign_ref[...] - base == ids)).astype(f32).astype(bf16))
        onehot = jnp.concatenate(halves, axis=0)
        sums = lax.dot_general(stack, onehot, (((1,), (1,)), ((), ())), preferred_element_type=f32)
        both = sums[0:200] + sums[200:400]
        keep_ref[i] = both[:, :LANES]
        send_ref[i] = both[:, LANES:]


VMEM = pl.BlockSpec(memory_space=pltpu.VMEM)
SMEM = pl.BlockSpec(memory_space=pltpu.SMEM)


def member(scalars, recv, place, table, assign):
    return pl.pallas_call(
        member_kernel,
        in_specs=[SMEM, VMEM, VMEM, VMEM, VMEM],
        out_specs=[VMEM, VMEM, VMEM],
        out_shape=[
            jax.ShapeDtypeStruct((TURN_CENT, HANDS), f32),
            jax.ShapeDtypeStruct((8, TURN_CENT, LANES), f32),
            jax.ShapeDtypeStruct((8, TURN_CENT, LANES), f32),
        ],
        scratch_shapes=[
            pltpu.VMEM((TILES, 64, TILE), bf16),
            pltpu.VMEM((264, HANDS), f32),
            pltpu.VMEM((264, HANDS), f32),
        ],
        compiler_params=pltpu.CompilerParams(vmem_limit_bytes=24 * 1024 * 1024),
        name="member",
    )(scalars, recv, place, table, assign)


def nearest_kernel(mine_ref, partner_ref, *refs):
    pieces, out_ref = refs[:-1], refs[-1]
    one = jnp.where(lax.broadcasted_iota(i32, (8, 2 * HANDS), 0) == 0, 1.0, 0.0)
    hands = jnp.concatenate([jnp.concatenate([mine_ref[...], partner_ref[...]], axis=1), one], axis=0)
    lane = lax.broadcasted_iota(i32, (8, LANES), 1)
    best = None
    for ref in pieces:
        c = ref[0:TURN_CENT, :]
        sq = jnp.broadcast_to(jnp.sum(c * c, axis=0, keepdims=True), (8, LANES))
        sides = jnp.concatenate([-2.0 * c, jnp.where(lane < PANEL, sq, 1e30)], axis=0)
        dist = lax.dot_general(
            sides, hands, (((0,), (0,)), ((), ())), precision=highest, preferred_element_type=f32)
        part = jnp.min(dist, axis=0, keepdims=True)
        best = part if best is None else jnp.minimum(best, part)
    out_ref[...] = best


def nearest_of(pieces, flop_hist, partner):
    best = pl.pallas_call(
        nearest_kernel,
        in_specs=[VMEM] * (2 + len(pieces)),
        out_specs=VMEM,
        out_shape=jax.ShapeDtypeStruct((1, 2 * HANDS), f32),
    compiler_params=pltpu.CompilerParams(vmem_limit_bytes=24 * 1024 * 1024),
        name="nearest",
    )(flop_hist, partner, *pieces)
    best = jnp.minimum(best[:, :HANDS], swap(best[:, HANDS:], "cent", 1))
    return best[0] + jnp.sum(jnp.square(flop_hist), axis=0)


def center_table(turn_centers):
    table = fold_table(BINS)
    values = turn_centers.astype(f32)
    normal = values / jnp.sum(values, axis=0, keepdims=True)
    center_cdf = jnp.dot(table, normal, precision=highest, preferred_element_type=f32)
    center_sq = jnp.sum(center_cdf * center_cdf, axis=0)
    folded = lax.dot_general(
        center_cdf, table, (((0,), (0,)), ((), ())), precision=highest, preferred_element_type=f32)
    folded = sharpness * center_sq[:, None] - 2.0 * sharpness * folded

    def spread(x):
        return jnp.concatenate(
            [x[:, :48], x[:, 48:], x[:, 48:], x[:, 48:], jnp.zeros((x.shape[0], 10), f32)], axis=1)

    hi = lax.reduce_precision(folded, 8, 7)
    mid = lax.reduce_precision(folded - hi, 8, 7)
    low = lax.reduce_precision(folded - hi - mid, 8, 7)
    top = jnp.concatenate([spread(hi), spread(mid), spread(low)], axis=1)
    rows = jnp.concatenate([table, jnp.zeros((6, BINS), f32), jnp.ones((8, BINS), f32)], axis=0)
    bottom = jnp.concatenate([spread(rows), jnp.zeros((64, 128), f32)], axis=1)
    return jnp.concatenate([top, bottom], axis=0).astype(bf16)


CHIPS = [[2 * i + c for i in range(8)] for c in range(2)]


def swap(x, axis, mask):
    size = 8 if axis == "board" else 16
    return lax.ppermute(x, axis, [(i, i ^ mask) for i in range(size)])


def finish(first, second, third, fourth, flop_scale, turn_scale):
    def kernel(a_ref, b_ref, c_ref, d_ref, flop_ref, turn_ref):
        total = (a_ref[...] + b_ref[...]) + (c_ref[...] + d_ref[...])
        flop_ref[...] = total[:TURN_CENT, :PANEL] * flop_scale
        turn = total[TURN_CENT:] * turn_scale
        turn_ref[:, :LANES] = turn[:BINS]
        turn_ref[:, LANES:] = turn[TURN_SPLIT:TURN_SPLIT + BINS, :TURN_CENT - LANES]

    return pl.pallas_call(
        kernel,
        in_specs=[VMEM] * 4,
        out_specs=[VMEM] * 2,
        out_shape=[
            jax.ShapeDtypeStruct((TURN_CENT, PANEL), f32),
            jax.ShapeDtypeStruct((BINS, TURN_CENT), f32),
        ],
        compiler_params=pltpu.CompilerParams(vmem_limit_bytes=8 * 1024 * 1024),
        name="finish",
    )(first, second, third, fourth)


def body(turn_hist, turn_assign, child_rows, turn_centers, flop_centers, flop_assign):
    sent = pack(turn_hist)
    turn_assign, sent = lax.optimization_barrier((turn_assign, sent))
    arrived = lax.all_to_all(sent, ("board", "cent"), split_axis=0, concat_axis=0, tiled=True)

    device = lax.axis_index("board") * 16 + lax.axis_index("cent")
    offset = (device * BLOCK) % LANES
    scalars = jnp.stack([offset, lax.axis_index("cent") % 2]).astype(i32)

    turn_part = turn_partial(turn_hist, turn_assign[None, :])
    own = jnp.concatenate([jnp.pad(flop_centers, ((0, 0), (0, LANES - PANEL))), turn_part], axis=0)
    pieces = [own]
    for mask in range(2, 16, 2):
        pieces.append(swap(own, "cent", mask))
    place = jnp.concatenate([child_rows.reshape(TILES, TILE), jnp.zeros((2, TILE), i32)], axis=0)
    table = center_table(turn_centers)

    place, table, scalars = lax.optimization_barrier((place, table, scalars))
    flop_hist, keep, send = member(scalars, arrived, place, table, flop_assign[None, :])

    turn_part = sum((piece[TURN_CENT:] for piece in pieces[1:]), turn_part)
    turn_part = turn_part + swap(turn_part, "cent", 1)
    turn_part = turn_part + swap(turn_part, "board", 1)
    half = keep + swap(send, "cent", 1)
    flop_hist, half = lax.optimization_barrier((flop_hist, half))
    partner = swap(flop_hist, "cent", 1)
    parts = lax.all_to_all(half, "cent", split_axis=0, concat_axis=0, tiled=True, axis_index_groups=CHIPS)
    flop_part = jnp.sum(parts, axis=0)
    flop_part = flop_part + swap(flop_part, "board", 1)
    total = jnp.concatenate([flop_part, turn_part], axis=0)
    flop_sums, turn_sums = finish(
        total, swap(total, "board", 2), swap(total, "board", 4), swap(total, "board", 6),
        PANEL * 16 / (HANDS * DEVICES), BINS * TURN_CENT / (turn_hist.shape[1] * DEVICES))
    flop_sums = flop_sums.T

    nearest = nearest_of(pieces, flop_hist, partner)
    return nearest, turn_sums, flop_sums


def solution(mesh):
    in_specs = (
        P(None, ("board", "cent")),
        P(("board", "cent")),
        P(None, ("board", "cent")),
        P(),
        P(None, "cent"),
        P(("board", "cent")),
    )
    out_specs = (P(("board", "cent")), P(), P("cent", None))
    return jax.shard_map(body, mesh=mesh, in_specs=in_specs, out_specs=out_specs, check_vma=False)
```
